32 devices in a mesh: row: 4 (over y, x), col: 8 (over z, core).
Axes of the slice: x: 2, y: 2, z: 4, core: 2. Of those that a mesh axis runs over, the one named last changes fastest.
Arguments:
- feat_rows: float32 [2048, 512], P(('row', 'col')), may hold values from -0.6 to 0.6
- feat_cols: float32 [2048, 512], P(('col', 'row')), may hold values from -0.6 to 0.6
- panel_rows: float32 [2048, 1024], P(('row', 'col')), may hold values from -0.6 to 0.6
- panel_cols: float32 [2048, 1024], P(('col', 'row')), may hold values from -0.6 to 0.6
- accumulator: float32 [2048, 2048], P('row', 'col'), may hold values from -1.8 to 1.8
Outputs:
- acc_new: float32 [2048, 2048], P('row', 'col')
- grad_rows: float32 [2048, 512], P(('row', 'col'))
- grad_cols: float32 [2048, 512], P(('col', 'row'))
The draws below stay inside these ranges and needn't reach their ends.
All inputs are finite; a program needn't handle non-finite values.
Results may differ from the reference program's by a relative error of at most 0.00011.
Values sent between devices are 32-bit elements; how exact they have to be, the bound alone decides.
A program may use at most 64 MiB of HBM per device.

```python
import jax
import jax.numpy as jnp
from jax import lax

F = 512
PANEL = 512
PANELS = 2
NA = 2048
NB = 2048
N_ROW = 4


def steps_of(key, extent, pieces, least, top_value):
    factor_of, own = 1.0, jax.random.fold_in(key, 6)
    for position, parts in pieces:
        heights = jnp.exp(jax.random.uniform(jax.random.fold_in(own, position), (parts,), jnp.float32, least / len(pieces), top_value / len(pieces)))
        factor_of = factor_of * jnp.repeat(heights, extent[position] // parts).reshape([-1 if axis == position else 1 for axis in range(len(extent))])
    return factor_of


def scatter_about(rng, extent, scale, limit, split=(), kind=jnp.bfloat16):
    gain = steps_of(rng, extent, split, -0.22, 0.18) if split else 1.0
    result = jax.random.normal(rng, extent, jnp.float32) * scale * gain
    return jnp.minimum(jnp.maximum(result, -limit), limit).astype(kind)


def setup_inputs(seed: int = 0) -> dict:
    streams_of = jax.random.split(jax.random.key(seed), 6)
    return {
        "feat_rows": scatter_about(streams_of[0], (NA, F), 0.1, 0.6, ((0, 32),), jnp.float32),
        "feat_cols": scatter_about(streams_of[1], (NB, F), 0.1, 0.6, ((0, 32),), jnp.float32),
        "panel_rows": scatter_about(streams_of[2], (NA, PANELS * PANEL), 0.1, 0.6, ((0, 32),), jnp.float32),
        "panel_cols": scatter_about(streams_of[3], (NB, PANELS * PANEL), 0.1, 0.6, ((0, 32),), jnp.float32),
        "accumulator": scatter_about(streams_of[4], (NA, NB), 0.3, 1.8, ((0, 4), (1, 8)), jnp.float32),
    }


decay_rate = 0.125
grad_scale = 0.25


def local_tile(rows_feat, rows_panel, acc_tile, cols_feat, cols_panel):
    grams_tile = acc_tile + jnp.dot(rows_panel, cols_panel.T, precision=lax.Precision.HIGHEST)
    cross_term = jnp.dot(rows_feat, cols_feat.T, precision=lax.Precision.HIGHEST)
    norm_rows = jnp.sum(rows_feat * rows_feat, axis=1)
    norm_cols = jnp.sum(cols_feat * cols_feat, axis=1)
    dist_sq = norm_rows[:, None] + norm_cols[None, :] - 2.0 * cross_term
    kernel = jnp.exp(-decay_rate * dist_sq)
    weights = grams_tile * kernel
    row_term = grad_scale * (jnp.dot(weights, cols_feat, precision=lax.Precision.HIGHEST) - jnp.sum(weights, axis=1)[:, None] * rows_feat)
    col_term = grad_scale * (jnp.dot(weights.T, rows_feat, precision=lax.Precision.HIGHEST) - jnp.sum(weights, axis=0)[:, None] * cols_feat)
    return grams_tile, row_term, col_term


def reference(feat_rows, feat_cols, panel_rows, panel_cols, accumulator):
    blocks = N_ROW
    height = NA // blocks
    rows_feat = feat_rows.reshape(blocks, height, F)
    rows_panel = panel_rows.reshape(blocks, height, PANELS * PANEL)
    acc_blocks = accumulator.reshape(blocks, height, NB)

    def step_fn(totals, inputs):
        feat_blk, panel_blk, acc_blk = inputs
        grams_tile, row_term, col_term = local_tile(feat_blk, panel_blk, acc_blk, feat_cols, panel_cols)
        return totals + col_term, (grams_tile, row_term)

    init = jnp.zeros((NB, F), jnp.float32)
    col_total, outputs = lax.scan(step_fn, init, (rows_feat, rows_panel, acc_blocks))
    acc_new = outputs[0].reshape(NA, NB)
    grad_rows = outputs[1].reshape(NA, F)
    return acc_new, grad_rows, col_total
```

```python
import functools

import jax
import jax.numpy as jnp
from jax import lax
from jax.experimental import pallas as pl
from jax.experimental.pallas import tpu as pltpu
from jax.sharding import PartitionSpec as P

decay_rate = 0.125
grad_scale = 0.25
MESH = pl.DeviceIdType.MESH
HALVES = 2
LEAD = 4
RELAY_SLOTS = 2
LATE = 2


def split(x):
    hi = x.astype(jnp.bfloat16)
    return hi, (x - hi.astype(jnp.float32)).astype(jnp.bfloat16)


def dot3(a, b, ca, cb):
    dims = (((ca,), (cb,)), ((), ()))
    f = functools.partial(lax.dot_general, dimension_numbers=dims, preferred_element_type=jnp.float32)
    return f(a[0], b[0]) + (f(a[0], b[1]) + f(a[1], b[0]))


def order(n, depth, y, t):
    src, chunk = y * 0, t * 0
    found = y < 0
    for _ in range(depth):
        lead = t < LEAD
        done = jnp.logical_or(lead, t >= LEAD + n * y)
        take = jnp.logical_and(done, jnp.logical_not(found))
        src = jnp.where(take, y, src)
        chunk = jnp.where(take, jnp.where(lead, t, t - n * y), chunk)
        found = jnp.logical_or(found, done)
        y, t = y - 1, t - LEAD
    return src, chunk


def ready(n, depth, z, s, chunks):
    def seq(y):
        own = [(y, i) for i in range(n)]
        return own if y == 0 else own[:LEAD] + seq(y - 1) + own[LEAD:]

    if s == z:
        return 0
    y, ys = (z, s) if s < z else (depth - 1 - z, depth - 1 - s)
    return 1 + max(t for t, (a, i) in enumerate(seq(y - 1)) if a == ys and i in chunks)


def plan(Q, depth):
    n = HALVES * Q
    table, need = [], []
    steps = [(2 * j, 2 * j + 1) for j in range(HALVES * depth // 2 - 1)]
    steps += [(HALVES * depth - 2,), (HALVES * depth - 1,)]
    for z in range(depth):
        own = [(z, h) for h in range(HALVES)]
        far = [(s, h) for s in range(depth) for h in range(HALVES) if s != z]
        at = {(s, h): ready(n, depth, z, s, range(h * Q, h * Q + Q)) for s, h in own + far}
        far = sorted(far, key=lambda u: (at[u], -abs(u[0] - z)))
        end = z in (0, depth - 1)
        subs = own + far if end else far + own
        total = n * max(z, depth - 1 - z)
        late = max(ready(n, depth, z, s, (h * Q,)) for s, h in subs[-LATE:])
        first = min(total, max(late, n + LEAD - 1)) if end else total
        taken, row = first, []
        for j, step in enumerate(steps):
            taken = max(taken, min(total, max(at[subs[i]] for i in step) + 1) if j else first)
            row.append(taken)
        table.append([s * HALVES + h for s, h in subs])
        need.append(row)
    return table, need


def pick(values, at):
    out = jnp.int32(values[0])
    for i, v in enumerate(values[1:], 1):
        out = jnp.where(at == i, jnp.int32(v), out)
    return out


def kernel(R, C, fr, fc, pr, pc, acc, accv, gr_out, gc_out,
           rows, cols, chi, clo, ncol, rowp, sibp, sumb, rgbuf, colacc, tacc, colr, lfeat, wlate, wlin,
           lsem, rrecv, srecv, crecv, xrecv, sends, bulk):
    me_r, me_c = lax.axis_index("row"), lax.axis_index("col")
    z, k = me_c // 2, me_c % 2
    Z = C // 2
    NR, F = fr.shape
    NC = fc.shape[0]
    Q = 1 + pr.shape[1] // F
    n = HALVES * Q
    hr = NR // HALVES
    UR = 2 * hr
    sibling = (me_r, me_c + 1 - 2 * k)
    place = (z, Z - 1 - z)
    step_to = (2, -2)
    table, need = plan(Q, Z)
    square = R == 4
    near = (me_r // 2 * 2 + 1 - me_r % 2, (1 - me_r // 2) * 2 + me_r % 2)
    across = R - 1 - me_r
    z_sent, sib_sent, col_sent, relay_sent, x_sent, row_sent, grad_sent, w_sent, feat_sent, pass_sent = (
        sends.at[i] for i in (0, 2, 3, 4, 5, 6, 7, 8, 9, 10))
    relay_in, row_in, grad_in, w_in, feat_in, pass_in = (bulk.at[i] for i in range(6))

    def at(start, size, mult):
        return pl.ds(pl.multiple_of(start, mult), size)

    def remote(src, dst, ss, rs, dev):
        return pltpu.make_async_remote_copy(src_ref=src, dst_ref=dst, send_sem=ss, recv_sem=rs, device_id=dev, device_id_type=MESH)

    def landed(ref, sem):
        pltpu.make_async_copy(ref, ref, sem).wait()

    def place_of(zs, h, core):
        return ((zs * HALVES + h) * 2 + core) * hr

    def rchunk(zs, core, i):
        return rows.at[i % Q, at(place_of(zs, i // Q, core), hr, 8), :]

    def own_chunk(i):
        q, h = i % Q, i // Q
        src = fr if q == 0 else pr
        return src.at[pl.ds(h * hr, hr), pl.ds(max(q - 1, 0) * F, F)]

    def own_cols(q):
        return fc if q == 0 else pc.at[:, pl.ds((q - 1) * F, F)]

    def zcopy(d, zs, i, src=None):
        dst = rchunk(zs, k, i)
        return remote(dst if src is None else src, dst, sends.at[d], rrecv.at[zs, i], (me_r, me_c + step_to[d]))

    def scopy(zs, i, src=None):
        dst = rchunk(zs, k, i)
        return remote(dst if src is None else src, dst, sib_sent, srecv.at[zs * HALVES + i // Q], sibling)

    for q in range(Q):
        for h in range(HALVES):
            pltpu.make_async_copy(own_chunk(h * Q + q), rchunk(z, k, h * Q + q), lsem.at[0]).start()
        pltpu.make_async_copy(own_cols(q), cols.at[q, at(me_r * NC, NC, 8), :], lsem.at[1]).start()
    acc_in = pltpu.make_async_copy(acc, accv, lsem.at[2])
    acc_in.start()

    barrier = pltpu.get_barrier_semaphore()
    if square:
        for axis in range(2):
            pl.semaphore_signal(barrier, inc=1, device_id=(near[axis], me_c), device_id_type=MESH)
    else:
        def greet(p, carry):
            pl.semaphore_signal(barrier, inc=1, device_id=((me_r + p) % R, me_c), device_id_type=MESH)
            return carry

        lax.fori_loop(1, R, greet, 0)
    pl.semaphore_signal(barrier, inc=1, device_id=sibling, device_id_type=MESH)
    for d in range(2):
        @pl.when(place[d] < Z - 1)
        def _():
            pl.semaphore_signal(barrier, inc=1, device_id=(me_r, me_c + step_to[d]), device_id_type=MESH)
    greeted = (2 if square else R - 1) + 1
    pl.semaphore_wait(barrier, greeted + (z > 0).astype(jnp.int32) + (z < Z - 1).astype(jnp.int32))

    def zown(d, lo, hi):
        for i in range(lo, hi):
            zcopy(d, z, i, own_chunk(i)).start()

    for d in range(2):
        @pl.when(place[d] < Z - 1)
        def _():
            zown(d, 0, LEAD)

    def own_push(axis, q):
        block = cols.at[q, at(me_r * NC, NC, 8), :]
        return remote(own_cols(q), block, col_sent, crecv.at[axis, q], (near[axis], me_c))

    def own_arrive(axis, q):
        block = cols.at[q, at(near[axis] * NC, NC, 8), :]
        return remote(block, block, col_sent, crecv.at[axis, q], (near[axis], me_c))

    def relay(axis, q):
        block = cols.at[q, at(near[axis] * NC + axis * (NC // 2), NC // 2, 8), :]
        return remote(block, block, relay_sent, relay_in, (near[1 - axis], me_c))

    def push_cols(p, carry):
        for q in range(Q):
            block = cols.at[q, at(me_r * NC, NC, 8), :]
            remote(own_cols(q), block, col_sent, relay_in, ((me_r + p) % R, me_c)).start()
        return carry

    if square:
        for q in range(Q):
            for axis in range(2):
                own_push(axis, q).start()
    else:
        lax.fori_loop(1, R, push_cols, 0)
    for d in range(2):
        @pl.when(place[d] == 0)
        def _():
            zown(d, LEAD, n)
    for i in range(n):
        scopy(z, i, own_chunk(i)).start()

    def slot(t, carry):
        for d in range(2):
            y = place[d]

            @pl.when(t < n * y)
            def _():
                ys, i = order(n, Z, y - 1, t)
                zs = ys if d == 0 else Z - 1 - ys
                zcopy(d, zs, i).wait_recv()

                @pl.when(y < Z - 1)
                def _():
                    zcopy(d, zs, i).start()

                scopy(zs, i).start()

                @pl.when(jnp.logical_and(t == n * y - 1, y < Z - 1))
                def _():
                    zown(d, LEAD, n)

        return carry

    def by_place(values, j):
        out = pick([row[j] for row in values], z) if isinstance(j, int) else None
        if out is None:
            out = pick(values[0], j)
            for place_z in range(1, Z):
                out = jnp.where(z == place_z, pick(values[place_z], j), out)
        return out

    first = by_place(need, 0)
    passed = 0
    if square:
        for q in range(Q):
            upto = min(RELAY_SLOTS * (q + 1), min(row[0] for row in need))
            lax.fori_loop(passed, upto, slot, 0)
            passed = upto
            for axis in range(2):
                own_arrive(axis, q).wait_recv()
                relay(axis, q).start()
    lax.fori_loop(passed, first, slot, 0)

    landed(rows.at[:, pl.ds(0, NR), :], lsem.at[0])
    landed(cols.at[:, pl.ds(0, NC), :], lsem.at[1])
    acc_in.wait()
    landed(cols.at[:, pl.ds(0, NC if square else (R - 1) * NC), :], relay_in)

    late = [by_place(table, HALVES * Z - LATE + s) for s in range(LATE)]

    def push_late(p, carry):
        for s in range(LATE):
            src = rows.at[0, at(late[s] * UR + k * hr, hr, 8), :]
            remote(src, lfeat.at[me_r, s, k], feat_sent, feat_in, ((me_r + p) % R, me_c)).start()
        return carry

    lax.fori_loop(1, R, push_late, 0)

    for q in range(Q):
        hi, lo = split(cols[q])
        chi[q] = hi
        clo[q] = lo
    feats = cols[0]
    ncol[...] = lax.dot_general(
        jnp.ones((8, F), jnp.float32), feats * feats, (((1,), (1,)), ((), ())),
        precision=lax.Precision.HIGHEST, preferred_element_type=jnp.float32)
    colacc[...] = jnp.zeros_like(colacc)
    tacc[...] = jnp.zeros_like(tacc)

    def exchange(sub):
        return remote(rowp.at[at(sub * UR + (1 - k) * hr, hr, 8), :], sibp.at[sub], x_sent, xrecv.at[sub], sibling)

    def weigh(subs):
        for sub in subs:
            landed(rows.at[:, pl.ds(0, hr), :], srecv.at[sub])
        blocks = [at(sub * UR, UR, 8) for sub in subs]
        parts = [at((2 * (sub // HALVES) + core) * NR + sub % HALVES * hr, hr, 8) for sub in subs for core in range(2)]
        f = jnp.concatenate([rows[0, b, :] for b in blocks], axis=0)
        cross = lax.dot_general(f, cols[0], (((1,), (1,)), ((), ())), precision=lax.Precision.HIGHEST, preferred_element_type=jnp.float32)
        g = jnp.concatenate([accv[b, :] for b in parts], axis=0)
        for q in range(1, Q):
            panel = jnp.concatenate([rows[q, b, :] for b in blocks], axis=0)
            g = g + dot3(split(panel), (chi[q], clo[q]), 1, 1)
        for i, b in enumerate(parts):
            accv[b, :] = g[i * hr:(i + 1) * hr, :]
        dist = jnp.sum(f * f, axis=1, keepdims=True) + ncol[0:1, :] - 2.0 * cross
        return f, g * jnp.exp(-decay_rate * dist)

    def row_part(subs, f, w):
        s = jnp.sum(w, axis=1, keepdims=True)
        part = grad_scale * (dot3(split(w), (chi[0], clo[0]), 1, 0) - s * f)
        for i, sub in enumerate(subs):
            rowp[at(sub * UR, UR, 8), :] = part[i * UR:(i + 1) * UR, :]
        for sub in subs:
            exchange(sub).start()

    def finish(subs):
        for sub in subs:
            exchange(sub).wait_recv()
            zs, h = sub // HALVES, sub % HALVES
            total = rowp[at(sub * UR + k * hr, hr, 8), :] + sibp[sub]

            @pl.when(zs == z)
            def _():
                rgbuf[z, at(h * hr, hr, 8), :] = total

            @pl.when(zs != z)
            def _():
                sumb[sub] = total
                remote(sumb.at[sub], rgbuf.at[z, at(h * hr, hr, 8), :], row_sent, row_in, (me_r, 2 * zs + k)).start()

    pairs = HALVES * Z // 2 - 1

    def pair_at(j):
        return [by_place(table, 2 * j + i) for i in range(2)]

    def step(j, carry):
        @pl.when(j > 0)
        def _():
            lax.fori_loop(by_place(need, j - 1), by_place(need, j), slot, 0)
            finish(pair_at(j - 1))

        subs = pair_at(j)
        f, w = weigh(subs)
        row_part(subs, f, w)
        colacc[...] += dot3(split(w.T), split(f), 1, 0)
        tacc[...] += jnp.broadcast_to(jnp.sum(w, axis=0, keepdims=True), tacc.shape)
        return carry

    lax.fori_loop(0, pairs, step, 0)

    tcol = jnp.broadcast_to(tacc[0:1, :], (128, tacc.shape[1])).T[:, 0:1]
    colacc[...] = grad_scale * (colacc[...] - tcol * cols[0])

    def push_grad(p, carry):
        to = (me_r + p) % R
        remote(colacc.at[at(to * NC, NC, 8), :], colr.at[me_r], grad_sent, grad_in, (to, me_c)).start()
        return carry

    lax.fori_loop(1, R, push_grad, 0)
    finish(pair_at(jnp.int32(pairs - 1)))

    landed(lfeat.at[pl.ds(0, R - 1), :, 0], feat_in)

    def pass_on(p, carry):
        block = lfeat.at[(me_r + p) % R, :, k]
        remote(block, block, pass_sent, pass_in, sibling).start()
        return carry

    lax.fori_loop(1, R, pass_on, 0)

    for s in range(LATE):
        lax.fori_loop(by_place(need, pairs + s - 1), by_place(need, pairs + s), slot, 0)
        if s:
            finish([late[s - 1]])
        f, w = weigh([late[s]])
        wlate[:, s * UR:(s + 1) * UR] = w.T
        for core in range(2):
            lfeat[me_r, s, core] = f[core * hr:(core + 1) * hr, :]
        if s == LATE - 1:
            def push_w(p, carry):
                to = (me_r + p) % R
                remote(wlate.at[at(to * NC, NC, 8), :], wlin.at[me_r], w_sent, w_in, (to, me_c)).start()
                return carry

            lax.fori_loop(1, R, push_w, 0)
            wlin[me_r] = wlate[at(me_r * NC, NC, 8), :]
        row_part([late[s]], f, w)

    landed(lfeat.at[pl.ds(0, R - 1), :, 0], pass_in)
    behind = split(lfeat[...].reshape(R * LATE * UR, F))
    finish([late[LATE - 1]])
    landed(colr.at[pl.ds(0, R - 1)], grad_in)
    mine = at(me_r * NC, NC, 8)
    gc_out[...] = colacc[mine, :]

    def add_grad(p, carry):
        gc_out[...] += colr[(me_r + p) % R]
        return carry

    lax.fori_loop(1, R, add_grad, 0)
    landed(wlin.at[pl.ds(0, R - 1)], w_in)
    w = jnp.concatenate([wlin[p] for p in range(R)], axis=1)
    gc_out[...] += grad_scale * (dot3(split(w), behind, 1, 0) - jnp.sum(w, axis=1, keepdims=True) * cols[0, mine, :])

    landed(rgbuf.at[pl.ds(0, Z - 1)], row_in)
    total = rgbuf[0]
    for zs in range(1, Z):
        total = total + rgbuf[zs]
    gr_out[...] = total

    for d in range(2):
        for y in range(Z - 1):
            @pl.when(place[d] == y)
            def _():
                landed(rows.at[:, pl.ds(0, (y + 1) * NR), :], sends.at[d])
    landed(rows.at[:, pl.ds(0, Z * NR), :], sib_sent)
    landed(cols.at[:, pl.ds(0, (2 if square else R - 1) * NC), :], col_sent)
    if square:
        landed(cols.at[:, pl.ds(0, NC), :], relay_sent)
    landed(sibp, x_sent)
    landed(rgbuf.at[pl.ds(0, Z - 1)], row_sent)
    landed(colr.at[pl.ds(0, R - 1)], grad_sent)
    landed(wlin.at[pl.ds(0, R - 1)], w_sent)
    landed(lfeat.at[pl.ds(0, R - 1), :, 0], feat_sent)
    landed(lfeat.at[pl.ds(0, R - 1), :, 0], pass_sent)


def put(a, b, c, x, y, w, sem):
    copies = [pltpu.make_async_copy(u, v, sem.at[i]) for i, (u, v) in enumerate(((a, x), (b, y), (c, w)))]
    for copy in copies:
        copy.start()
    for copy in copies:
        copy.wait()


def solution(mesh):
    R, C = mesh.shape["row"], mesh.shape["col"]
    in_specs = (
        P(("row", "col"), None),
        P(("col", "row"), None),
        P(("row", "col"), None),
        P(("col", "row"), None),
        P("row", "col"),
    )
    out_specs = (P("row", "col"), P(("row", "col"), None), P(("col", "row"), None))

    def local(fr, fc, pr, pc, acc):
        NR, F = fr.shape
        NC = fc.shape[0]
        Q = 1 + pr.shape[1] // F
        Z, n = C // 2, HALVES * Q
        hr, subs = NR // HALVES, HALVES * (C // 2)
        f32, bf16 = jnp.float32, jnp.bfloat16
        V, D = pltpu.VMEM, pltpu.SemaphoreType.DMA
        hbm = pl.BlockSpec(memory_space=pl.ANY)
        vmem = pl.BlockSpec(memory_space=pltpu.VMEM)
        shapes = (acc.shape, fr.shape, fc.shape)
        made = pl.pallas_call(
            functools.partial(kernel, R, C),
            out_shape=tuple(pltpu.VMEM(s, f32) for s in shapes),
            in_specs=[hbm] * 5,
            out_specs=(vmem,) * 3,
            scratch_shapes=[
                V((Q, C * NR, F), f32), V((Q, R * NC, F), f32),
                V((Q, R * NC, F), bf16), V((Q, R * NC, F), bf16),
                V((8, R * NC), f32),
                V((C * NR, F), f32), V((subs, hr, F), f32), V((subs, hr, F), f32), V((Z, NR, F), f32),
                V((R * NC, F), f32), V((8, R * NC), f32), V((R, NC, F), f32),
                V((R, LATE, 2, hr, F), f32), V((R * NC, LATE * 2 * hr), f32), V((R, NC, LATE * 2 * hr), f32),
                D((3,)), D((Z, n)), D((subs,)), D((2, Q)), D((subs,)), D((11,)), D((6,)),
            ],
            compiler_params=pltpu.CompilerParams(
                collective_id=0, has_side_effects=True, vmem_limit_bytes=56 * 1024 * 1024),
        )(fr, fc, pr, pc, acc)
        made = [pltpu.with_memory_space_constraint(m, pltpu.VMEM) for m in made]
        done = pl.pallas_call(
            put,
            out_shape=tuple(jax.ShapeDtypeStruct(s, f32) for s in shapes),
            in_specs=[vmem] * 3,
            out_specs=(hbm,) * 3,
            scratch_shapes=[D((3,))],
        )(*made)
        return tuple(done)

    return jax.shard_map(local, mesh=mesh, in_specs=in_specs, out_specs=out_specs, check_vma=False)
```

```python
import functools

import jax
import jax.numpy as jnp
from jax import lax
from jax.experimental import pallas as pl
from jax.experimental.pallas import tpu as pltpu
from jax.sharding import PartitionSpec as P

decay_rate = 0.125
grad_scale = 0.25
MESH = pl.DeviceIdType.MESH
HALVES = 2
LEAD = 4
RELAY_SLOTS = 2
LATE = 2


def split(x):
    hi = x.astype(jnp.bfloat16)
    return hi, (x - hi.astype(jnp.float32)).astype(jnp.bfloat16)


def dot3(a, b, ca, cb):
    dims = (((ca,), (cb,)), ((), ()))
    f = functools.partial(lax.dot_general, dimension_numbers=dims, preferred_element_type=jnp.float32)
    return f(a[0], b[0]) + (f(a[0], b[1]) + f(a[1], b[0]))


def split3(x):
    hi = x.astype(jnp.bfloat16)
    rest = x - hi.astype(jnp.float32)
    mid = rest.astype(jnp.bfloat16)
    return hi, mid, (rest - mid.astype(jnp.float32)).astype(jnp.bfloat16)


def dot6(a, b, ca, cb):
    dims = (((ca,), (cb,)), ((), ()))
    f = functools.partial(lax.dot_general, dimension_numbers=dims, preferred_element_type=jnp.float32)
    low = f(a[0], b[2]) + (f(a[2], b[0]) + f(a[1], b[1]))
    return f(a[0], b[0]) + ((f(a[0], b[1]) + f(a[1], b[0])) + low)


def order(n, depth, y, t):
    src, chunk = y * 0, t * 0
    found = y < 0
    for _ in range(depth):
        lead = t < LEAD
        done = jnp.logical_or(lead, t >= LEAD + n * y)
        take = jnp.logical_and(done, jnp.logical_not(found))
        src = jnp.where(take, y, src)
        chunk = jnp.where(take, jnp.where(lead, t, t - n * y), chunk)
        found = jnp.logical_or(found, done)
        y, t = y - 1, t - LEAD
    return src, chunk


def ready(n, depth, z, s, chunks):
    def seq(y):
        own = [(y, i) for i in range(n)]
        return own if y == 0 else own[:LEAD] + seq(y - 1) + own[LEAD:]

    if s == z:
        return 0
    y, ys = (z, s) if s < z else (depth - 1 - z, depth - 1 - s)
    return 1 + max(t for t, (a, i) in enumerate(seq(y - 1)) if a == ys and i in chunks)


def plan(Q, depth):
    n = HALVES * Q
    table, need, early = [], [], []
    steps = [(2 * j, 2 * j + 1) for j in range(HALVES * depth // 2 - 1)]
    steps += [(HALVES * depth - 2,), (HALVES * depth - 1,)]
    for z in range(depth):
        own = [(z, h) for h in range(HALVES)]
        far = [(s, h) for s in range(depth) for h in range(HALVES) if s != z]
        at = {(s, h): ready(n, depth, z, s, range(h * Q, h * Q + Q)) for s, h in own + far}
        far = sorted(far, key=lambda u: (at[u], -abs(u[0] - z)))
        end = z in (0, depth - 1)
        subs = own + far if end else far + own
        total = n * max(z, depth - 1 - z)
        late = max(ready(n, depth, z, s, (h * Q,)) for s, h in subs[-LATE:])
        first = min(total, max(late, n + LEAD - 1))
        early.append((first, first if end else max(first, total - 1)))
        taken, row = first if end else total, []
        for j, step in enumerate(steps):
            taken = max(taken, min(total, max(at[subs[i]] for i in step) + 1) if j else taken)
            row.append(taken)
        table.append([s * HALVES + h for s, h in subs])
        need.append(row)
    return table, need, early


def pick(values, at):
    out = jnp.int32(values[0])
    for i, v in enumerate(values[1:], 1):
        out = jnp.where(at == i, jnp.int32(v), out)
    return out


def kernel(R, C, fr, fc, pr, pc, acc, accv, gr_out, gc_out,
           rows, cols, chi, clo, cend, ncol, rowp, sibp, sumb, inbox, csum, colacc, tacc, colr, lfeat, lkern, wlate, wlin,
           lsem, rrecv, srecv, crecv, xrecv, sends, bulk):
    me_r, me_c = lax.axis_index("row"), lax.axis_index("col")
    z, k = me_c // 2, me_c % 2
    Z = C // 2
    NR, F = fr.shape
    NC = fc.shape[0]
    Q = 1 + pr.shape[1] // F
    n = HALVES * Q
    hr = NR // HALVES
    UR = 2 * hr
    sibling = (me_r, me_c + 1 - 2 * k)
    place = (z, Z - 1 - z)
    step_to = (2, -2)
    table, need, early = plan(Q, Z)
    square = R == 4
    near = (me_r // 2 * 2 + 1 - me_r % 2, (1 - me_r // 2) * 2 + me_r % 2)
    across = R - 1 - me_r
    z_sent, sib_sent, col_sent, relay_sent, x_sent, row_sent, grad_sent, w_sent, feat_sent, pass_sent = (
        sends.at[i] for i in (0, 2, 3, 4, 5, 6, 7, 8, 9, 10))
    grad_in, w_in, feat_in, pass_in, relay_in = (bulk.at[i] for i in range(2, 7))

    def at(start, size, mult):
        return pl.ds(pl.multiple_of(start, mult), size)

    def remote(src, dst, ss, rs, dev):
        return pltpu.make_async_remote_copy(src_ref=src, dst_ref=dst, send_sem=ss, recv_sem=rs, device_id=dev, device_id_type=MESH)

    def landed(ref, sem):
        pltpu.make_async_copy(ref, ref, sem).wait()

    def place_of(zs, h, core):
        return ((zs * HALVES + h) * 2 + core) * hr

    def rchunk(zs, core, i):
        return rows.at[i % Q, at(place_of(zs, i // Q, core), hr, 8), :]

    def own_chunk(i):
        q, h = i % Q, i // Q
        src = fr if q == 0 else pr
        return src.at[pl.ds(h * hr, hr), pl.ds(max(q - 1, 0) * F, F)]

    def own_cols(q):
        return fc if q == 0 else pc.at[:, pl.ds((q - 1) * F, F)]

    def zcopy(d, zs, i, src=None):
        dst = rchunk(zs, k, i)
        return remote(dst if src is None else src, dst, sends.at[d], rrecv.at[zs, i], (me_r, me_c + step_to[d]))

    def scopy(zs, i, src=None):
        dst = rchunk(zs, k, i)
        return remote(dst if src is None else src, dst, sib_sent, srecv.at[zs * HALVES + i // Q, min(i % Q, 1) if isinstance(i, int) else (i % Q > 0).astype(jnp.int32)], sibling)

    for q in range(Q):
        for h in range(HALVES):
            pltpu.make_async_copy(own_chunk(h * Q + q), rchunk(z, k, h * Q + q), lsem.at[0]).start()
        pltpu.make_async_copy(own_cols(q), cols.at[q, at(me_r * NC, NC, 8), :], lsem.at[1]).start()
    acc_in = pltpu.make_async_copy(acc, accv, lsem.at[2])
    acc_in.start()

    barrier = pltpu.get_barrier_semaphore()
    if square:
        for axis in range(2):
            pl.semaphore_signal(barrier, inc=1, device_id=(near[axis], me_c), device_id_type=MESH)
    else:
        def greet(p, carry):
            pl.semaphore_signal(barrier, inc=1, device_id=((me_r + p) % R, me_c), device_id_type=MESH)
            return carry

        lax.fori_loop(1, R, greet, 0)
    pl.semaphore_signal(barrier, inc=1, device_id=sibling, device_id_type=MESH)
    for d in range(2):
        @pl.when(place[d] < Z - 1)
        def _():
            pl.semaphore_signal(barrier, inc=1, device_id=(me_r, me_c + step_to[d]), device_id_type=MESH)
    greeted = (2 if square else R - 1) + 1
    pl.semaphore_wait(barrier, greeted + (z > 0).astype(jnp.int32) + (z < Z - 1).astype(jnp.int32))

    def zown(d, lo, hi):
        for i in range(lo, hi):
            zcopy(d, z, i, own_chunk(i)).start()

    for d in range(2):
        @pl.when(place[d] < Z - 1)
        def _():
            zown(d, 0, LEAD)

    def own_push(axis, q):
        block = cols.at[q, at(me_r * NC, NC, 8), :]
        return remote(own_cols(q), block, col_sent, crecv.at[axis, q], (near[axis], me_c))

    def own_arrive(axis, q):
        block = cols.at[q, at(near[axis] * NC, NC, 8), :]
        return remote(block, block, col_sent, crecv.at[axis, q], (near[axis], me_c))

    def relay(axis, q):
        block = cols.at[q, at(near[axis] * NC + axis * (NC // 2), NC // 2, 8), :]
        return remote(block, block, relay_sent, relay_in, (near[1 - axis], me_c))

    def push_cols(p, carry):
        for q in range(Q):
            block = cols.at[q, at(me_r * NC, NC, 8), :]
            remote(own_cols(q), block, col_sent, relay_in, ((me_r + p) % R, me_c)).start()
        return carry

    if square:
        for q in range(Q):
            for axis in range(2):
                own_push(axis, q).start()
    else:
        lax.fori_loop(1, R, push_cols, 0)
    for d in range(2):
        @pl.when(place[d] == 0)
        def _():
            zown(d, LEAD, n)
    for i in range(n):
        scopy(z, i, own_chunk(i)).start()

    def slot(t, carry):
        for d in range(2):
            y = place[d]

            @pl.when(t < n * y)
            def _():
                ys, i = order(n, Z, y - 1, t)
                zs = ys if d == 0 else Z - 1 - ys
                zcopy(d, zs, i).wait_recv()

                @pl.when(y < Z - 1)
                def _():
                    zcopy(d, zs, i).start()

                scopy(zs, i).start()

                @pl.when(jnp.logical_and(t == n * y - 1, y < Z - 1))
                def _():
                    zown(d, LEAD, n)

        return carry

    def by_place(values, j):
        out = pick([row[j] for row in values], z) if isinstance(j, int) else None
        if out is None:
            out = pick(values[0], j)
            for place_z in range(1, Z):
                out = jnp.where(z == place_z, pick(values[place_z], j), out)
        return out

    passed = 0
    if square:
        for q in range(Q):
            upto = min(RELAY_SLOTS * (q + 1), min(row[0] for row in early))
            lax.fori_loop(passed, upto, slot, 0)
            passed = upto
            for axis in range(2):
                own_arrive(axis, q).wait_recv()
                relay(axis, q).start()
    lax.fori_loop(passed, by_place(early, 0), slot, 0)

    landed(rows.at[:, pl.ds(0, NR), :], lsem.at[0])
    landed(cols.at[:, pl.ds(0, NC), :], lsem.at[1])
    acc_in.wait()
    landed(cols.at[:, pl.ds(0, NC if square else (R - 1) * NC), :], relay_in)

    late = [by_place(table, HALVES * Z - LATE + s) for s in range(LATE)]

    def push_late(p, carry):
        for s in range(LATE):
            src = rows.at[0, at(late[s] * UR + k * hr, hr, 8), :]
            remote(src, lfeat.at[me_r, s, k], feat_sent, feat_in, ((me_r + p) % R, me_c)).start()
        return carry

    lax.fori_loop(1, R, push_late, 0)

    for q in range(Q):
        hi, lo = split(cols[q])
        chi[q] = hi
        clo[q] = lo
    feats = cols[0]
    cend[...] = split3(feats)[2]
    ones = jnp.ones((8, F), jnp.bfloat16)
    ncol[...] = sum(lax.dot_general(
        ones, piece, (((1,), (1,)), ((), ())), preferred_element_type=jnp.float32) for piece in reversed(split3(feats * feats)))
    colacc[...] = jnp.zeros_like(colacc)
    tacc[...] = jnp.zeros_like(tacc)

    def exchange(sub):
        return remote(rowp.at[at(sub * UR + (1 - k) * hr, hr, 8), :], sibp.at[sub], x_sent, xrecv.at[sub], sibling)

    def take(subs, q):
        for sub in subs:
            landed(rows.at[:Q - 1 if q else 1, pl.ds(0, hr), :], srecv.at[sub, min(q, 1)])

    def kern(subs):
        take(subs, 0)
        f = jnp.concatenate([rows[0, at(sub * UR, UR, 8), :] for sub in subs], axis=0)
        pieces = split3(f)
        cross = dot6(pieces, (chi[0], clo[0], cend[...]), 1, 1)
        dist = jnp.sum(f * f, axis=1, keepdims=True) + ncol[0:1, :] - 2.0 * cross
        return f, pieces, jnp.exp(-decay_rate * dist)

    def gram(subs):
        take(subs, 1)
        parts = [at((2 * (sub // HALVES) + core) * NR + sub % HALVES * hr, hr, 8) for sub in subs for core in range(2)]
        g = jnp.concatenate([accv[b, :] for b in parts], axis=0)
        for q in range(1, Q):
            panel = jnp.concatenate([rows[q, at(sub * UR, UR, 8), :] for sub in subs], axis=0)
            g = g + dot3(split(panel), (chi[q], clo[q]), 1, 1)
        for i, b in enumerate(parts):
            accv[b, :] = g[i * hr:(i + 1) * hr, :]
        return g

    def row_part(subs, f, w):
        s = jnp.sum(w, axis=1, keepdims=True)
        part = grad_scale * (dot3(split(w), (chi[0], clo[0]), 1, 0) - s * f)
        for i, sub in enumerate(subs):
            rowp[at(sub * UR, UR, 8), :] = part[i * UR:(i + 1) * UR, :]
        for sub in subs:
            exchange(sub).start()

    def inward(end):
        return 1 if end == 0 else Z - 2

    def finish(subs):
        for sub in subs:
            exchange(sub).wait_recv()
            zs, h = sub // HALVES, sub % HALVES
            total = rowp[at(sub * UR + k * hr, hr, 8), :] + sibp[sub]
            own = zs == z
            group = jnp.where(own, 0, jnp.where(zs == 0, 1, jnp.where(zs == Z - 1, 2, 0)))
            to = jnp.where(group == 0, zs, jnp.where(group == 1, inward(0), inward(1)))
            dst = inbox.at[group * Z + z, at(h * hr, hr, 8), :]

            @pl.when(to == z)
            def _():
                dst[...] = total

            @pl.when(to != z)
            def _():
                sumb[sub] = total
                remote(sumb.at[sub], dst, row_sent, bulk.at[jnp.minimum(group, 1)], (me_r, 2 * to + k)).start()

    def collect():
        for e, end in enumerate((0, Z - 1)):
            @pl.when(jnp.logical_and(z == inward(end), z != end))
            def _():
                if Z > 2:
                    landed(inbox.at[pl.ds(0, Z - 2)], bulk.at[1])
                terms = [inbox[(e + 1) * Z + zs] for zs in range(Z) if zs != end]
                csum[e] = sum(terms[1:], terms[0])
                remote(csum.at[e], inbox.at[z], row_sent, bulk.at[0], (me_r, 2 * end + k)).start()

    pairs = HALVES * Z // 2 - 1

    def pair_at(j):
        return [by_place(table, 2 * j + i) for i in range(2)]

    lax.fori_loop(by_place(early, 0), by_place(early, 1), slot, 0)
    f, _, weight = kern(late)
    lkern[...] = weight
    for s in range(LATE):
        for core in range(2):
            lfeat[me_r, s, core] = f[(2 * s + core) * hr:(2 * s + core + 1) * hr, :]
    lax.fori_loop(by_place(early, 1), by_place(need, 0), slot, 0)

    def step(j, carry):
        @pl.when(j > 0)
        def _():
            lax.fori_loop(by_place(need, j - 1), by_place(need, j), slot, 0)

        subs = pair_at(j)
        f, pieces, weight = kern(subs)
        w = gram(subs) * weight
        row_part(subs, f, w)
        colacc[...] += dot3(split(w.T), pieces[:2], 1, 0)
        tacc[...] += jnp.broadcast_to(jnp.sum(w, axis=0, keepdims=True), tacc.shape)

        @pl.when(j > 0)
        def _():
            finish(pair_at(j - 1))

        return carry

    lax.fori_loop(0, pairs, step, 0)

    tcol = jnp.broadcast_to(tacc[0:1, :], (128, tacc.shape[1])).T[:, 0:1]
    colacc[...] = grad_scale * (colacc[...] - tcol * cols[0])

    def push_grad(p, carry):
        to = (me_r + p) % R
        remote(colacc.at[at(to * NC, NC, 8), :], colr.at[me_r], grad_sent, grad_in, (to, me_c)).start()
        return carry

    lax.fori_loop(1, R, push_grad, 0)
    finish(pair_at(jnp.int32(pairs - 1)))

    landed(lfeat.at[pl.ds(0, R - 1), :, 0], feat_in)

    def pass_on(p, carry):
        block = lfeat.at[(me_r + p) % R, :, k]
        remote(block, block, pass_sent, pass_in, sibling).start()
        return carry

    lax.fori_loop(1, R, pass_on, 0)

    for s in range(LATE):
        lax.fori_loop(by_place(need, pairs + s - 1), by_place(need, pairs + s), slot, 0)
        if s:
            finish([late[s - 1]])
        w = gram([late[s]]) * lkern[s * UR:(s + 1) * UR, :]
        wlate[:, s * UR:(s + 1) * UR] = w.T
        if s == LATE - 1:
            def push_w(p, carry):
                to = (me_r + p) % R
                remote(wlate.at[at(to * NC, NC, 8), :], wlin.at[me_r], w_sent, w_in, (to, me_c)).start()
                return carry

            lax.fori_loop(1, R, push_w, 0)
            wlin[me_r] = wlate[at(me_r * NC, NC, 8), :]
        row_part([late[s]], rows[0, at(late[s] * UR, UR, 8), :], w)

    landed(lfeat.at[pl.ds(0, R - 1), :, 0], pass_in)
    behind = split(lfeat[...].reshape(R * LATE * UR, F))
    finish([late[LATE - 1]])
    collect()
    landed(colr.at[pl.ds(0, R - 1)], grad_in)
    mine = at(me_r * NC, NC, 8)
    gc_out[...] = colacc[mine, :]

    def add_grad(p, carry):
        gc_out[...] += colr[(me_r + p) % R]
        return carry

    lax.fori_loop(1, R, add_grad, 0)
    landed(wlin.at[pl.ds(0, R - 1)], w_in)
    w = jnp.concatenate([wlin[p] for p in range(R)], axis=1)
    gc_out[...] += grad_scale * (dot3(split(w), behind, 1, 0) - jnp.sum(w, axis=1, keepdims=True) * cols[0, mine, :])

    for end in (0, Z - 1):
        @pl.when(z == end)
        def _():
            landed(inbox.at[pl.ds(0, 1)], bulk.at[0])
            gr_out[...] = inbox[end] + inbox[inward(end)]

    @pl.when(jnp.logical_and(z > 0, z < Z - 1))
    def _():
        landed(inbox.at[pl.ds(0, Z - 1)], bulk.at[0])
        total = inbox[0]
        for zs in range(1, Z):
            total = total + inbox[zs]
        gr_out[...] = total

    for d in range(2):
        for y in range(Z - 1):
            @pl.when(place[d] == y)
            def _():
                landed(rows.at[:, pl.ds(0, (y + 1) * NR), :], sends.at[d])
    landed(rows.at[:, pl.ds(0, Z * NR), :], sib_sent)
    landed(cols.at[:, pl.ds(0, (2 if square else R - 1) * NC), :], col_sent)
    if square:
        landed(cols.at[:, pl.ds(0, NC), :], relay_sent)
    landed(sibp, x_sent)
    landed(inbox.at[pl.ds(0, Z - 1)], row_sent)
    landed(colr.at[pl.ds(0, R - 1)], grad_sent)
    landed(wlin.at[pl.ds(0, R - 1)], w_sent)
    landed(lfeat.at[pl.ds(0, R - 1), :, 0], feat_sent)
    landed(lfeat.at[pl.ds(0, R - 1), :, 0], pass_sent)


def put(a, b, c, x, y, w, sem):
    copies = [pltpu.make_async_copy(u, v, sem.at[i]) for i, (u, v) in enumerate(((a, x), (b, y), (c, w)))]
    for copy in copies:
        copy.start()
    for copy in copies:
        copy.wait()


def solution(mesh):
    R, C = mesh.shape["row"], mesh.shape["col"]
    in_specs = (
        P(("row", "col"), None),
        P(("col", "row"), None),
        P(("row", "col"), None),
        P(("col", "row"), None),
        P("row", "col"),
    )
    out_specs = (P("row", "col"), P(("row", "col"), None), P(("col", "row"), None))

    def local(fr, fc, pr, pc, acc):
        NR, F = fr.shape
        NC = fc.shape[0]
        Q = 1 + pr.shape[1] // F
        Z, n = C // 2, HALVES * Q
        hr, subs = NR // HALVES, HALVES * (C // 2)
        f32, bf16 = jnp.float32, jnp.bfloat16
        V, D = pltpu.VMEM, pltpu.SemaphoreType.DMA
        hbm = pl.BlockSpec(memory_space=pl.ANY)
        vmem = pl.BlockSpec(memory_space=pltpu.VMEM)
        shapes = (acc.shape, fr.shape, fc.shape)
        made = pl.pallas_call(
            functools.partial(kernel, R, C),
            out_shape=tuple(pltpu.VMEM(s, f32) for s in shapes),
            in_specs=[hbm] * 5,
            out_specs=(vmem,) * 3,
            scratch_shapes=[
                V((Q, C * NR, F), f32), V((Q, R * NC, F), f32),
                V((Q, R * NC, F), bf16), V((Q, R * NC, F), bf16),
                V((R * NC, F), bf16), V((8, R * NC), f32),
                V((C * NR, F), f32), V((subs, hr, F), f32), V((subs, hr, F), f32), V((3 * Z, NR, F), f32), V((2, NR, F), f32),
                V((R * NC, F), f32), V((8, R * NC), f32), V((R, NC, F), f32),
                V((R, LATE, 2, hr, F), f32), V((LATE * 2 * hr, R * NC), f32), V((R * NC, LATE * 2 * hr), f32), V((R, NC, LATE * 2 * hr), f32),
                D((3,)), D((Z, n)), D((subs, 2)), D((2, Q)), D((subs,)), D((11,)), D((7,)),
            ],
            compiler_params=pltpu.CompilerParams(
                collective_id=0, has_side_effects=True, vmem_limit_bytes=56 * 1024 * 1024),
        )(fr, fc, pr, pc, acc)
        made = [pltpu.with_memory_space_constraint(m, pltpu.VMEM) for m in made]
        done = pl.pallas_call(
            put,
            out_shape=tuple(jax.ShapeDtypeStruct(s, f32) for s in shapes),
            in_specs=[vmem] * 3,
            out_specs=(hbm,) * 3,
            scratch_shapes=[D((3,))],
        )(*made)
        return tuple(done)

    return jax.shard_map(local, mesh=mesh, in_specs=in_specs, out_specs=out_specs, check_vma=False)
```

```python
import functools

import jax
import jax.numpy as jnp
from jax import lax
from jax.experimental import pallas as pl
from jax.experimental.pallas import tpu as pltpu
from jax.sharding import PartitionSpec as P

decay_rate = 0.125
grad_scale = 0.25
MESH = pl.DeviceIdType.MESH
HALVES = 2
LEAD = 4
RELAY_SLOTS = 2
LATE = 2


def split(x):
    hi = x.astype(jnp.bfloat16)
    return hi, (x - hi.astype(jnp.float32)).astype(jnp.bfloat16)


def dot3(a, b, ca, cb):
    dims = (((ca,), (cb,)), ((), ()))
    f = functools.partial(lax.dot_general, dimension_numbers=dims, preferred_element_type=jnp.float32)
    return f(a[0], b[0]) + (f(a[0], b[1]) + f(a[1], b[0]))


def split3(x):
    hi = x.astype(jnp.bfloat16)
    rest = x - hi.astype(jnp.float32)
    mid = rest.astype(jnp.bfloat16)
    return hi, mid, (rest - mid.astype(jnp.float32)).astype(jnp.bfloat16)


def order(n, depth, y, t):
    src, chunk = y * 0, t * 0
    found = y < 0
    for _ in range(depth):
        lead = t < LEAD
        done = jnp.logical_or(lead, t >= LEAD + n * y)
        take = jnp.logical_and(done, jnp.logical_not(found))
        src = jnp.where(take, y, src)
        chunk = jnp.where(take, jnp.where(lead, t, t - n * y), chunk)
        found = jnp.logical_or(found, done)
        y, t = y - 1, t - LEAD
    return src, chunk


def ready(n, depth, z, s, chunks):
    def seq(y):
        own = [(y, i) for i in range(n)]
        return own if y == 0 else own[:LEAD] + seq(y - 1) + own[LEAD:]

    if s == z:
        return 0
    y, ys = (z, s) if s < z else (depth - 1 - z, depth - 1 - s)
    return 1 + max(t for t, (a, i) in enumerate(seq(y - 1)) if a == ys and i in chunks)


def plan(Q, depth):
    n = HALVES * Q
    table, need, early = [], [], []
    steps = [(2 * j, 2 * j + 1) for j in range(HALVES * depth // 2 - 1)]
    steps += [(HALVES * depth - 2,), (HALVES * depth - 1,)]
    for z in range(depth):
        own = [(z, h) for h in range(HALVES)]
        far = [(s, h) for s in range(depth) for h in range(HALVES) if s != z]
        at = {(s, h): ready(n, depth, z, s, range(h * Q, h * Q + Q)) for s, h in own + far}
        far = sorted(far, key=lambda u: (at[u], -abs(u[0] - z)))
        end = z in (0, depth - 1)
        subs = own + far if end else far + own
        total = n * max(z, depth - 1 - z)
        late = max(ready(n, depth, z, s, (h * Q,)) for s, h in subs[-LATE:])
        first = min(total, max(late, n + LEAD - 2))
        early.append((first,))
        taken, row = first if end else total, []
        for j, step in enumerate(steps):
            taken = max(taken, min(total, max(at[subs[i]] for i in step) + 1) if j else taken)
            row.append(taken if len(step) > 1 else total)
        table.append([s * HALVES + h for s, h in subs])
        need.append(row)
    return table, need, early


def pick(values, at):
    out = jnp.int32(values[0])
    for i, v in enumerate(values[1:], 1):
        out = jnp.where(at == i, jnp.int32(v), out)
    return out


def kernel(R, C, fr, fc, pr, pc, acc, accv, gr_out, gc_out,
           rows, cols, chi, clo, ncol, rowp, sibp, sumb, inbox, csum, colacc, tacc, colr, lfeat, wlate, wlin,
           lsem, rrecv, srecv, crecv, xrecv, sends, bulk):
    me_r, me_c = lax.axis_index("row"), lax.axis_index("col")
    z, k = me_c // 2, me_c % 2
    Z = C // 2
    NR, F = fr.shape
    NC = fc.shape[0]
    Q = 1 + pr.shape[1] // F
    n = HALVES * Q
    hr = NR // HALVES
    UR = 2 * hr
    sibling = (me_r, me_c + 1 - 2 * k)
    place = (z, Z - 1 - z)
    step_to = (2, -2)
    table, need, early = plan(Q, Z)
    square = R == 4
    near = (me_r // 2 * 2 + 1 - me_r % 2, (1 - me_r // 2) * 2 + me_r % 2)
    across = R - 1 - me_r
    z_sent, sib_sent, col_sent, relay_sent, x_sent, row_sent, grad_sent, w_sent, feat_sent, pass_sent = (
        sends.at[i] for i in (0, 2, 3, 4, 5, 6, 7, 8, 9, 10))
    row_in, grad_in, w_in, feat_in, pass_in, relay_in = (bulk.at[i] for i in range(6))
    half_in = 6

    def at(start, size, mult):
        return pl.ds(pl.multiple_of(start, mult), size)

    def remote(src, dst, ss, rs, dev):
        return pltpu.make_async_remote_copy(src_ref=src, dst_ref=dst, send_sem=ss, recv_sem=rs, device_id=dev, device_id_type=MESH)

    def landed(ref, sem):
        pltpu.make_async_copy(ref, ref, sem).wait()

    def place_of(zs, h, core):
        return ((zs * HALVES + h) * 2 + core) * hr

    def rchunk(zs, core, i):
        return rows.at[i % Q, at(place_of(zs, i // Q, core), hr, 8), :]

    def own_chunk(i):
        q, h = i % Q, i // Q
        src = fr if q == 0 else pr
        return src.at[pl.ds(h * hr, hr), pl.ds(max(q - 1, 0) * F, F)]

    def own_cols(q):
        return fc if q == 0 else pc.at[:, pl.ds((q - 1) * F, F)]

    def zcopy(d, zs, i, src=None):
        dst = rchunk(zs, k, i)
        return remote(dst if src is None else src, dst, sends.at[d], rrecv.at[zs, i], (me_r, me_c + step_to[d]))

    def scopy(zs, i, src=None):
        dst = rchunk(zs, k, i)
        return remote(dst if src is None else src, dst, sib_sent, srecv.at[zs * HALVES + i // Q], sibling)

    for q in range(Q):
        for h in range(HALVES):
            pltpu.make_async_copy(own_chunk(h * Q + q), rchunk(z, k, h * Q + q), lsem.at[0]).start()
        pltpu.make_async_copy(own_cols(q), cols.at[q, at(me_r * NC, NC, 8), :], lsem.at[1]).start()
    acc_in = pltpu.make_async_copy(acc, accv, lsem.at[2])
    acc_in.start()

    barrier = pltpu.get_barrier_semaphore()
    if square:
        for axis in range(2):
            pl.semaphore_signal(barrier, inc=1, device_id=(near[axis], me_c), device_id_type=MESH)
    else:
        def greet(p, carry):
            pl.semaphore_signal(barrier, inc=1, device_id=((me_r + p) % R, me_c), device_id_type=MESH)
            return carry

        lax.fori_loop(1, R, greet, 0)
    pl.semaphore_signal(barrier, inc=1, device_id=sibling, device_id_type=MESH)
    for d in range(2):
        @pl.when(place[d] < Z - 1)
        def _():
            pl.semaphore_signal(barrier, inc=1, device_id=(me_r, me_c + step_to[d]), device_id_type=MESH)
    greeted = (2 if square else R - 1) + 1
    pl.semaphore_wait(barrier, greeted + (z > 0).astype(jnp.int32) + (z < Z - 1).astype(jnp.int32))

    def zown(d, lo, hi):
        for i in range(lo, hi):
            zcopy(d, z, i, own_chunk(i)).start()

    for d in range(2):
        @pl.when(place[d] < Z - 1)
        def _():
            zown(d, 0, LEAD)

    def own_push(axis, q):
        block = cols.at[q, at(me_r * NC, NC, 8), :]
        return remote(own_cols(q), block, col_sent, crecv.at[axis, q], (near[axis], me_c))

    def own_arrive(axis, q):
        block = cols.at[q, at(near[axis] * NC, NC, 8), :]
        return remote(block, block, col_sent, crecv.at[axis, q], (near[axis], me_c))

    def relay(axis, q):
        block = cols.at[q, at(near[axis] * NC + axis * (NC // 2), NC // 2, 8), :]
        return remote(block, block, relay_sent, relay_in, (near[1 - axis], me_c))

    def push_cols(p, carry):
        for q in range(Q):
            block = cols.at[q, at(me_r * NC, NC, 8), :]
            remote(own_cols(q), block, col_sent, relay_in, ((me_r + p) % R, me_c)).start()
        return carry

    if square:
        for q in range(Q):
            for axis in range(2):
                own_push(axis, q).start()
    else:
        lax.fori_loop(1, R, push_cols, 0)
    for d in range(2):
        @pl.when(place[d] == 0)
        def _():
            zown(d, LEAD, n)
    for i in range(n):
        scopy(z, i, own_chunk(i)).start()

    def slot(t, carry):
        for d in range(2):
            y = place[d]

            @pl.when(t < n * y)
            def _():
                ys, i = order(n, Z, y - 1, t)
                zs = ys if d == 0 else Z - 1 - ys
                zcopy(d, zs, i).wait_recv()

                @pl.when(y < Z - 1)
                def _():
                    zcopy(d, zs, i).start()

                scopy(zs, i).start()

                @pl.when(jnp.logical_and(t == n * y - 1, y < Z - 1))
                def _():
                    zown(d, LEAD, n)

        return carry

    def by_place(values, j):
        out = pick([row[j] for row in values], z) if isinstance(j, int) else None
        if out is None:
            out = pick(values[0], j)
            for place_z in range(1, Z):
                out = jnp.where(z == place_z, pick(values[place_z], j), out)
        return out

    passed = 0
    if square:
        for q in range(Q):
            until = min(RELAY_SLOTS * (q + 1), min(row[0] for row in early))
            lax.fori_loop(passed, until, slot, 0)
            passed = until
            for axis in range(2):
                own_arrive(axis, q).wait_recv()
                relay(axis, q).start()
    lax.fori_loop(passed, by_place(early, 0), slot, 0)

    landed(rows.at[:, pl.ds(0, NR), :], lsem.at[0])
    landed(cols.at[:, pl.ds(0, NC), :], lsem.at[1])
    acc_in.wait()
    landed(cols.at[:, pl.ds(0, NC if square else (R - 1) * NC), :], relay_in)

    late = [by_place(table, HALVES * Z - LATE + s) for s in range(LATE)]

    def push_late(p, carry):
        for s in range(LATE):
            src = rows.at[0, at(late[s] * UR + k * hr, hr, 8), :]
            remote(src, lfeat.at[me_r, s, k], feat_sent, feat_in, ((me_r + p) % R, me_c)).start()
        return carry

    lax.fori_loop(1, R, push_late, 0)

    for q in range(Q):
        hi, lo = split(cols[q])
        chi[q] = hi
        clo[q] = lo
    feats = cols[0]
    ones = jnp.ones((8, F), jnp.bfloat16)
    ncol[...] = sum(lax.dot_general(
        ones, piece, (((1,), (1,)), ((), ())), preferred_element_type=jnp.float32) for piece in reversed(split3(feats * feats)))
    colacc[...] = jnp.zeros_like(colacc)
    tacc[...] = jnp.zeros_like(tacc)

    def exchange(sub):
        return remote(rowp.at[at(sub * UR + (1 - k) * hr, hr, 8), :], sibp.at[sub], x_sent, xrecv.at[sub], sibling)

    def weigh(subs):
        for sub in subs:
            landed(rows.at[:, pl.ds(0, hr), :], srecv.at[sub])
        blocks = [at(sub * UR, UR, 8) for sub in subs]
        parts = [at((2 * (sub // HALVES) + core) * NR + sub % HALVES * hr, hr, 8) for sub in subs for core in range(2)]
        f = jnp.concatenate([rows[0, b, :] for b in blocks], axis=0)
        cross = lax.dot_general(f, cols[0], (((1,), (1,)), ((), ())), precision=lax.Precision.HIGHEST, preferred_element_type=jnp.float32)
        g = jnp.concatenate([accv[b, :] for b in parts], axis=0)
        for q in range(1, Q):
            panel = jnp.concatenate([rows[q, b, :] for b in blocks], axis=0)
            g = g + dot3(split(panel), (chi[q], clo[q]), 1, 1)
        for i, b in enumerate(parts):
            accv[b, :] = g[i * hr:(i + 1) * hr, :]
        dist = jnp.sum(f * f, axis=1, keepdims=True) + ncol[0:1, :] - 2.0 * cross
        return f, g * jnp.exp(-decay_rate * dist)

    def row_part(subs, f, w):
        s = jnp.sum(w, axis=1, keepdims=True)
        part = grad_scale * (dot3(split(w), (chi[0], clo[0]), 1, 0) - s * f)
        for i, sub in enumerate(subs):
            rowp[at(sub * UR, UR, 8), :] = part[i * UR:(i + 1) * UR, :]
        for sub in subs:
            exchange(sub).start()

    def inward(end):
        return 1 if end == 0 else Z - 2

    def finish(subs):
        for sub in subs:
            exchange(sub).wait_recv()
            zs, h = sub // HALVES, sub % HALVES
            total = rowp[at(sub * UR + k * hr, hr, 8), :] + sibp[sub]
            own = zs == z
            straight = jnp.logical_or(own, zs == Z - 1 - z)
            group = jnp.where(straight, 0, jnp.where(zs == 0, 1, jnp.where(zs == Z - 1, 2, 0)))
            to = jnp.where(group == 0, zs, jnp.where(group == 1, inward(0), inward(1)))
            dst = inbox.at[group * Z + z, at(h * hr, hr, 8), :]

            @pl.when(to == z)
            def _():
                dst[...] = total

            @pl.when(to != z)
            def _():
                sumb[sub] = total
                got = bulk.at[jnp.where(group > 0, half_in + h, 0)]
                remote(sumb.at[sub], dst, row_sent, got, (me_r, 2 * to + k)).start()

    def collect():
        for e, end in enumerate((0, Z - 1)):
            @pl.when(jnp.logical_and(z == inward(end), z != end))
            def _():
                for h in range(HALVES):
                    part = pl.ds(h * hr, hr)
                    if Z > 3:
                        landed(inbox.at[pl.ds(0, Z - 3), part, :], bulk.at[half_in + h])
                    terms = [inbox[(e + 1) * Z + zs, part, :] for zs in range(1, Z - 1)]
                    csum[e, part, :] = sum(terms[1:], terms[0])
                    remote(csum.at[e, part, :], inbox.at[z, part, :], row_sent, row_in, (me_r, 2 * end + k)).start()

    pairs = HALVES * Z // 2 - 1

    def pair_at(j):
        return [by_place(table, 2 * j + i) for i in range(2)]

    lax.fori_loop(by_place(early, 0), by_place(need, 0), slot, 0)

    def upto(a, b):
        lax.fori_loop(a, b, slot, 0)

    def col_part(f, w):
        colacc[...] += dot3(split(w.T), split(f), 1, 0)
        tacc[...] += jnp.broadcast_to(jnp.sum(w, axis=0, keepdims=True), tacc.shape)

    def step(j, carry):
        @pl.when(j > 0)
        def _():
            upto(by_place(need, j - 1), by_place(need, j))

        subs = pair_at(j)
        f, w = weigh(subs)
        row_part(subs, f, w)
        col_part(f, w)

        @pl.when(j > 0)
        def _():
            finish(pair_at(j - 1))

        return carry

    lax.fori_loop(0, pairs - 1, step, 0)
    if pairs > 1:
        upto(by_place(need, pairs - 2), by_place(need, pairs - 1))
    final = pair_at(pairs - 1)
    stops = [by_place(need, pairs - 1)] + [by_place([[row[-1] - 2 + i] for row in need], 0) for i in range(3)]
    stops = [jnp.maximum(stops[0], stop) for stop in stops]
    f, w = weigh(final)
    upto(stops[0], stops[1])
    row_part(final, f, w)
    col_part(f, w)
    tcol = jnp.broadcast_to(tacc[0:1, :], (128, tacc.shape[1])).T[:, 0:1]
    colacc[...] = grad_scale * (colacc[...] - tcol * cols[0])

    def push_grad(p, carry):
        to = (me_r + p) % R
        remote(colacc.at[at(to * NC, NC, 8), :], colr.at[me_r], grad_sent, grad_in, (to, me_c)).start()
        return carry

    lax.fori_loop(1, R, push_grad, 0)
    upto(stops[1], stops[2])
    if pairs > 1:
        finish(pair_at(pairs - 2))
    finish(final)
    upto(stops[2], stops[3])

    landed(lfeat.at[pl.ds(0, R - 1), :, 0], feat_in)

    def pass_on(p, carry):
        block = lfeat.at[(me_r + p) % R, :, k]
        remote(block, block, pass_sent, pass_in, sibling).start()
        return carry

    lax.fori_loop(1, R, pass_on, 0)

    for s in range(LATE):
        f, w = weigh([late[s]])
        wlate[:, s * UR:(s + 1) * UR] = w.T
        for core in range(2):
            lfeat[me_r, s, core] = f[core * hr:(core + 1) * hr, :]
        if s == LATE - 1:
            def push_w(p, carry):
                to = (me_r + p) % R
                remote(wlate.at[at(to * NC, NC, 8), :], wlin.at[me_r], w_sent, w_in, (to, me_c)).start()
                return carry

            lax.fori_loop(1, R, push_w, 0)
            wlin[me_r] = wlate[at(me_r * NC, NC, 8), :]
        row_part([late[s]], f, w)
    finish([late[0]])

    landed(lfeat.at[pl.ds(0, R - 1), :, 0], pass_in)
    behind = split(lfeat[...].reshape(R * LATE * UR, F))
    finish([late[LATE - 1]])
    collect()
    landed(colr.at[pl.ds(0, R - 1)], grad_in)
    mine = at(me_r * NC, NC, 8)
    gc_out[...] = colacc[mine, :]

    def add_grad(p, carry):
        gc_out[...] += colr[(me_r + p) % R]
        return carry

    lax.fori_loop(1, R, add_grad, 0)
    landed(wlin.at[pl.ds(0, R - 1)], w_in)
    w = jnp.concatenate([wlin[p] for p in range(R)], axis=1)
    gc_out[...] += grad_scale * (dot3(split(w), behind, 1, 0) - jnp.sum(w, axis=1, keepdims=True) * cols[0, mine, :])

    for end in (0, Z - 1):
        @pl.when(z == end)
        def _():
            landed(inbox.at[pl.ds(0, 2)], row_in)
            gr_out[...] = inbox[end] + (inbox[inward(end)] + inbox[Z - 1 - end])

    @pl.when(jnp.logical_and(z > 0, z < Z - 1))
    def _():
        landed(inbox.at[pl.ds(0, Z - 1)], row_in)
        total = inbox[0]
        for zs in range(1, Z):
            total = total + inbox[zs]
        gr_out[...] = total

    for d in range(2):
        for y in range(Z - 1):
            @pl.when(place[d] == y)
            def _():
                landed(rows.at[:, pl.ds(0, (y + 1) * NR), :], sends.at[d])
    landed(rows.at[:, pl.ds(0, Z * NR), :], sib_sent)
    landed(cols.at[:, pl.ds(0, (2 if square else R - 1) * NC), :], col_sent)
    if square:
        landed(cols.at[:, pl.ds(0, NC), :], relay_sent)
    landed(sibp, x_sent)
    landed(inbox.at[pl.ds(0, Z - 1)], row_sent)
    landed(colr.at[pl.ds(0, R - 1)], grad_sent)
    landed(wlin.at[pl.ds(0, R - 1)], w_sent)
    landed(lfeat.at[pl.ds(0, R - 1), :, 0], feat_sent)
    landed(lfeat.at[pl.ds(0, R - 1), :, 0], pass_sent)


def put(a, b, c, x, y, w, sem):
    copies = [pltpu.make_async_copy(u, v, sem.at[i]) for i, (u, v) in enumerate(((a, x), (b, y), (c, w)))]
    for copy in copies:
        copy.start()
    for copy in copies:
        copy.wait()


def solution(mesh):
    R, C = mesh.shape["row"], mesh.shape["col"]
    in_specs = (
        P(("row", "col"), None),
        P(("col", "row"), None),
        P(("row", "col"), None),
        P(("col", "row"), None),
        P("row", "col"),
    )
    out_specs = (P("row", "col"), P(("row", "col"), None), P(("col", "row"), None))

    def local(fr, fc, pr, pc, acc):
        NR, F = fr.shape
        NC = fc.shape[0]
        Q = 1 + pr.shape[1] // F
        Z, n = C // 2, HALVES * Q
        hr, subs = NR // HALVES, HALVES * (C // 2)
        f32, bf16 = jnp.float32, jnp.bfloat16
        V, D = pltpu.VMEM, pltpu.SemaphoreType.DMA
        hbm = pl.BlockSpec(memory_space=pl.ANY)
        vmem = pl.BlockSpec(memory_space=pltpu.VMEM)
        shapes = (acc.shape, fr.shape, fc.shape)
        made = pl.pallas_call(
            functools.partial(kernel, R, C),
            out_shape=tuple(pltpu.VMEM(s, f32) for s in shapes),
            in_specs=[hbm] * 5,
            out_specs=(vmem,) * 3,
            scratch_shapes=[
                V((Q, C * NR, F), f32), V((Q, R * NC, F), f32),
                V((Q, R * NC, F), bf16), V((Q, R * NC, F), bf16),
                V((8, R * NC), f32),
                V((C * NR, F), f32), V((subs, hr, F), f32), V((subs, hr, F), f32), V((3 * Z, NR, F), f32), V((2, NR, F), f32),
                V((R * NC, F), f32), V((8, R * NC), f32), V((R, NC, F), f32),
                V((R, LATE, 2, hr, F), f32), V((R * NC, LATE * 2 * hr), f32), V((R, NC, LATE * 2 * hr), f32),
                D((3,)), D((Z, n)), D((subs,)), D((2, Q)), D((subs,)), D((11,)), D((8,)),
            ],
            compiler_params=pltpu.CompilerParams(
                collective_id=0, has_side_effects=True, vmem_limit_bytes=56 * 1024 * 1024),
        )(fr, fc, pr, pc, acc)
        made = [pltpu.with_memory_space_constraint(m, pltpu.VMEM) for m in made]
        done = pl.pallas_call(
            put,
            out_shape=tuple(jax.ShapeDtypeStruct(s, f32) for s in shapes),
            in_specs=[vmem] * 3,
            out_specs=(hbm,) * 3,
            scratch_shapes=[D((3,))],
        )(*made)
        return tuple(done)

    return jax.shard_map(local, mesh=mesh, in_specs=in_specs, out_specs=out_specs, check_vma=False)
```

```python
import functools

import jax
import jax.numpy as jnp
from jax import lax
from jax.experimental import pallas as pl
from jax.experimental.pallas import tpu as pltpu
from jax.sharding import PartitionSpec as P

decay_rate = 0.125
grad_scale = 0.25
MESH = pl.DeviceIdType.MESH
HALVES = 2
LEAD = 4
RELAY_SLOTS = 2
LATE = 2


def split(x):
    hi = x.astype(jnp.bfloat16)
    return hi, (x - hi.astype(jnp.float32)).astype(jnp.bfloat16)


def dot3(a, b, ca, cb):
    dims = (((ca,), (cb,)), ((), ()))
    f = functools.partial(lax.dot_general, dimension_numbers=dims, preferred_element_type=jnp.float32)
    return f(a[0], b[0]) + (f(a[0], b[1]) + f(a[1], b[0]))


def split3(x):
    hi = x.astype(jnp.bfloat16)
    rest = x - hi.astype(jnp.float32)
    mid = rest.astype(jnp.bfloat16)
    return hi, mid, (rest - mid.astype(jnp.float32)).astype(jnp.bfloat16)


def order(n, depth, y, t):
    src, chunk = y * 0, t * 0
    found = y < 0
    for _ in range(depth):
        lead = t < LEAD
        done = jnp.logical_or(lead, t >= LEAD + n * y)
        take = jnp.logical_and(done, jnp.logical_not(found))
        src = jnp.where(take, y, src)
        chunk = jnp.where(take, jnp.where(lead, t, t - n * y), chunk)
        found = jnp.logical_or(found, done)
        y, t = y - 1, t - LEAD
    return src, chunk


def ready(n, depth, z, s, chunks):
    def seq(y):
        own = [(y, i) for i in range(n)]
        return own if y == 0 else own[:LEAD] + seq(y - 1) + own[LEAD:]

    if s == z:
        return 0
    y, ys = (z, s) if s < z else (depth - 1 - z, depth - 1 - s)
    return 1 + max(t for t, (a, i) in enumerate(seq(y - 1)) if a == ys and i in chunks)


def plan(Q, depth):
    n = HALVES * Q
    table, need, early = [], [], []
    steps = [(2 * j, 2 * j + 1) for j in range(HALVES * depth // 2 - 1)]
    steps += [(HALVES * depth - 2,), (HALVES * depth - 1,)]
    for z in range(depth):
        own = [(z, h) for h in range(HALVES)]
        far = [(s, h) for s in range(depth) for h in range(HALVES) if s != z]
        at = {(s, h): ready(n, depth, z, s, range(h * Q, h * Q + Q)) for s, h in own + far}
        far = sorted(far, key=lambda u: (at[u], -abs(u[0] - z)))
        end = z in (0, depth - 1)
        subs = own + far if end else far + own
        total = n * max(z, depth - 1 - z)
        late = max(ready(n, depth, z, s, (h * Q,)) for s, h in subs[-LATE:])
        first = min(total, max(late, n + LEAD - 2))
        early.append((first,))
        taken, row = first if end else total, []
        for j, step in enumerate(steps):
            taken = max(taken, min(total, max(at[subs[i]] for i in step)) if j else taken)
            row.append(taken if len(step) > 1 else total)
        table.append([s * HALVES + h for s, h in subs])
        need.append(row)
    return table, need, early


def pick(values, at):
    out = jnp.int32(values[0])
    for i, v in enumerate(values[1:], 1):
        out = jnp.where(at == i, jnp.int32(v), out)
    return out


def kernel(R, C, fr, fc, pr, pc, acc, accv, gr_out, gc_out,
           rows, cols, chi, clo, tall, thi, tlo, ncol, rowp, sibp, sumb, inbox, csum, colacc, tacc, colr, cmid, lfeat, wlate, wlin,
           lsem, rrecv, srecv, crecv, xrecv, sends, bulk):
    me_r, me_c = lax.axis_index("row"), lax.axis_index("col")
    z, k = me_c // 2, me_c % 2
    Z = C // 2
    NR, F = fr.shape
    NC = fc.shape[0]
    Q = 1 + pr.shape[1] // F
    n = HALVES * Q
    hr = NR // HALVES
    UR = 2 * hr
    sibling = (me_r, me_c + 1 - 2 * k)
    place = (z, Z - 1 - z)
    step_to = (2, -2)
    table, need, early = plan(Q, Z)
    square = R == 4
    near = (me_r // 2 * 2 + 1 - me_r % 2, (1 - me_r // 2) * 2 + me_r % 2)
    across = R - 1 - me_r
    z_sent, sib_sent, col_sent, relay_sent, x_sent, row_sent, grad_sent, w_sent, feat_sent, pass_sent = (
        sends.at[i] for i in (0, 2, 3, 4, 5, 6, 7, 8, 9, 10))
    row_in, grad_in, w_in, feat_in, pass_in, relay_in = (bulk.at[i] for i in range(6))
    half_in = 6

    def at(start, size, mult):
        return pl.ds(pl.multiple_of(start, mult), size)

    def remote(src, dst, ss, rs, dev):
        return pltpu.make_async_remote_copy(src_ref=src, dst_ref=dst, send_sem=ss, recv_sem=rs, device_id=dev, device_id_type=MESH)

    def landed(ref, sem):
        pltpu.make_async_copy(ref, ref, sem).wait()

    def place_of(zs, h, core):
        return ((zs * HALVES + h) * 2 + core) * hr

    def rchunk(zs, core, i):
        return rows.at[i % Q, at(place_of(zs, i // Q, core), hr, 8), :]

    def own_chunk(i):
        q, h = i % Q, i // Q
        src = fr if q == 0 else pr
        return src.at[pl.ds(h * hr, hr), pl.ds(max(q - 1, 0) * F, F)]

    def own_cols(q):
        return fc if q == 0 else pc.at[:, pl.ds((q - 1) * F, F)]

    def zcopy(d, zs, i, src=None):
        dst = rchunk(zs, k, i)
        return remote(dst if src is None else src, dst, sends.at[d], rrecv.at[zs, i], (me_r, me_c + step_to[d]))

    def scopy(zs, i, src=None):
        dst = rchunk(zs, k, i)
        return remote(dst if src is None else src, dst, sib_sent, srecv.at[zs * HALVES + i // Q], sibling)

    for q in range(Q):
        for h in range(HALVES):
            pltpu.make_async_copy(own_chunk(h * Q + q), rchunk(z, k, h * Q + q), lsem.at[0]).start()
        pltpu.make_async_copy(own_cols(q), cols.at[q, at(me_r * NC, NC, 8), :], lsem.at[1]).start()
    acc_in = pltpu.make_async_copy(acc, accv, lsem.at[2])
    acc_in.start()

    barrier = pltpu.get_barrier_semaphore()
    if square:
        for axis in range(2):
            pl.semaphore_signal(barrier, inc=1, device_id=(near[axis], me_c), device_id_type=MESH)
    else:
        def greet(p, carry):
            pl.semaphore_signal(barrier, inc=1, device_id=((me_r + p) % R, me_c), device_id_type=MESH)
            return carry

        lax.fori_loop(1, R, greet, 0)
    pl.semaphore_signal(barrier, inc=1, device_id=sibling, device_id_type=MESH)
    for d in range(2):
        @pl.when(place[d] < Z - 1)
        def _():
            pl.semaphore_signal(barrier, inc=1, device_id=(me_r, me_c + step_to[d]), device_id_type=MESH)
    greeted = (2 if square else R - 1) + 1
    pl.semaphore_wait(barrier, greeted + (z > 0).astype(jnp.int32) + (z < Z - 1).astype(jnp.int32))

    def zown(d, lo, hi):
        for i in range(lo, hi):
            zcopy(d, z, i, own_chunk(i)).start()

    for d in range(2):
        @pl.when(place[d] < Z - 1)
        def _():
            zown(d, 0, LEAD)

    def own_push(axis, q):
        block = cols.at[q, at(me_r * NC, NC, 8), :]
        return remote(own_cols(q), block, col_sent, crecv.at[axis, q], (near[axis], me_c))

    def own_arrive(axis, q):
        block = cols.at[q, at(near[axis] * NC, NC, 8), :]
        return remote(block, block, col_sent, crecv.at[axis, q], (near[axis], me_c))

    def relay(axis, q):
        block = cols.at[q, at(near[axis] * NC + axis * (NC // 2), NC // 2, 8), :]
        return remote(block, block, relay_sent, relay_in, (near[1 - axis], me_c))

    def push_cols(p, carry):
        for q in range(Q):
            block = cols.at[q, at(me_r * NC, NC, 8), :]
            remote(own_cols(q), block, col_sent, relay_in, ((me_r + p) % R, me_c)).start()
        return carry

    if square:
        for q in range(Q):
            for axis in range(2):
                own_push(axis, q).start()
    else:
        lax.fori_loop(1, R, push_cols, 0)
    for d in range(2):
        @pl.when(place[d] == 0)
        def _():
            zown(d, LEAD, n)
    for i in range(n):
        scopy(z, i, own_chunk(i)).start()

    def slot(t, carry):
        for d in range(2):
            y = place[d]

            @pl.when(t < n * y)
            def _():
                ys, i = order(n, Z, y - 1, t)
                zs = ys if d == 0 else Z - 1 - ys
                zcopy(d, zs, i).wait_recv()

                @pl.when(y < Z - 1)
                def _():
                    zcopy(d, zs, i).start()

                scopy(zs, i).start()

                @pl.when(jnp.logical_and(t == n * y - 1, y < Z - 1))
                def _():
                    zown(d, LEAD, n)

        return carry

    def by_place(values, j):
        out = pick([row[j] for row in values], z) if isinstance(j, int) else None
        if out is None:
            out = pick(values[0], j)
            for place_z in range(1, Z):
                out = jnp.where(z == place_z, pick(values[place_z], j), out)
        return out

    passed = 0
    if square:
        for q in range(Q):
            until = min(RELAY_SLOTS * (q + 1), min(row[0] for row in early))
            lax.fori_loop(passed, until, slot, 0)
            passed = until
            for axis in range(2):
                own_arrive(axis, q).wait_recv()
                relay(axis, q).start()
    lax.fori_loop(passed, by_place(early, 0), slot, 0)

    landed(rows.at[:, pl.ds(0, NR), :], lsem.at[0])
    landed(cols.at[:, pl.ds(0, NC), :], lsem.at[1])
    acc_in.wait()
    landed(cols.at[:, pl.ds(0, NC if square else (R - 1) * NC), :], relay_in)

    late = [by_place(table, HALVES * Z - LATE + s) for s in range(LATE)]

    def push_late(p, carry):
        for s in range(LATE):
            src = rows.at[0, at(late[s] * UR + k * hr, hr, 8), :]
            remote(src, lfeat.at[me_r, s, k], feat_sent, feat_in, ((me_r + p) % R, me_c)).start()
        return carry

    lax.fori_loop(1, R, push_late, 0)

    for q in range(Q):
        turned = cols[q].T
        hi, lo = split(turned)
        if q == 0:
            tall[...] = turned
        else:
            thi[q - 1] = hi
            tlo[q - 1] = lo
    feats = cols[0]
    hi, lo = split(feats)
    chi[...] = hi
    clo[...] = lo
    ones = jnp.ones((8, F), jnp.bfloat16)
    ncol[...] = sum(lax.dot_general(
        ones, piece, (((1,), (1,)), ((), ())), preferred_element_type=jnp.float32) for piece in reversed(split3(feats * feats)))
    colacc[...] = jnp.zeros_like(colacc)
    tacc[...] = jnp.zeros_like(tacc)

    def exchange(sub):
        return remote(rowp.at[at(sub * UR + (1 - k) * hr, hr, 8), :], sibp.at[sub], x_sent, xrecv.at[sub], sibling)

    def weigh(subs):
        for sub in subs:
            landed(rows.at[:, pl.ds(0, hr), :], srecv.at[sub])
        blocks = [at(sub * UR, UR, 8) for sub in subs]
        parts = [at((2 * (sub // HALVES) + core) * NR + sub % HALVES * hr, hr, 8) for sub in subs for core in range(2)]
        f = jnp.concatenate([rows[0, b, :] for b in blocks], axis=0)
        cross = lax.dot_general(f, tall[...], (((1,), (0,)), ((), ())), precision=lax.Precision.HIGHEST, preferred_element_type=jnp.float32)
        g = jnp.concatenate([accv[b, :] for b in parts], axis=0)
        for q in range(1, Q):
            panel = jnp.concatenate([rows[q, b, :] for b in blocks], axis=0)
            g = g + dot3(split(panel), (thi[q - 1], tlo[q - 1]), 1, 0)
        for i, b in enumerate(parts):
            accv[b, :] = g[i * hr:(i + 1) * hr, :]
        dist = jnp.sum(f * f, axis=1, keepdims=True) + ncol[0:1, :] - 2.0 * cross
        return f, g * jnp.exp(-decay_rate * dist)

    def row_part(subs, f, w):
        s = jnp.sum(w, axis=1, keepdims=True)
        part = grad_scale * (dot3(split(w), (chi[...], clo[...]), 1, 0) - s * f)
        for i, sub in enumerate(subs):
            rowp[at(sub * UR, UR, 8), :] = part[i * UR:(i + 1) * UR, :]
        for sub in subs:
            exchange(sub).start()

    def inward(end):
        return 1 if end == 0 else Z - 2

    def finish(subs):
        for sub in subs:
            exchange(sub).wait_recv()
            zs, h = sub // HALVES, sub % HALVES
            total = rowp[at(sub * UR + k * hr, hr, 8), :] + sibp[sub]
            own = zs == z
            straight = jnp.logical_or(own, zs == Z - 1 - z)
            group = jnp.where(straight, 0, jnp.where(zs == 0, 1, jnp.where(zs == Z - 1, 2, 0)))
            to = jnp.where(group == 0, zs, jnp.where(group == 1, inward(0), inward(1)))
            dst = inbox.at[group * Z + z, at(h * hr, hr, 8), :]

            @pl.when(to == z)
            def _():
                dst[...] = total

            @pl.when(to != z)
            def _():
                sumb[sub] = total
                got = bulk.at[jnp.where(group > 0, half_in + h, 0)]
                remote(sumb.at[sub], dst, row_sent, got, (me_r, 2 * to + k)).start()

    def collect():
        for e, end in enumerate((0, Z - 1)):
            @pl.when(jnp.logical_and(z == inward(end), z != end))
            def _():
                for h in range(HALVES):
                    part = pl.ds(h * hr, hr)
                    if Z > 3:
                        landed(inbox.at[pl.ds(0, Z - 3), part, :], bulk.at[half_in + h])
                    terms = [inbox[(e + 1) * Z + zs, part, :] for zs in range(1, Z - 1)]
                    csum[e, part, :] = sum(terms[1:], terms[0])
                    remote(csum.at[e, part, :], inbox.at[z, part, :], row_sent, row_in, (me_r, 2 * end + k)).start()

    pairs = HALVES * Z // 2 - 1

    def pair_at(j):
        return [by_place(table, 2 * j + i) for i in range(2)]

    lax.fori_loop(by_place(early, 0), by_place(need, 0), slot, 0)

    def upto(a, b):
        lax.fori_loop(a, b, slot, 0)

    def col_part(f, w):
        colacc[...] += dot3(split(w.T), split(f), 1, 0)
        tacc[...] += jnp.broadcast_to(jnp.sum(w, axis=0, keepdims=True), tacc.shape)

    def step(j, carry):
        @pl.when(j > 0)
        def _():
            upto(by_place(need, j - 1), by_place(need, j))

        subs = pair_at(j)
        f, w = weigh(subs)
        row_part(subs, f, w)
        col_part(f, w)

        @pl.when(j > 0)
        def _():
            finish(pair_at(j - 1))

        return carry

    lax.fori_loop(0, pairs - 1, step, 0)
    if pairs > 1:
        upto(by_place(need, pairs - 2), by_place(need, pairs - 1))
        finish(pair_at(pairs - 2))
    final = pair_at(pairs - 1)
    stops = [by_place(need, pairs - 1)] + [by_place([[row[-1] - 2 + i] for row in need], 0) for i in range(3)]
    stops = [jnp.maximum(stops[0], stop) for stop in stops]
    f, w = weigh(final)
    row_part(final, f, w)
    col_part(f, w)
    tcol = jnp.broadcast_to(tacc[0:1, :], (128, tacc.shape[1])).T[:, 0:1]
    colacc[...] = grad_scale * (colacc[...] - tcol * cols[0])

    def push_grad(p, carry):
        to = (me_r + p) % R
        remote(colacc.at[at(to * NC, NC, 8), :], colr.at[me_r], grad_sent, grad_in, (to, me_c)).start()
        return carry

    def half_of(axis):
        return pl.ds(axis * (F // 2), F // 2)

    def grad_near(axis, half):
        block = colacc.at[at(near[axis] * NC, NC, 8), half_of(half)]
        return remote(block, colr.at[axis, :, half_of(half)], grad_sent, grad_in, (near[axis], me_c))

    def grad_across(axis):
        block = colacc.at[at(across * NC, NC, 8), half_of(axis)]
        return remote(block, cmid.at[axis], grad_sent, bulk.at[half_in + HALVES + axis], (near[axis], me_c))

    if square:
        for axis in range(2):
            grad_across(axis).start()
        for axis in range(2):
            grad_near(axis, axis).start()
    else:
        lax.fori_loop(1, R, push_grad, 0)
    upto(stops[0], stops[2])
    finish(final)
    upto(stops[2], stops[3])

    landed(lfeat.at[pl.ds(0, R - 1), :, 0], feat_in)

    def pass_on(p, carry):
        block = lfeat.at[(me_r + p) % R, :, k]
        remote(block, block, pass_sent, pass_in, sibling).start()
        return carry

    lax.fori_loop(1, R, pass_on, 0)

    for s in range(LATE):
        f, w = weigh([late[s]])
        wlate[:, s * UR:(s + 1) * UR] = w.T
        for core in range(2):
            lfeat[me_r, s, core] = f[core * hr:(core + 1) * hr, :]
        if s == LATE - 1:
            def push_w(p, carry):
                to = (me_r + p) % R
                remote(wlate.at[at(to * NC, NC, 8), :], wlin.at[me_r], w_sent, w_in, (to, me_c)).start()
                return carry

            lax.fori_loop(1, R, push_w, 0)
            wlin[me_r] = wlate[at(me_r * NC, NC, 8), :]
        row_part([late[s]], f, w)
        if s == 0 and square:
            for axis in range(2):
                other = 1 - axis
                grad_across(other).wait_recv()
                colacc[at(near[axis] * NC, NC, 8), half_of(other)] += cmid[other]
                grad_near(axis, other).start()
    finish([late[0]])

    landed(lfeat.at[pl.ds(0, R - 1), :, 0], pass_in)
    behind = split(lfeat[...].reshape(R * LATE * UR, F))
    finish([late[LATE - 1]])
    collect()
    mine = at(me_r * NC, NC, 8)
    landed(colr.at[pl.ds(0, 2 if square else R - 1)], grad_in)
    if square:
        gc_out[...] = colacc[mine, :] + (colr[0] + colr[1])
    else:
        gc_out[...] = colacc[mine, :]

        def add_grad(p, carry):
            gc_out[...] += colr[(me_r + p) % R]
            return carry

        lax.fori_loop(1, R, add_grad, 0)
    landed(wlin.at[pl.ds(0, R - 1)], w_in)
    w = jnp.concatenate([wlin[p] for p in range(R)], axis=1)
    gc_out[...] += grad_scale * (dot3(split(w), behind, 1, 0) - jnp.sum(w, axis=1, keepdims=True) * cols[0, mine, :])

    for end in (0, Z - 1):
        @pl.when(z == end)
        def _():
            landed(inbox.at[pl.ds(0, 2)], row_in)
            gr_out[...] = inbox[end] + (inbox[inward(end)] + inbox[Z - 1 - end])

    @pl.when(jnp.logical_and(z > 0, z < Z - 1))
    def _():
        landed(inbox.at[pl.ds(0, Z - 1)], row_in)
        total = inbox[0]
        for zs in range(1, Z):
            total = total + inbox[zs]
        gr_out[...] = total

    for d in range(2):
        for y in range(Z - 1):
            @pl.when(place[d] == y)
            def _():
                landed(rows.at[:, pl.ds(0, (y + 1) * NR), :], sends.at[d])
    landed(rows.at[:, pl.ds(0, Z * NR), :], sib_sent)
    landed(cols.at[:, pl.ds(0, (2 if square else R - 1) * NC), :], col_sent)
    if square:
        landed(cols.at[:, pl.ds(0, NC), :], relay_sent)
    landed(sibp, x_sent)
    landed(inbox.at[pl.ds(0, Z - 1)], row_sent)
    landed(colr.at[pl.ds(0, R - 1)], grad_sent)
    landed(wlin.at[pl.ds(0, R - 1)], w_sent)
    landed(lfeat.at[pl.ds(0, R - 1), :, 0], feat_sent)
    landed(lfeat.at[pl.ds(0, R - 1), :, 0], pass_sent)


def put(a, b, c, x, y, w, sem):
    copies = [pltpu.make_async_copy(u, v, sem.at[i]) for i, (u, v) in enumerate(((a, x), (b, y), (c, w)))]
    for copy in copies:
        copy.start()
    for copy in copies:
        copy.wait()


def solution(mesh):
    R, C = mesh.shape["row"], mesh.shape["col"]
    in_specs = (
        P(("row", "col"), None),
        P(("col", "row"), None),
        P(("row", "col"), None),
        P(("col", "row"), None),
        P("row", "col"),
    )
    out_specs = (P("row", "col"), P(("row", "col"), None), P(("col", "row"), None))

    def local(fr, fc, pr, pc, acc):
        NR, F = fr.shape
        NC = fc.shape[0]
        Q = 1 + pr.shape[1] // F
        Z, n = C // 2, HALVES * Q
        hr, subs = NR // HALVES, HALVES * (C // 2)
        f32, bf16 = jnp.float32, jnp.bfloat16
        V, D = pltpu.VMEM, pltpu.SemaphoreType.DMA
        hbm = pl.BlockSpec(memory_space=pl.ANY)
        vmem = pl.BlockSpec(memory_space=pltpu.VMEM)
        shapes = (acc.shape, fr.shape, fc.shape)
        made = pl.pallas_call(
            functools.partial(kernel, R, C),
            out_shape=tuple(pltpu.VMEM(s, f32) for s in shapes),
            in_specs=[hbm] * 5,
            out_specs=(vmem,) * 3,
            scratch_shapes=[
                V((Q, C * NR, F), f32), V((Q, R * NC, F), f32),
                V((R * NC, F), bf16), V((R * NC, F), bf16), V((F, R * NC), f32),
                V((Q - 1, F, R * NC), bf16), V((Q - 1, F, R * NC), bf16),
                V((8, R * NC), f32),
                V((C * NR, F), f32), V((subs, hr, F), f32), V((subs, hr, F), f32), V((3 * Z, NR, F), f32), V((2, NR, F), f32),
                V((R * NC, F), f32), V((8, R * NC), f32), V((R, NC, F), f32), V((2, NC, F // 2), f32),
                V((R, LATE, 2, hr, F), f32), V((R * NC, LATE * 2 * hr), f32), V((R, NC, LATE * 2 * hr), f32),
                D((3,)), D((Z, n)), D((subs,)), D((2, Q)), D((subs,)), D((11,)), D((10,)),
            ],
            compiler_params=pltpu.CompilerParams(
                collective_id=0, has_side_effects=True, vmem_limit_bytes=56 * 1024 * 1024),
        )(fr, fc, pr, pc, acc)
        made = [pltpu.with_memory_space_constraint(m, pltpu.VMEM) for m in made]
        done = pl.pallas_call(
            put,
            out_shape=tuple(jax.ShapeDtypeStruct(s, f32) for s in shapes),
            in_specs=[vmem] * 3,
            out_specs=(hbm,) * 3,
            scratch_shapes=[D((3,))],
        )(*made)
        return tuple(done)

    return jax.shard_map(local, mesh=mesh, in_specs=in_specs, out_specs=out_specs, check_vma=False)
```

```python
import functools

import jax
import jax.numpy as jnp
from jax import lax
from jax.experimental import pallas as pl
from jax.experimental.pallas import tpu as pltpu
from jax.sharding import PartitionSpec as P

decay_rate = 0.125
grad_scale = 0.25
MESH = pl.DeviceIdType.MESH
HALVES = 2
LEAD = 4
RELAY_SLOTS = 2
LATE = 2
PIECES = 4


def split(x):
    hi = x.astype(jnp.bfloat16)
    return hi, (x - hi.astype(jnp.float32)).astype(jnp.bfloat16)


def dot3(a, b, ca, cb):
    dims = (((ca,), (cb,)), ((), ()))
    f = functools.partial(lax.dot_general, dimension_numbers=dims, preferred_element_type=jnp.float32)
    return f(a[0], b[0]) + (f(a[0], b[1]) + f(a[1], b[0]))


def split3(x):
    hi = x.astype(jnp.bfloat16)
    rest = x - hi.astype(jnp.float32)
    mid = rest.astype(jnp.bfloat16)
    return hi, mid, (rest - mid.astype(jnp.float32)).astype(jnp.bfloat16)


def order(n, depth, y, t):
    src, chunk = y * 0, t * 0
    found = y < 0
    for _ in range(depth):
        lead = t < LEAD
        done = jnp.logical_or(lead, t >= LEAD + n * y)
        take = jnp.logical_and(done, jnp.logical_not(found))
        src = jnp.where(take, y, src)
        chunk = jnp.where(take, jnp.where(lead, t, t - n * y), chunk)
        found = jnp.logical_or(found, done)
        y, t = y - 1, t - LEAD
    return src, chunk


def ready(n, depth, z, s, chunks):
    def seq(y):
        own = [(y, i) for i in range(n)]
        return own if y == 0 else own[:LEAD] + seq(y - 1) + own[LEAD:]

    if s == z:
        return 0
    y, ys = (z, s) if s < z else (depth - 1 - z, depth - 1 - s)
    return 1 + max(t for t, (a, i) in enumerate(seq(y - 1)) if a == ys and i in chunks)


def plan(Q, depth):
    n = HALVES * Q
    table, need, early = [], [], []
    steps = [(2 * j, 2 * j + 1) for j in range(HALVES * depth // 2 - 1)]
    steps += [(HALVES * depth - 2,), (HALVES * depth - 1,)]
    for z in range(depth):
        own = [(z, h) for h in range(HALVES)]
        far = [(s, h) for s in range(depth) for h in range(HALVES) if s != z]
        at = {(s, h): ready(n, depth, z, s, range(h * Q, h * Q + Q)) for s, h in own + far}
        end = z in (0, depth - 1)
        far = sorted(far, key=lambda u: (at[u], -abs(u[0] - z)) if end else (u[0] not in (0, depth - 1),))
        subs = own + far if end else far + own
        total = n * max(z, depth - 1 - z)
        late = max(ready(n, depth, z, s, (h * Q,)) for s, h in subs[-LATE:])
        first = min(total, max(late, n + LEAD - 2))
        early.append((first,))
        taken, row = first if end else total, []
        for j, step in enumerate(steps):
            taken = max(taken, min(total, max(at[subs[i]] for i in step)) if j else taken)
            row.append(taken if len(step) > 1 else total)
        table.append([s * HALVES + h for s, h in subs])
        need.append(row)
    return table, need, early


def pick(values, at):
    out = jnp.int32(values[0])
    for i, v in enumerate(values[1:], 1):
        out = jnp.where(at == i, jnp.int32(v), out)
    return out


def kernel(R, C, fr, fc, pr, pc, acc, accv, gr_out, gc_out,
           rows, cols, chi, clo, tall, thi, tlo, ncol, rowp, sibp, sumb, inbox, csum, colacc, colr, cmid, lfeat, wlate, wlin,
           lsem, rrecv, srecv, crecv, xrecv, sends, bulk):
    me_r, me_c = lax.axis_index("row"), lax.axis_index("col")
    z, k = me_c // 2, me_c % 2
    Z = C // 2
    NR, F = fr.shape
    NC = fc.shape[0]
    Q = 1 + pr.shape[1] // F
    n = HALVES * Q
    hr = NR // HALVES
    UR = 2 * hr
    sibling = (me_r, me_c + 1 - 2 * k)
    place = (z, Z - 1 - z)
    step_to = (2, -2)
    table, need, early = plan(Q, Z)
    square = R == 4
    near = (me_r // 2 * 2 + 1 - me_r % 2, (1 - me_r // 2) * 2 + me_r % 2)
    across = R - 1 - me_r
    sent = sends.at[2]
    row_in, grad_in, w_in, feat_in, pass_in, relay_in = (bulk.at[i] for i in range(6))
    half_in = 6

    def at(start, size, mult):
        return pl.ds(pl.multiple_of(start, mult), size)

    def remote(src, dst, ss, rs, dev):
        return pltpu.make_async_remote_copy(src_ref=src, dst_ref=dst, send_sem=ss, recv_sem=rs, device_id=dev, device_id_type=MESH)

    def landed(ref, sem):
        pltpu.make_async_copy(ref, ref, sem).wait()

    def place_of(zs, h, core):
        return ((zs * HALVES + h) * 2 + core) * hr

    def rchunk(zs, core, i):
        return rows.at[i % Q, at(place_of(zs, i // Q, core), hr, 8), :]

    def own_chunk(i):
        q, h = i % Q, i // Q
        src = fr if q == 0 else pr
        return src.at[pl.ds(h * hr, hr), pl.ds(max(q - 1, 0) * F, F)]

    def own_cols(q):
        return fc if q == 0 else pc.at[:, pl.ds((q - 1) * F, F)]

    def zcopy(d, zs, i, src=None):
        dst = rchunk(zs, k, i)
        return remote(dst if src is None else src, dst, sends.at[d], rrecv.at[zs, i], (me_r, me_c + step_to[d]))

    def scopy(zs, i, src=None):
        dst = rchunk(zs, k, i)
        return remote(dst if src is None else src, dst, sent, srecv.at[zs * HALVES + i // Q], sibling)

    barrier = pltpu.get_barrier_semaphore()
    if square:
        for axis in range(2):
            pl.semaphore_signal(barrier, inc=1, device_id=(near[axis], me_c), device_id_type=MESH)
    else:
        def greet(p, carry):
            pl.semaphore_signal(barrier, inc=1, device_id=((me_r + p) % R, me_c), device_id_type=MESH)
            return carry

        lax.fori_loop(1, R, greet, 0)
    pl.semaphore_signal(barrier, inc=1, device_id=sibling, device_id_type=MESH)
    for d in range(2):
        @pl.when(place[d] < Z - 1)
        def _():
            pl.semaphore_signal(barrier, inc=1, device_id=(me_r, me_c + step_to[d]), device_id_type=MESH)
    for q in range(Q):
        for h in range(HALVES):
            pltpu.make_async_copy(own_chunk(h * Q + q), rchunk(z, k, h * Q + q), lsem.at[0]).start()
        pltpu.make_async_copy(own_cols(q), cols.at[q, at(me_r * NC, NC, 8), :], lsem.at[1]).start()
    acc_in = pltpu.make_async_copy(acc, accv, lsem.at[2])
    acc_in.start()

    greeted = (2 if square else R - 1) + 1
    pl.semaphore_wait(barrier, greeted + (z > 0).astype(jnp.int32) + (z < Z - 1).astype(jnp.int32))

    def zown(d, lo, hi):
        for i in range(lo, hi):
            zcopy(d, z, i, own_chunk(i)).start()

    for d in range(2):
        @pl.when(place[d] < Z - 1)
        def _():
            zown(d, 0, LEAD)

    def own_push(axis, q):
        block = cols.at[q, at(me_r * NC, NC, 8), :]
        return remote(own_cols(q), block, sent, crecv.at[axis, q], (near[axis], me_c))

    def own_arrive(axis, q):
        block = cols.at[q, at(near[axis] * NC, NC, 8), :]
        return remote(block, block, sent, crecv.at[axis, q], (near[axis], me_c))

    def relay(axis, q):
        block = cols.at[q, at(near[axis] * NC + axis * (NC // 2), NC // 2, 8), :]
        return remote(block, block, sent, relay_in, (near[1 - axis], me_c))

    def push_cols(p, carry):
        for q in range(Q):
            block = cols.at[q, at(me_r * NC, NC, 8), :]
            remote(own_cols(q), block, sent, relay_in, ((me_r + p) % R, me_c)).start()
        return carry

    if square:
        for q in range(Q):
            for axis in range(2):
                own_push(axis, q).start()
    else:
        lax.fori_loop(1, R, push_cols, 0)
    for d in range(2):
        @pl.when(place[d] == 0)
        def _():
            zown(d, LEAD, n)
    for i in range(n):
        scopy(z, i, own_chunk(i)).start()

    def slot(t, carry):
        for d in range(2):
            y = place[d]

            @pl.when(t < n * y)
            def _():
                ys, i = order(n, Z, y - 1, t)
                zs = ys if d == 0 else Z - 1 - ys
                zcopy(d, zs, i).wait_recv()

                @pl.when(y < Z - 1)
                def _():
                    zcopy(d, zs, i).start()

                scopy(zs, i).start()

                @pl.when(jnp.logical_and(t == n * y - 1, y < Z - 1))
                def _():
                    zown(d, LEAD, n)

        return carry

    def by_place(values, j):
        out = pick([row[j] for row in values], z) if isinstance(j, int) else None
        if out is None:
            out = pick(values[0], j)
            for place_z in range(1, Z):
                out = jnp.where(z == place_z, pick(values[place_z], j), out)
        return out

    passed = 0
    if square:
        for q in range(Q):
            until = min(RELAY_SLOTS * (q + 1), min(row[0] for row in early))
            lax.fori_loop(passed, until, slot, 0)
            passed = until
            for axis in range(2):
                own_arrive(axis, q).wait_recv()
                relay(axis, q).start()
    lax.fori_loop(passed, by_place(early, 0), slot, 0)

    landed(rows.at[:, pl.ds(0, NR), :], lsem.at[0])
    landed(cols.at[:, pl.ds(0, NC), :], lsem.at[1])
    acc_in.wait()
    landed(cols.at[:, pl.ds(0, NC if square else (R - 1) * NC), :], relay_in)

    late = [by_place(table, HALVES * Z - LATE + s) for s in range(LATE)]

    def push_late(p, carry):
        for s in range(LATE):
            src = rows.at[0, at(late[s] * UR + k * hr, hr, 8), :]
            remote(src, lfeat.at[me_r, s, k], sent, feat_in, ((me_r + p) % R, me_c)).start()
        return carry

    lax.fori_loop(1, R, push_late, 0)

    for q in range(Q):
        turned = cols[q].T
        hi, lo = split(turned)
        if q == 0:
            tall[...] = turned
        else:
            thi[q - 1] = hi
            tlo[q - 1] = lo
    feats = cols[0]
    hi, lo = split(feats)
    chi[...] = hi
    clo[...] = lo
    ones = jnp.ones((8, F), jnp.bfloat16)
    ncol[...] = sum(lax.dot_general(
        ones, piece, (((1,), (1,)), ((), ())), preferred_element_type=jnp.float32) for piece in reversed(split3(feats * feats)))
    colacc[...] = jnp.zeros_like(colacc)

    def exchange(sub):
        return remote(rowp.at[at(sub * UR + (1 - k) * hr, hr, 8), :], sibp.at[sub], sent, xrecv.at[sub], sibling)

    def weigh(subs):
        for sub in subs:
            landed(rows.at[:, pl.ds(0, hr), :], srecv.at[sub])
        blocks = [at(sub * UR, UR, 8) for sub in subs]
        parts = [at((2 * (sub // HALVES) + core) * NR + sub % HALVES * hr, hr, 8) for sub in subs for core in range(2)]
        f = jnp.concatenate([rows[0, b, :] for b in blocks], axis=0)
        cross = lax.dot_general(f, tall[...], (((1,), (0,)), ((), ())), precision=lax.Precision.HIGHEST, preferred_element_type=jnp.float32)
        g = jnp.concatenate([accv[b, :] for b in parts], axis=0)
        for q in range(1, Q):
            panel = jnp.concatenate([rows[q, b, :] for b in blocks], axis=0)
            g = g + dot3(split(panel), (thi[q - 1], tlo[q - 1]), 1, 0)
        for i, b in enumerate(parts):
            accv[b, :] = g[i * hr:(i + 1) * hr, :]
        dist = jnp.sum(f * f, axis=1, keepdims=True) + ncol[0:1, :] - 2.0 * cross
        return f, g * jnp.exp(-decay_rate * dist)

    def row_part(subs, f, w):
        s = jnp.sum(w, axis=1, keepdims=True)
        part = grad_scale * (dot3(split(w), (chi[...], clo[...]), 1, 0) - s * f)
        for i, sub in enumerate(subs):
            rowp[at(sub * UR, UR, 8), :] = part[i * UR:(i + 1) * UR, :]
        for sub in subs:
            exchange(sub).start()

    def inward(end):
        return 1 if end == 0 else Z - 2

    def finish(subs):
        for sub in subs:
            exchange(sub).wait_recv()
            zs, h = sub // HALVES, sub % HALVES
            total = rowp[at(sub * UR + k * hr, hr, 8), :] + sibp[sub]
            own = zs == z
            straight = jnp.logical_or(own, zs == Z - 1 - z)
            group = jnp.where(straight, 0, jnp.where(zs == 0, 1, jnp.where(zs == Z - 1, 2, 0)))
            to = jnp.where(group == 0, zs, jnp.where(group == 1, inward(0), inward(1)))
            dst = inbox.at[group * Z + z, at(h * hr, hr, 8), :]

            @pl.when(to == z)
            def _():
                dst[...] = total

            @pl.when(to != z)
            def _():
                sumb[sub] = total
                got = bulk.at[jnp.where(group > 0, half_in + h, 0)]
                remote(sumb.at[sub], dst, sent, got, (me_r, 2 * to + k)).start()

    def collect():
        for e, end in enumerate((0, Z - 1)):
            @pl.when(jnp.logical_and(z == inward(end), z != end))
            def _():
                for h in range(HALVES):
                    part = pl.ds(h * hr, hr)
                    if Z > 3:
                        landed(inbox.at[pl.ds(0, Z - 3), part, :], bulk.at[half_in + h])
                    terms = [inbox[(e + 1) * Z + zs, part, :] for zs in range(1, Z - 1)]
                    csum[e, part, :] = sum(terms[1:], terms[0])
                    remote(csum.at[e, part, :], inbox.at[z, part, :], sent, row_in, (me_r, 2 * end + k)).start()

    pairs = HALVES * Z // 2 - 1

    def pair_at(j):
        return [by_place(table, 2 * j + i) for i in range(2)]

    lax.fori_loop(by_place(early, 0), by_place(need, 0), slot, 0)

    def upto(a, b):
        lax.fori_loop(a, b, slot, 0)

    def col_part(f, w):
        turned = w.T
        part = dot3(split(turned), split(f), 1, 0)
        colacc[...] += grad_scale * (part - jnp.sum(turned, axis=1, keepdims=True) * cols[0])

    def step(j, carry):
        @pl.when(j > 0)
        def _():
            upto(by_place(need, j - 1), by_place(need, j))

        subs = pair_at(j)
        f, w = weigh(subs)
        row_part(subs, f, w)
        col_part(f, w)

        @pl.when(j > 0)
        def _():
            finish(pair_at(j - 1))

        return carry

    lax.fori_loop(0, pairs - 1, step, 0)
    if pairs > 1:
        upto(by_place(need, pairs - 2), by_place(need, pairs - 1))
        finish(pair_at(pairs - 2))
    final = pair_at(pairs - 1)
    stops = [by_place(need, pairs - 1)] + [by_place([[row[-1] - 2 + i] for row in need], 0) for i in range(3)]
    stops = [jnp.maximum(stops[0], stop) for stop in stops]
    f, w = weigh(final)
    row_part(final, f, w)
    col_part(f, w)

    def push_grad(p, carry):
        to = (me_r + p) % R
        remote(colacc.at[at(to * NC, NC, 8), :], colr.at[me_r], sent, grad_in, (to, me_c)).start()
        return carry

    def half_of(axis):
        return pl.ds(axis * (F // 2), F // 2)

    def grad_near(axis, half):
        block = colacc.at[at(near[axis] * NC, NC, 8), half_of(half)]
        return remote(block, colr.at[axis, :, half_of(half)], sent, grad_in, (near[axis], me_c))

    def grad_across(axis):
        block = colacc.at[at(across * NC, NC, 8), half_of(axis)]
        return remote(block, cmid.at[axis], sent, bulk.at[half_in + HALVES + axis], (near[axis], me_c))

    if square:
        for axis in range(2):
            grad_across(axis).start()
    else:
        lax.fori_loop(1, R, push_grad, 0)
    upto(stops[0], stops[2])
    finish(final)
    if square:
        for axis in range(2):
            grad_near(axis, axis).start()
    upto(stops[2], stops[3])

    landed(lfeat.at[pl.ds(0, R - 1), :, 0], feat_in)

    def pass_on(p, carry):
        block = lfeat.at[(me_r + p) % R, :, k]
        remote(block, block, sent, pass_in, sibling).start()
        return carry

    lax.fori_loop(1, R, pass_on, 0)

    for s in range(LATE):
        f, w = weigh([late[s]])
        wlate[:, s * UR:(s + 1) * UR] = w.T
        for core in range(2):
            lfeat[me_r, s, core] = f[core * hr:(core + 1) * hr, :]
        if s == LATE - 1:
            def push_w(p, carry):
                to = (me_r + p) % R
                remote(wlate.at[at(to * NC, NC, 8), :], wlin.at[me_r], sent, w_in, (to, me_c)).start()
                return carry

            lax.fori_loop(1, R, push_w, 0)
            wlin[me_r] = wlate[at(me_r * NC, NC, 8), :]
        row_part([late[s]], f, w)
        if s == 0:
            collect()
        if s == 0 and square:
            for axis in range(2):
                other = 1 - axis
                grad_across(other).wait_recv()
                colacc[at(near[axis] * NC, NC, 8), half_of(other)] += cmid[other]
                grad_near(axis, other).start()
        if s == 0:
            finish([late[0]])
    landed(lfeat.at[pl.ds(0, R - 1), :, 0], pass_in)
    behind = split(lfeat[...].reshape(R * LATE * UR, F))
    finish([late[LATE - 1]])
    mine = at(me_r * NC, NC, 8)
    landed(colr.at[pl.ds(0, 2 if square else R - 1)], grad_in)
    if square:
        gc_out[...] = colacc[mine, :] + (colr[0] + colr[1])
    else:
        gc_out[...] = colacc[mine, :]

        def add_grad(p, carry):
            gc_out[...] += colr[(me_r + p) % R]
            return carry

        lax.fori_loop(1, R, add_grad, 0)
    landed(wlin.at[pl.ds(0, R - 1)], w_in)
    w = jnp.concatenate([wlin[p] for p in range(R)], axis=1)
    gc_out[...] += grad_scale * (dot3(split(w), behind, 1, 0) - jnp.sum(w, axis=1, keepdims=True) * cols[0, mine, :])

    for end in (0, Z - 1):
        @pl.when(z == end)
        def _():
            landed(inbox.at[pl.ds(0, 2)], row_in)
            gr_out[...] = inbox[end] + (inbox[inward(end)] + inbox[Z - 1 - end])

    @pl.when(jnp.logical_and(z > 0, z < Z - 1))
    def _():
        landed(inbox.at[pl.ds(0, Z - 1)], row_in)
        total = inbox[0]
        for zs in range(1, Z):
            total = total + inbox[zs]
        gr_out[...] = total

    for d in range(2):
        for y in range(Z - 1):
            @pl.when(place[d] == y)
            def _():
                landed(rows.at[:, pl.ds(0, (y + 1) * NR), :], sends.at[d])
    landed(rows.at[:, pl.ds(0, Z * NR), :], sent)
    landed(cols.at[:, pl.ds(0, (2 if square else R - 1) * NC), :], sent)
    if square:
        landed(cols.at[:, pl.ds(0, NC), :], sent)
    landed(sibp, sent)
    landed(inbox.at[pl.ds(0, Z - 1)], sent)
    landed(colr.at[pl.ds(0, R - 1)], sent)
    landed(wlin.at[pl.ds(0, R - 1)], sent)
    landed(lfeat.at[pl.ds(0, R - 1), :, 0], sent)
    landed(lfeat.at[pl.ds(0, R - 1), :, 0], sent)


def put(a, b, c, x, y, w, sem):
    size = a.shape[0] // PIECES
    parts = [(a.at[pl.ds(i * size, size), :], x.at[pl.ds(i * size, size), :]) for i in range(PIECES)]
    copies = [pltpu.make_async_copy(u, v, sem.at[i]) for i, (u, v) in enumerate(parts + [(b, y), (c, w)])]
    for copy in copies:
        copy.start()
    for copy in copies:
        copy.wait()


def solution(mesh):
    R, C = mesh.shape["row"], mesh.shape["col"]
    in_specs = (
        P(("row", "col"), None),
        P(("col", "row"), None),
        P(("row", "col"), None),
        P(("col", "row"), None),
        P("row", "col"),
    )
    out_specs = (P("row", "col"), P(("row", "col"), None), P(("col", "row"), None))

    def local(fr, fc, pr, pc, acc):
        NR, F = fr.shape
        NC = fc.shape[0]
        Q = 1 + pr.shape[1] // F
        Z, n = C // 2, HALVES * Q
        hr, subs = NR // HALVES, HALVES * (C // 2)
        f32, bf16 = jnp.float32, jnp.bfloat16
        V, D = pltpu.VMEM, pltpu.SemaphoreType.DMA
        hbm = pl.BlockSpec(memory_space=pl.ANY)
        vmem = pl.BlockSpec(memory_space=pltpu.VMEM)
        shapes = (acc.shape, fr.shape, fc.shape)
        made = pl.pallas_call(
            functools.partial(kernel, R, C),
            out_shape=tuple(pltpu.VMEM(s, f32) for s in shapes),
            in_specs=[hbm] * 5,
            out_specs=(vmem,) * 3,
            scratch_shapes=[
                V((Q, C * NR, F), f32), V((Q, R * NC, F), f32),
                V((R * NC, F), bf16), V((R * NC, F), bf16), V((F, R * NC), f32),
                V((Q - 1, F, R * NC), bf16), V((Q - 1, F, R * NC), bf16),
                V((8, R * NC), f32),
                V((C * NR, F), f32), V((subs, hr, F), f32), V((subs, hr, F), f32), V((3 * Z, NR, F), f32), V((2, NR, F), f32),
                V((R * NC, F), f32), V((R, NC, F), f32), V((2, NC, F // 2), f32),
                V((R, LATE, 2, hr, F), f32), V((R * NC, LATE * 2 * hr), f32), V((R, NC, LATE * 2 * hr), f32),
                D((3,)), D((Z, n)), D((subs,)), D((2, Q)), D((subs,)), D((3,)), D((10,)),
            ],
            compiler_params=pltpu.CompilerParams(
                collective_id=0, has_side_effects=True, vmem_limit_bytes=56 * 1024 * 1024),
        )(fr, fc, pr, pc, acc)
        made = [pltpu.with_memory_space_constraint(m, pltpu.VMEM) for m in made]
        done = pl.pallas_call(
            put,
            out_shape=tuple(jax.ShapeDtypeStruct(s, f32) for s in shapes),
            in_specs=[vmem] * 3,
            out_specs=(hbm,) * 3,
            scratch_shapes=[D((PIECES + 2,))],
        )(*made)
        return tuple(done)

    return jax.shard_map(local, mesh=mesh, in_specs=in_specs, out_specs=out_specs, check_vma=False)
```

```python
import functools

import jax
import jax.numpy as jnp
from jax import lax
from jax.experimental import pallas as pl
from jax.experimental.pallas import tpu as pltpu
from jax.sharding import PartitionSpec as P

decay_rate = 0.125
grad_scale = 0.25
MESH = pl.DeviceIdType.MESH
HALVES = 2
LEAD = 4
RELAY_SLOTS = 2
LATE = 2
PIECES = 4


def split(x):
    hi = x.astype(jnp.bfloat16)
    return hi, (x - hi.astype(jnp.float32)).astype(jnp.bfloat16)


def dot3(a, b, ca, cb):
    dims = (((ca,), (cb,)), ((), ()))
    f = functools.partial(lax.dot_general, dimension_numbers=dims, preferred_element_type=jnp.float32)
    return f(a[0], b[0]) + (f(a[0], b[1]) + f(a[1], b[0]))


def split3(x):
    hi = x.astype(jnp.bfloat16)
    rest = x - hi.astype(jnp.float32)
    mid = rest.astype(jnp.bfloat16)
    return hi, mid, (rest - mid.astype(jnp.float32)).astype(jnp.bfloat16)


def order(n, depth, y, t):
    src, chunk = y * 0, t * 0
    found = y < 0
    for _ in range(depth):
        lead = t < LEAD
        done = jnp.logical_or(lead, t >= LEAD + n * y)
        take = jnp.logical_and(done, jnp.logical_not(found))
        src = jnp.where(take, y, src)
        chunk = jnp.where(take, jnp.where(lead, t, t - n * y), chunk)
        found = jnp.logical_or(found, done)
        y, t = y - 1, t - LEAD
    return src, chunk


def ready(n, depth, z, s, chunks):
    def seq(y):
        own = [(y, i) for i in range(n)]
        return own if y == 0 else own[:LEAD] + seq(y - 1) + own[LEAD:]

    if s == z:
        return 0
    y, ys = (z, s) if s < z else (depth - 1 - z, depth - 1 - s)
    return 1 + max(t for t, (a, i) in enumerate(seq(y - 1)) if a == ys and i in chunks)


def plan(Q, depth):
    n = HALVES * Q
    table, need, early = [], [], []
    steps = [(2 * j, 2 * j + 1) for j in range(HALVES * depth // 2 - 1)]
    steps += [(HALVES * depth - 2,), (HALVES * depth - 1,)]
    for z in range(depth):
        own = [(z, h) for h in range(HALVES)]
        far = [(s, h) for s in range(depth) for h in range(HALVES) if s != z]
        at = {(s, h): ready(n, depth, z, s, range(h * Q, h * Q + Q)) for s, h in own + far}
        end = z in (0, depth - 1)
        far = sorted(far, key=lambda u: (at[u], -abs(u[0] - z)) if end else (u[0] not in (0, depth - 1),))
        subs = own + far if end else far + own
        total = n * max(z, depth - 1 - z)
        late = max(ready(n, depth, z, s, (h * Q,)) for s, h in subs[-LATE:])
        first = min(total, max(late, n + LEAD - 2))
        early.append((first,))
        taken, row = first if end else total, []
        for j, step in enumerate(steps):
            taken = max(taken, min(total, max(at[subs[i]] for i in step)) if j else taken)
            row.append(taken if len(step) > 1 else total)
        table.append([s * HALVES + h for s, h in subs])
        need.append(row)
    return table, need, early


def pick(values, at):
    out = jnp.int32(values[0])
    for i, v in enumerate(values[1:], 1):
        out = jnp.where(at == i, jnp.int32(v), out)
    return out


def kernel(R, C, fr, fc, pr, pc, acc, accv, gr_out, gc_out,
           rows, cols, chi, clo, tall, thi, tlo, ncol, rowp, sibp, sumb, inbox, csum, colacc, colr, cmid, lfeat, wlate, wlin,
           lsem, rrecv, srecv, crecv, xrecv, sends, bulk):
    me_r, me_c = lax.axis_index("row"), lax.axis_index("col")
    z, k = me_c // 2, me_c % 2
    Z = C // 2
    NR, F = fr.shape
    NC = fc.shape[0]
    Q = 1 + pr.shape[1] // F
    n = HALVES * Q
    hr = NR // HALVES
    UR = 2 * hr
    sibling = (me_r, me_c + 1 - 2 * k)
    place = (z, Z - 1 - z)
    step_to = (2, -2)
    table, need, early = plan(Q, Z)
    square = R == 4
    near = (me_r // 2 * 2 + 1 - me_r % 2, (1 - me_r // 2) * 2 + me_r % 2)
    across = R - 1 - me_r
    sent = sends.at[2]
    row_in, grad_in, w_in, feat_in, pass_in, relay_in = (bulk.at[i] for i in range(6))
    half_in = 6

    def at(start, size, mult):
        return pl.ds(pl.multiple_of(start, mult), size)

    def remote(src, dst, ss, rs, dev):
        return pltpu.make_async_remote_copy(src_ref=src, dst_ref=dst, send_sem=ss, recv_sem=rs, device_id=dev, device_id_type=MESH)

    def landed(ref, sem):
        pltpu.make_async_copy(ref, ref, sem).wait()

    def place_of(zs, h, core):
        return ((zs * HALVES + h) * 2 + core) * hr

    def rchunk(zs, core, i):
        return rows.at[i % Q, at(place_of(zs, i // Q, core), hr, 8), :]

    def own_chunk(i):
        q, h = i % Q, i // Q
        src = fr if q == 0 else pr
        return src.at[pl.ds(h * hr, hr), pl.ds(max(q - 1, 0) * F, F)]

    def own_cols(q):
        return fc if q == 0 else pc.at[:, pl.ds((q - 1) * F, F)]

    def zcopy(d, zs, i, src=None):
        dst = rchunk(zs, k, i)
        return remote(dst if src is None else src, dst, sends.at[d], rrecv.at[zs, i], (me_r, me_c + step_to[d]))

    def scopy(zs, i, src=None):
        dst = rchunk(zs, k, i)
        return remote(dst if src is None else src, dst, sent, srecv.at[zs * HALVES + i // Q], sibling)

    barrier = pltpu.get_barrier_semaphore()
    if square:
        for axis in range(2):
            pl.semaphore_signal(barrier, inc=1, device_id=(near[axis], me_c), device_id_type=MESH)
    else:
        def greet(p, carry):
            pl.semaphore_signal(barrier, inc=1, device_id=((me_r + p) % R, me_c), device_id_type=MESH)
            return carry

        lax.fori_loop(1, R, greet, 0)
    pl.semaphore_signal(barrier, inc=1, device_id=sibling, device_id_type=MESH)
    for d in range(2):
        @pl.when(place[d] < Z - 1)
        def _():
            pl.semaphore_signal(barrier, inc=1, device_id=(me_r, me_c + step_to[d]), device_id_type=MESH)
    for q in range(Q):
        for h in range(HALVES):
            pltpu.make_async_copy(own_chunk(h * Q + q), rchunk(z, k, h * Q + q), lsem.at[0]).start()
        pltpu.make_async_copy(own_cols(q), cols.at[q, at(me_r * NC, NC, 8), :], lsem.at[1]).start()
    acc_in = pltpu.make_async_copy(acc, accv, lsem.at[2])
    acc_in.start()

    greeted = (2 if square else R - 1) + 1
    pl.semaphore_wait(barrier, greeted + (z > 0).astype(jnp.int32) + (z < Z - 1).astype(jnp.int32))

    def zown(d, lo, hi):
        for i in range(lo, hi):
            zcopy(d, z, i, own_chunk(i)).start()

    for d in range(2):
        @pl.when(place[d] < Z - 1)
        def _():
            zown(d, 0, LEAD)

    def own_push(axis, q):
        block = cols.at[q, at(me_r * NC, NC, 8), :]
        return remote(own_cols(q), block, sent, crecv.at[axis, q], (near[axis], me_c))

    def own_arrive(axis, q):
        block = cols.at[q, at(near[axis] * NC, NC, 8), :]
        return remote(block, block, sent, crecv.at[axis, q], (near[axis], me_c))

    def relay(axis, q):
        block = cols.at[q, at(near[axis] * NC + axis * (NC // 2), NC // 2, 8), :]
        return remote(block, block, sent, relay_in, (near[1 - axis], me_c))

    def push_cols(p, carry):
        for q in range(Q):
            block = cols.at[q, at(me_r * NC, NC, 8), :]
            remote(own_cols(q), block, sent, relay_in, ((me_r + p) % R, me_c)).start()
        return carry

    if square:
        for q in range(Q):
            for axis in range(2):
                own_push(axis, q).start()
    else:
        lax.fori_loop(1, R, push_cols, 0)
    for d in range(2):
        @pl.when(place[d] == 0)
        def _():
            zown(d, LEAD, n)
    for i in range(n):
        scopy(z, i, own_chunk(i)).start()

    def slot(t, carry):
        for d in range(2):
            y = place[d]

            @pl.when(t < n * y)
            def _():
                ys, i = order(n, Z, y - 1, t)
                zs = ys if d == 0 else Z - 1 - ys
                zcopy(d, zs, i).wait_recv()

                @pl.when(y < Z - 1)
                def _():
                    zcopy(d, zs, i).start()

                scopy(zs, i).start()

                @pl.when(jnp.logical_and(t == n * y - 1, y < Z - 1))
                def _():
                    zown(d, LEAD, n)

        return carry

    def by_place(values, j):
        out = pick([row[j] for row in values], z) if isinstance(j, int) else None
        if out is None:
            out = pick(values[0], j)
            for place_z in range(1, Z):
                out = jnp.where(z == place_z, pick(values[place_z], j), out)
        return out

    passed = 0
    if square:
        for q in range(Q):
            until = min(RELAY_SLOTS * (q + 1), min(row[0] for row in early))
            lax.fori_loop(passed, until, slot, 0)
            passed = until
            for axis in range(2):
                own_arrive(axis, q).wait_recv()
                relay(axis, q).start()
    lax.fori_loop(passed, by_place(early, 0), slot, 0)

    landed(rows.at[:, pl.ds(0, NR), :], lsem.at[0])
    landed(cols.at[:, pl.ds(0, NC), :], lsem.at[1])
    acc_in.wait()
    landed(cols.at[:, pl.ds(0, NC if square else (R - 1) * NC), :], relay_in)

    late = [by_place(table, HALVES * Z - LATE + s) for s in range(LATE)]

    def push_late(p, carry):
        for s in range(LATE):
            src = rows.at[0, at(late[s] * UR + k * hr, hr, 8), :]
            remote(src, lfeat.at[me_r, s, k], sent, feat_in, ((me_r + p) % R, me_c)).start()
        return carry

    lax.fori_loop(1, R, push_late, 0)

    for q in range(Q):
        turned = cols[q].T
        hi, lo = split(turned)
        if q == 0:
            tall[...] = turned
        else:
            thi[q - 1] = hi
            tlo[q - 1] = lo
    feats = cols[0]
    hi, lo = split(feats)
    chi[...] = hi
    clo[...] = lo
    ones = jnp.ones((8, F), jnp.bfloat16)
    ncol[...] = sum(lax.dot_general(
        ones, piece, (((1,), (1,)), ((), ())), preferred_element_type=jnp.float32) for piece in reversed(split3(feats * feats)))
    colacc[...] = jnp.zeros_like(colacc)

    def exchange(sub):
        return remote(rowp.at[at(sub * UR + (1 - k) * hr, hr, 8), :], sibp.at[sub], sent, xrecv.at[sub], sibling)

    def weigh(subs):
        for sub in subs:
            landed(rows.at[:, pl.ds(0, hr), :], srecv.at[sub])
        blocks = [at(sub * UR, UR, 8) for sub in subs]
        parts = [at((2 * (sub // HALVES) + core) * NR + sub % HALVES * hr, hr, 8) for sub in subs for core in range(2)]
        f = jnp.concatenate([rows[0, b, :] for b in blocks], axis=0)
        cross = lax.dot_general(f, tall[...], (((1,), (0,)), ((), ())), precision=lax.Precision.HIGHEST, preferred_element_type=jnp.float32)
        g = jnp.concatenate([accv[b, :] for b in parts], axis=0)
        for q in range(1, Q):
            panel = jnp.concatenate([rows[q, b, :] for b in blocks], axis=0)
            g = g + dot3(split(panel), (thi[q - 1], tlo[q - 1]), 1, 0)
        for i, b in enumerate(parts):
            accv[b, :] = g[i * hr:(i + 1) * hr, :]
        dist = jnp.sum(f * f, axis=1, keepdims=True) + ncol[0:1, :] - 2.0 * cross
        return f, g * jnp.exp(-decay_rate * dist)

    def row_part(subs, f, w):
        s = jnp.sum(w, axis=1, keepdims=True)
        part = grad_scale * (dot3(split(w), (chi[...], clo[...]), 1, 0) - s * f)
        for i, sub in enumerate(subs):
            rowp[at(sub * UR, UR, 8), :] = part[i * UR:(i + 1) * UR, :]
        for sub in subs:
            exchange(sub).start()

    def inward(end):
        return 1 if end == 0 else Z - 2

    def finish(subs):
        for sub in subs:
            exchange(sub).wait_recv()
            zs, h = sub // HALVES, sub % HALVES
            total = rowp[at(sub * UR + k * hr, hr, 8), :] + sibp[sub]
            own = zs == z
            straight = jnp.logical_or(own, zs == Z - 1 - z)
            group = jnp.where(straight, 0, jnp.where(zs == 0, 1, jnp.where(zs == Z - 1, 2, 0)))
            to = jnp.where(group == 0, zs, jnp.where(group == 1, inward(0), inward(1)))
            dst = inbox.at[group * Z + z, at(h * hr, hr, 8), :]

            @pl.when(to == z)
            def _():
                dst[...] = total

            @pl.when(to != z)
            def _():
                sumb[sub] = total
                got = bulk.at[jnp.where(group > 0, half_in + h, 0)]
                remote(sumb.at[sub], dst, sent, got, (me_r, 2 * to + k)).start()

    def collect():
        for e, end in enumerate((0, Z - 1)):
            @pl.when(jnp.logical_and(z == inward(end), z != end))
            def _():
                for h in range(HALVES):
                    part = pl.ds(h * hr, hr)
                    if Z > 3:
                        landed(inbox.at[pl.ds(0, Z - 3), part, :], bulk.at[half_in + h])
                    terms = [inbox[(e + 1) * Z + zs, part, :] for zs in range(1, Z - 1)]
                    csum[e, part, :] = sum(terms[1:], terms[0])
                    remote(csum.at[e, part, :], inbox.at[z, part, :], sent, row_in, (me_r, 2 * end + k)).start()

    pairs = HALVES * Z // 2 - 1

    def pair_at(j):
        return [by_place(table, 2 * j + i) for i in range(2)]

    lax.fori_loop(by_place(early, 0), by_place(need, 0), slot, 0)

    def upto(a, b):
        lax.fori_loop(a, b, slot, 0)

    def col_part(f, w):
        turned = w.T
        part = dot3(split(turned), split(f), 1, 0)
        colacc[...] += grad_scale * (part - jnp.sum(turned, axis=1, keepdims=True) * cols[0])

    def step(j, carry):
        @pl.when(j > 0)
        def _():
            upto(by_place(need, j - 1), by_place(need, j))

        subs = pair_at(j)
        f, w = weigh(subs)
        row_part(subs, f, w)
        col_part(f, w)

        @pl.when(j > 0)
        def _():
            finish(pair_at(j - 1))

        return carry

    lax.fori_loop(0, pairs - 1, step, 0)
    if pairs > 1:
        upto(by_place(need, pairs - 2), by_place(need, pairs - 1))
        finish(pair_at(pairs - 2))
    final = pair_at(pairs - 1)
    stops = [by_place(need, pairs - 1)] + [by_place([[row[-1] - 2 + i] for row in need], 0) for i in range(3)]
    stops = [jnp.maximum(stops[0], stop) for stop in stops]
    f, w = weigh(final)
    row_part(final, f, w)
    col_part(f, w)

    def push_grad(p, carry):
        to = (me_r + p) % R
        remote(colacc.at[at(to * NC, NC, 8), :], colr.at[me_r], sent, grad_in, (to, me_c)).start()
        return carry

    def half_of(axis):
        return pl.ds(axis * (F // 2), F // 2)

    def grad_near(axis, half):
        block = colacc.at[at(near[axis] * NC, NC, 8), half_of(half)]
        return remote(block, colr.at[axis, :, half_of(half)], sent, grad_in, (near[axis], me_c))

    def grad_across(axis):
        block = colacc.at[at(across * NC, NC, 8), half_of(axis)]
        return remote(block, cmid.at[axis], sent, bulk.at[half_in + HALVES + axis], (near[axis], me_c))

    if square:
        for axis in range(2):
            grad_across(axis).start()
    else:
        lax.fori_loop(1, R, push_grad, 0)
    upto(stops[0], stops[2])
    finish(final)
    if square:
        for axis in range(2):
            grad_near(axis, axis).start()
    upto(stops[2], stops[3])

    landed(lfeat.at[pl.ds(0, R - 1), :, 0], feat_in)

    def pass_on(p, carry):
        block = lfeat.at[(me_r + p) % R, :, k]
        remote(block, block, sent, pass_in, sibling).start()
        return carry

    lax.fori_loop(1, R, pass_on, 0)

    for s in range(LATE):
        f, w = weigh([late[s]])
        turned, half = w.T, NC // 2
        for p in range(R):
            wlate[s, p * half:(p + 1) * half, :] = jnp.concatenate(
                [turned[p * NC + side * half:p * NC + (side + 1) * half, :] for side in range(2)], axis=1)
        for core in range(2):
            lfeat[me_r, s, core] = f[core * hr:(core + 1) * hr, :]

        def push_w(p, carry, s=s):
            to = (me_r + p) % R
            remote(wlate.at[s, at(to * (NC // 2), NC // 2, 8), :], wlin.at[s, me_r], sent, w_in, (to, me_c)).start()
            return carry

        lax.fori_loop(1, R, push_w, 0)
        wlin[s, me_r] = wlate[s, at(me_r * half, half, 8), :]
        row_part([late[s]], f, w)
        if s == 0:
            collect()
        if s == 0 and square:
            for axis in range(2):
                other = 1 - axis
                grad_across(other).wait_recv()
                colacc[at(near[axis] * NC, NC, 8), half_of(other)] += cmid[other]
                grad_near(axis, other).start()
        if s == 0:
            finish([late[0]])
    landed(lfeat.at[pl.ds(0, R - 1), :, 0], pass_in)
    behind = split(lfeat[...].reshape(R * LATE * UR, F))
    finish([late[LATE - 1]])
    mine = at(me_r * NC, NC, 8)
    landed(colr.at[pl.ds(0, 2 if square else R - 1)], grad_in)
    if square:
        gc_out[...] = colacc[mine, :] + (colr[0] + colr[1])
    else:
        gc_out[...] = colacc[mine, :]

        def add_grad(p, carry):
            gc_out[...] += colr[(me_r + p) % R]
            return carry

        lax.fori_loop(1, R, add_grad, 0)
    landed(wlin.at[:, pl.ds(0, R - 1)], w_in)
    w = jnp.concatenate([jnp.concatenate(
        [jnp.concatenate([wlin[s, p, :, side * UR:(side + 1) * UR] for s in range(LATE)], axis=1) for side in range(2)],
        axis=0) for p in range(R)], axis=1)
    gc_out[...] += grad_scale * (dot3(split(w), behind, 1, 0) - jnp.sum(w, axis=1, keepdims=True) * cols[0, mine, :])

    for end in (0, Z - 1):
        @pl.when(z == end)
        def _():
            landed(inbox.at[pl.ds(0, 2)], row_in)
            gr_out[...] = inbox[end] + (inbox[inward(end)] + inbox[Z - 1 - end])

    @pl.when(jnp.logical_and(z > 0, z < Z - 1))
    def _():
        landed(inbox.at[pl.ds(0, Z - 1)], row_in)
        total = inbox[0]
        for zs in range(1, Z):
            total = total + inbox[zs]
        gr_out[...] = total

    for d in range(2):
        for y in range(Z - 1):
            @pl.when(place[d] == y)
            def _():
                landed(rows.at[:, pl.ds(0, (y + 1) * NR), :], sends.at[d])
    landed(rows.at[:, pl.ds(0, Z * NR), :], sent)
    landed(cols.at[:, pl.ds(0, (2 if square else R - 1) * NC), :], sent)
    if square:
        landed(cols.at[:, pl.ds(0, NC), :], sent)
    landed(sibp, sent)
    landed(inbox.at[pl.ds(0, Z - 1)], sent)
    landed(colr.at[pl.ds(0, R - 1)], sent)
    landed(wlin.at[:, pl.ds(0, R - 1)], sent)
    landed(lfeat.at[pl.ds(0, R - 1), :, 0], sent)
    landed(lfeat.at[pl.ds(0, R - 1), :, 0], sent)


def put(a, b, c, x, y, w, sem):
    size = a.shape[0] // PIECES
    parts = [(a.at[pl.ds(i * size, size), :], x.at[pl.ds(i * size, size), :]) for i in range(PIECES)]
    copies = [pltpu.make_async_copy(u, v, sem.at[i]) for i, (u, v) in enumerate(parts + [(b, y), (c, w)])]
    for copy in copies:
        copy.start()
    for copy in copies:
        copy.wait()


def solution(mesh):
    R, C = mesh.shape["row"], mesh.shape["col"]
    in_specs = (
        P(("row", "col"), None),
        P(("col", "row"), None),
        P(("row", "col"), None),
        P(("col", "row"), None),
        P("row", "col"),
    )
    out_specs = (P("row", "col"), P(("row", "col"), None), P(("col", "row"), None))

    def local(fr, fc, pr, pc, acc):
        NR, F = fr.shape
        NC = fc.shape[0]
        Q = 1 + pr.shape[1] // F
        Z, n = C // 2, HALVES * Q
        hr, subs = NR // HALVES, HALVES * (C // 2)
        f32, bf16 = jnp.float32, jnp.bfloat16
        V, D = pltpu.VMEM, pltpu.SemaphoreType.DMA
        hbm = pl.BlockSpec(memory_space=pl.ANY)
        vmem = pl.BlockSpec(memory_space=pltpu.VMEM)
        shapes = (acc.shape, fr.shape, fc.shape)
        made = pl.pallas_call(
            functools.partial(kernel, R, C),
            out_shape=tuple(pltpu.VMEM(s, f32) for s in shapes),
            in_specs=[hbm] * 5,
            out_specs=(vmem,) * 3,
            scratch_shapes=[
                V((Q, C * NR, F), f32), V((Q, R * NC, F), f32),
                V((R * NC, F), bf16), V((R * NC, F), bf16), V((F, R * NC), f32),
                V((Q - 1, F, R * NC), bf16), V((Q - 1, F, R * NC), bf16),
                V((8, R * NC), f32),
                V((C * NR, F), f32), V((subs, hr, F), f32), V((subs, hr, F), f32), V((3 * Z, NR, F), f32), V((2, NR, F), f32),
                V((R * NC, F), f32), V((R, NC, F), f32), V((2, NC, F // 2), f32),
                V((R, LATE, 2, hr, F), f32), V((LATE, R * NC // 2, 4 * hr), f32), V((LATE, R, NC // 2, 4 * hr), f32),
                D((3,)), D((Z, n)), D((subs,)), D((2, Q)), D((subs,)), D((3,)), D((10,)),
            ],
            compiler_params=pltpu.CompilerParams(
                collective_id=0, has_side_effects=True, vmem_limit_bytes=56 * 1024 * 1024),
        )(fr, fc, pr, pc, acc)
        made = [pltpu.with_memory_space_constraint(m, pltpu.VMEM) for m in made]
        done = pl.pallas_call(
            put,
            out_shape=tuple(jax.ShapeDtypeStruct(s, f32) for s in shapes),
            in_specs=[vmem] * 3,
            out_specs=(hbm,) * 3,
            scratch_shapes=[D((PIECES + 2,))],
        )(*made)
        return tuple(done)

    return jax.shard_map(local, mesh=mesh, in_specs=in_specs, out_specs=out_specs, check_vma=False)
```

```python
import functools

import jax
import jax.numpy as jnp
from jax import lax
from jax.experimental import pallas as pl
from jax.experimental.pallas import tpu as pltpu
from jax.sharding import PartitionSpec as P

decay_rate = 0.125
grad_scale = 0.25
MESH = pl.DeviceIdType.MESH
HALVES = 2
LEAD = 4
RELAY_SLOTS = 2
LATE = 2
PIECES = 4


def split(x):
    hi = x.astype(jnp.bfloat16)
    return hi, (x - hi.astype(jnp.float32)).astype(jnp.bfloat16)


def dot3(a, b, ca, cb):
    dims = (((ca,), (cb,)), ((), ()))
    f = functools.partial(lax.dot_general, dimension_numbers=dims, preferred_element_type=jnp.float32)
    return f(a[0], b[0]) + (f(a[0], b[1]) + f(a[1], b[0]))


def split3(x):
    hi = x.astype(jnp.bfloat16)
    rest = x - hi.astype(jnp.float32)
    mid = rest.astype(jnp.bfloat16)
    return hi, mid, (rest - mid.astype(jnp.float32)).astype(jnp.bfloat16)


def order(n, depth, y, t):
    src, chunk = y * 0, t * 0
    found = y < 0
    for _ in range(depth):
        lead = t < LEAD
        done = jnp.logical_or(lead, t >= LEAD + n * y)
        take = jnp.logical_and(done, jnp.logical_not(found))
        src = jnp.where(take, y, src)
        chunk = jnp.where(take, jnp.where(lead, t, t - n * y), chunk)
        found = jnp.logical_or(found, done)
        y, t = y - 1, t - LEAD
    return src, chunk


def ready(n, depth, z, s, chunks):
    def seq(y):
        own = [(y, i) for i in range(n)]
        return own if y == 0 else own[:LEAD] + seq(y - 1) + own[LEAD:]

    if s == z:
        return 0
    y, ys = (z, s) if s < z else (depth - 1 - z, depth - 1 - s)
    return 1 + max(t for t, (a, i) in enumerate(seq(y - 1)) if a == ys and i in chunks)


def plan(Q, depth):
    n = HALVES * Q
    table, need, early = [], [], []
    steps = [(2 * j, 2 * j + 1) for j in range(HALVES * depth // 2 - 1)]
    steps += [(HALVES * depth - 2,), (HALVES * depth - 1,)]
    for z in range(depth):
        own = [(z, h) for h in range(HALVES)]
        far = [(s, h) for s in range(depth) for h in range(HALVES) if s != z]
        at = {(s, h): ready(n, depth, z, s, range(h * Q, h * Q + Q)) for s, h in own + far}
        end = z in (0, depth - 1)
        far = sorted(far, key=lambda u: (at[u], -abs(u[0] - z)) if end else (u[0] not in (0, depth - 1),))
        subs = own + far if end else far + own
        total = n * max(z, depth - 1 - z)
        late = max(ready(n, depth, z, s, (h * Q,)) for s, h in subs[-LATE:])
        first = min(total, max(late, n + LEAD - 2))
        early.append((first,))
        taken, row = first if end else total, []
        for j, step in enumerate(steps):
            taken = max(taken, min(total, max(at[subs[i]] for i in step)) if j else taken)
            row.append(taken if len(step) > 1 else total)
        table.append([s * HALVES + h for s, h in subs])
        need.append(row)
    return table, need, early


def pick(values, at):
    out = jnp.int32(values[0])
    for i, v in enumerate(values[1:], 1):
        out = jnp.where(at == i, jnp.int32(v), out)
    return out


def kernel(R, C, fr, fc, pr, pc, acc, accv, gr_out, gc_out,
           rows, cols, chi, clo, tall, thi, tlo, ncol, rowp, sibp, sumb, inbox, csum, colacc, colr, cmid, lfeat, wlate, wlin,
           lsem, rrecv, srecv, crecv, xrecv, sends, bulk):
    me_r, me_c = lax.axis_index("row"), lax.axis_index("col")
    z, k = me_c // 2, me_c % 2
    Z = C // 2
    NR, F = fr.shape
    NC = fc.shape[0]
    Q = 1 + pr.shape[1] // F
    n = HALVES * Q
    hr = NR // HALVES
    UR = 2 * hr
    sibling = (me_r, me_c + 1 - 2 * k)
    place = (z, Z - 1 - z)
    step_to = (2, -2)
    table, need, early = plan(Q, Z)
    square = R == 4
    near = (me_r // 2 * 2 + 1 - me_r % 2, (1 - me_r // 2) * 2 + me_r % 2)
    across = R - 1 - me_r
    sent = sends.at[2]
    row_in, grad_in, feat_in, pass_in, relay_in = (bulk.at[i] for i in range(5))
    half_in, w_in = 5, bulk.at[pl.ds(5 + HALVES + 2, LATE)]

    def at(start, size, mult):
        return pl.ds(pl.multiple_of(start, mult), size)

    def remote(src, dst, ss, rs, dev):
        return pltpu.make_async_remote_copy(src_ref=src, dst_ref=dst, send_sem=ss, recv_sem=rs, device_id=dev, device_id_type=MESH)

    def landed(ref, sem):
        pltpu.make_async_copy(ref, ref, sem).wait()

    def place_of(zs, h, core):
        return ((zs * HALVES + h) * 2 + core) * hr

    def rchunk(zs, core, i):
        return rows.at[i % Q, at(place_of(zs, i // Q, core), hr, 8), :]

    def own_chunk(i):
        q, h = i % Q, i // Q
        src = fr if q == 0 else pr
        return src.at[pl.ds(h * hr, hr), pl.ds(max(q - 1, 0) * F, F)]

    def own_cols(q):
        return fc if q == 0 else pc.at[:, pl.ds((q - 1) * F, F)]

    def far(zs, d):
        return zs if d == 0 else zs - 1

    def zcopy(d, zs, i, src=None):
        dst = rchunk(zs, k, i)
        return remote(dst if src is None else src, dst, sends.at[d], rrecv.at[far(zs, d), i], (me_r, me_c + step_to[d]))

    def scopy(zs, i, src=None):
        dst = rchunk(zs, k, i)
        return remote(dst if src is None else src, dst, sent, srecv.at[zs * HALVES + i // Q], sibling)

    barrier = pltpu.get_barrier_semaphore()
    if square:
        for axis in range(2):
            pl.semaphore_signal(barrier, inc=1, device_id=(near[axis], me_c), device_id_type=MESH)
    else:
        def greet(p, carry):
            pl.semaphore_signal(barrier, inc=1, device_id=((me_r + p) % R, me_c), device_id_type=MESH)
            return carry

        lax.fori_loop(1, R, greet, 0)
    pl.semaphore_signal(barrier, inc=1, device_id=sibling, device_id_type=MESH)
    for d in range(2):
        @pl.when(place[d] < Z - 1)
        def _():
            pl.semaphore_signal(barrier, inc=1, device_id=(me_r, me_c + step_to[d]), device_id_type=MESH)
    for q in range(Q):
        for h in range(HALVES):
            pltpu.make_async_copy(own_chunk(h * Q + q), rchunk(z, k, h * Q + q), lsem.at[0]).start()
        pltpu.make_async_copy(own_cols(q), cols.at[q, at(me_r * NC, NC, 8), :], lsem.at[1]).start()
    acc_in = pltpu.make_async_copy(acc, accv, lsem.at[2])
    acc_in.start()

    greeted = (2 if square else R - 1) + 1
    pl.semaphore_wait(barrier, greeted + (z > 0).astype(jnp.int32) + (z < Z - 1).astype(jnp.int32))

    def zown(d, lo, hi):
        for i in range(lo, hi):
            zcopy(d, z, i, own_chunk(i)).start()

    for d in range(2):
        @pl.when(place[d] < Z - 1)
        def _():
            zown(d, 0, LEAD)

    def own_push(axis, q):
        block = cols.at[q, at(me_r * NC, NC, 8), :]
        return remote(own_cols(q), block, sent, crecv.at[q], (near[axis], me_c))

    def relay(axis, q):
        block = cols.at[q, at(near[axis] * NC + axis * (NC // 2), NC // 2, 8), :]
        return remote(block, block, sent, relay_in, (near[1 - axis], me_c))

    def push_cols(p, carry):
        for q in range(Q):
            block = cols.at[q, at(me_r * NC, NC, 8), :]
            remote(own_cols(q), block, sent, relay_in, ((me_r + p) % R, me_c)).start()
        return carry

    if square:
        for q in range(Q):
            for axis in range(2):
                own_push(axis, q).start()
    else:
        lax.fori_loop(1, R, push_cols, 0)
    for d in range(2):
        @pl.when(place[d] == 0)
        def _():
            zown(d, LEAD, n)
    for i in range(n):
        scopy(z, i, own_chunk(i)).start()

    def slot(t, carry):
        for d in range(2):
            y = place[d]

            @pl.when(t < n * y)
            def _():
                ys, i = order(n, Z, y - 1, t)
                zs = ys if d == 0 else Z - 1 - ys
                zcopy(d, zs, i).wait_recv()

                @pl.when(y < Z - 1)
                def _():
                    zcopy(d, zs, i).start()

                scopy(zs, i).start()

                @pl.when(jnp.logical_and(t == n * y - 1, y < Z - 1))
                def _():
                    zown(d, LEAD, n)

        return carry

    def by_place(values, j):
        out = pick([row[j] for row in values], z) if isinstance(j, int) else None
        if out is None:
            out = pick(values[0], j)
            for place_z in range(1, Z):
                out = jnp.where(z == place_z, pick(values[place_z], j), out)
        return out

    passed = 0
    if square:
        for q in range(Q):
            until = min(RELAY_SLOTS * (q + 1), min(row[0] for row in early))
            lax.fori_loop(passed, until, slot, 0)
            passed = until
            landed(cols.at[q, pl.ds(0, 2 * NC), :], crecv.at[q])
            for axis in range(2):
                relay(axis, q).start()
    lax.fori_loop(passed, by_place(early, 0), slot, 0)

    landed(rows.at[:, pl.ds(0, NR), :], lsem.at[0])
    landed(cols.at[:, pl.ds(0, NC), :], lsem.at[1])
    acc_in.wait()
    landed(cols.at[:, pl.ds(0, NC if square else (R - 1) * NC), :], relay_in)

    late = [by_place(table, HALVES * Z - LATE + s) for s in range(LATE)]

    def push_late(p, carry):
        for s in range(LATE):
            src = rows.at[0, at(late[s] * UR + k * hr, hr, 8), :]
            remote(src, lfeat.at[me_r, s, k], sent, feat_in, ((me_r + p) % R, me_c)).start()
        return carry

    lax.fori_loop(1, R, push_late, 0)

    for q in range(Q):
        turned = cols[q].T
        hi, lo = split(turned)
        if q == 0:
            tall[...] = turned
        else:
            thi[q - 1] = hi
            tlo[q - 1] = lo
    feats = cols[0]
    hi, lo = split(feats)
    chi[...] = hi
    clo[...] = lo
    ones = jnp.ones((8, F), jnp.bfloat16)
    ncol[...] = sum(lax.dot_general(
        ones, piece, (((1,), (1,)), ((), ())), preferred_element_type=jnp.float32) for piece in reversed(split3(feats * feats)))
    colacc[...] = jnp.zeros_like(colacc)

    def exchange(sub):
        return remote(rowp.at[at(sub * UR + (1 - k) * hr, hr, 8), :], sibp.at[sub], sent, xrecv.at[sub], sibling)

    def weigh(subs):
        for sub in subs:
            landed(rows.at[:, pl.ds(0, hr), :], srecv.at[sub])
        blocks = [at(sub * UR, UR, 8) for sub in subs]
        parts = [at((2 * (sub // HALVES) + core) * NR + sub % HALVES * hr, hr, 8) for sub in subs for core in range(2)]
        f = jnp.concatenate([rows[0, b, :] for b in blocks], axis=0)
        cross = lax.dot_general(f, tall[...], (((1,), (0,)), ((), ())), precision=lax.Precision.HIGHEST, preferred_element_type=jnp.float32)
        g = jnp.concatenate([accv[b, :] for b in parts], axis=0)
        for q in range(1, Q):
            panel = jnp.concatenate([rows[q, b, :] for b in blocks], axis=0)
            g = g + dot3(split(panel), (thi[q - 1], tlo[q - 1]), 1, 0)
        for i, b in enumerate(parts):
            accv[b, :] = g[i * hr:(i + 1) * hr, :]
        dist = jnp.sum(f * f, axis=1, keepdims=True) + ncol[0:1, :] - 2.0 * cross
        return f, g * jnp.exp(-decay_rate * dist)

    def row_part(subs, f, w):
        s = jnp.sum(w, axis=1, keepdims=True)
        part = grad_scale * (dot3(split(w), (chi[...], clo[...]), 1, 0) - s * f)
        for i, sub in enumerate(subs):
            rowp[at(sub * UR, UR, 8), :] = part[i * UR:(i + 1) * UR, :]
        for sub in subs:
            exchange(sub).start()

    def inward(end):
        return 1 if end == 0 else Z - 2

    def finish(subs):
        for sub in subs:
            exchange(sub).wait_recv()
            zs, h = sub // HALVES, sub % HALVES
            total = rowp[at(sub * UR + k * hr, hr, 8), :] + sibp[sub]
            own = zs == z
            straight = jnp.logical_or(own, zs == Z - 1 - z)
            group = jnp.where(straight, 0, jnp.where(zs == 0, 1, jnp.where(zs == Z - 1, 2, 0)))
            to = jnp.where(group == 0, zs, jnp.where(group == 1, inward(0), inward(1)))
            dst = inbox.at[group * Z + z, at(h * hr, hr, 8), :]

            @pl.when(to == z)
            def _():
                dst[...] = total

            @pl.when(to != z)
            def _():
                sumb[sub] = total
                got = bulk.at[jnp.where(group > 0, half_in + h, 0)]
                remote(sumb.at[sub], dst, sent, got, (me_r, 2 * to + k)).start()

    def collect():
        for e, end in enumerate((0, Z - 1)):
            @pl.when(jnp.logical_and(z == inward(end), z != end))
            def _():
                for h in range(HALVES):
                    part = pl.ds(h * hr, hr)
                    if Z > 3:
                        landed(inbox.at[pl.ds(0, Z - 3), part, :], bulk.at[half_in + h])
                    terms = [inbox[(e + 1) * Z + zs, part, :] for zs in range(1, Z - 1)]
                    csum[e, part, :] = sum(terms[1:], terms[0])
                    remote(csum.at[e, part, :], inbox.at[z, part, :], sent, row_in, (me_r, 2 * end + k)).start()

    pairs = HALVES * Z // 2 - 1

    def pair_at(j):
        return [by_place(table, 2 * j + i) for i in range(2)]

    lax.fori_loop(by_place(early, 0), by_place(need, 0), slot, 0)

    def upto(a, b):
        lax.fori_loop(a, b, slot, 0)

    def col_part(f, w):
        turned = w.T
        part = dot3(split(turned), split(f), 1, 0)
        colacc[...] += grad_scale * (part - jnp.sum(turned, axis=1, keepdims=True) * cols[0])

    def step(j, carry):
        @pl.when(j > 0)
        def _():
            upto(by_place(need, j - 1), by_place(need, j))

        subs = pair_at(j)
        f, w = weigh(subs)
        row_part(subs, f, w)
        col_part(f, w)

        @pl.when(j > 0)
        def _():
            finish(pair_at(j - 1))

        return carry

    lax.fori_loop(0, pairs - 1, step, 0)
    if pairs > 1:
        upto(by_place(need, pairs - 2), by_place(need, pairs - 1))
        finish(pair_at(pairs - 2))
    final = pair_at(pairs - 1)
    stops = [by_place(need, pairs - 1)] + [by_place([[row[-1] - 2 + i] for row in need], 0) for i in range(3)]
    stops = [jnp.maximum(stops[0], stop) for stop in stops]
    f, w = weigh(final)
    row_part(final, f, w)
    col_part(f, w)

    def push_grad(p, carry):
        to = (me_r + p) % R
        remote(colacc.at[at(to * NC, NC, 8), :], colr.at[me_r], sent, grad_in, (to, me_c)).start()
        return carry

    def half_of(axis):
        return pl.ds(axis * (F // 2), F // 2)

    def grad_near(axis, half):
        block = colacc.at[at(near[axis] * NC, NC, 8), half_of(half)]
        return remote(block, colr.at[axis, :, half_of(half)], sent, grad_in, (near[axis], me_c))

    def grad_across(axis):
        block = colacc.at[at(across * NC, NC, 8), half_of(axis)]
        return remote(block, cmid.at[axis], sent, bulk.at[half_in + HALVES + axis], (near[axis], me_c))

    if square:
        for axis in range(2):
            grad_across(axis).start()
    else:
        lax.fori_loop(1, R, push_grad, 0)
    upto(stops[0], stops[1])
    if square:
        for axis in range(2):
            grad_near(axis, axis).start()
    finish(final)
    upto(stops[1], stops[3])

    landed(lfeat.at[pl.ds(0, R - 1), :, 0], feat_in)

    def pass_on(p, carry):
        block = lfeat.at[(me_r + p) % R, :, k]
        remote(block, block, sent, pass_in, sibling).start()
        return carry

    lax.fori_loop(1, R, pass_on, 0)

    for s in range(LATE):
        f, w = weigh([late[s]])
        turned, half = w.T, NC // 2
        for p in range(R):
            wlate[s, p * half:(p + 1) * half, :] = jnp.concatenate(
                [turned[p * NC + side * half:p * NC + (side + 1) * half, :] for side in range(2)], axis=1)
        for core in range(2):
            lfeat[me_r, s, core] = f[core * hr:(core + 1) * hr, :]

        def push_w(p, carry, s=s):
            to = (me_r + p) % R
            remote(wlate.at[s, at(to * (NC // 2), NC // 2, 8), :], wlin.at[s, me_r], sent, w_in.at[s], (to, me_c)).start()
            return carry

        lax.fori_loop(1, R, push_w, 0)
        wlin[s, me_r] = wlate[s, at(me_r * half, half, 8), :]
        row_part([late[s]], f, w)
        if s == 0 and square:
            for axis in range(2):
                other = 1 - axis
                grad_across(other).wait_recv()
                colacc[at(near[axis] * NC, NC, 8), half_of(other)] += cmid[other]
                grad_near(axis, other).start()
        if s == 0:
            collect()
            finish([late[0]])
    landed(lfeat.at[pl.ds(0, R - 1), :, 0], pass_in)
    finish([late[LATE - 1]])
    mine = at(me_r * NC, NC, 8)

    def late_part(s):
        landed(wlin.at[s, pl.ds(0, R - 1)], w_in.at[s])
        w = jnp.concatenate([jnp.concatenate(
            [wlin[s, p, :, side * UR:(side + 1) * UR] for p in range(R)], axis=1) for side in range(2)], axis=0)
        there = lfeat[:, s].reshape(R * UR, F)
        return grad_scale * (dot3(split(w), split(there), 1, 0) - jnp.sum(w, axis=1, keepdims=True) * cols[0, mine, :])

    gc_out[...] = colacc[mine, :] + late_part(0)
    landed(colr.at[pl.ds(0, 2 if square else R - 1)], grad_in)
    if square:
        gc_out[...] += colr[0] + colr[1]
    else:
        def add_grad(p, carry):
            gc_out[...] += colr[(me_r + p) % R]
            return carry

        lax.fori_loop(1, R, add_grad, 0)
    for s in range(1, LATE):
        gc_out[...] += late_part(s)

    for end in (0, Z - 1):
        @pl.when(z == end)
        def _():
            landed(inbox.at[pl.ds(0, 2)], row_in)
            gr_out[...] = inbox[end] + (inbox[inward(end)] + inbox[Z - 1 - end])

    @pl.when(jnp.logical_and(z > 0, z < Z - 1))
    def _():
        landed(inbox.at[pl.ds(0, Z - 1)], row_in)
        total = inbox[0]
        for zs in range(1, Z):
            total = total + inbox[zs]
        gr_out[...] = total

    for d in range(2):
        for y in range(Z - 1):
            @pl.when(place[d] == y)
            def _():
                landed(rows.at[:, pl.ds(0, (y + 1) * NR), :], sends.at[d])
    landed(rows.at[:, pl.ds(0, Z * NR), :], sent)
    landed(cols.at[:, pl.ds(0, (2 if square else R - 1) * NC), :], sent)
    if square:
        landed(cols.at[:, pl.ds(0, NC), :], sent)
    landed(sibp, sent)
    landed(inbox.at[pl.ds(0, Z - 1)], sent)
    landed(colr.at[pl.ds(0, R - 1)], sent)
    landed(wlin.at[:, pl.ds(0, R - 1)], sent)
    landed(lfeat.at[pl.ds(0, R - 1), :, 0], sent)
    landed(lfeat.at[pl.ds(0, R - 1), :, 0], sent)


def put(a, b, c, x, y, w, sem):
    size = a.shape[0] // PIECES
    parts = [(a.at[pl.ds(i * size, size), :], x.at[pl.ds(i * size, size), :]) for i in range(PIECES)]
    copies = [pltpu.make_async_copy(u, v, sem.at[i]) for i, (u, v) in enumerate(parts + [(b, y), (c, w)])]
    for copy in copies:
        copy.start()
    for copy in copies:
        copy.wait()


def solution(mesh):
    R, C = mesh.shape["row"], mesh.shape["col"]
    in_specs = (
        P(("row", "col"), None),
        P(("col", "row"), None),
        P(("row", "col"), None),
        P(("col", "row"), None),
        P("row", "col"),
    )
    out_specs = (P("row", "col"), P(("row", "col"), None), P(("col", "row"), None))

    def local(fr, fc, pr, pc, acc):
        NR, F = fr.shape
        NC = fc.shape[0]
        Q = 1 + pr.shape[1] // F
        Z, n = C // 2, HALVES * Q
        hr, subs = NR // HALVES, HALVES * (C // 2)
        f32, bf16 = jnp.float32, jnp.bfloat16
        V, D = pltpu.VMEM, pltpu.SemaphoreType.DMA
        hbm = pl.BlockSpec(memory_space=pl.ANY)
        vmem = pl.BlockSpec(memory_space=pltpu.VMEM)
        shapes = (acc.shape, fr.shape, fc.shape)
        made = pl.pallas_call(
            functools.partial(kernel, R, C),
            out_shape=tuple(pltpu.VMEM(s, f32) for s in shapes),
            in_specs=[hbm] * 5,
            out_specs=(vmem,) * 3,
            scratch_shapes=[
                V((Q, C * NR, F), f32), V((Q, R * NC, F), f32),
                V((R * NC, F), bf16), V((R * NC, F), bf16), V((F, R * NC), f32),
                V((Q - 1, F, R * NC), bf16), V((Q - 1, F, R * NC), bf16),
                V((8, R * NC), f32),
                V((C * NR, F), f32), V((subs, hr, F), f32), V((subs, hr, F), f32), V((3 * Z, NR, F), f32), V((2, NR, F), f32),
                V((R * NC, F), f32), V((R, NC, F), f32), V((2, NC, F // 2), f32),
                V((R, LATE, 2, hr, F), f32), V((LATE, R * NC // 2, 4 * hr), f32), V((LATE, R, NC // 2, 4 * hr), f32),
                D((3,)), D((Z - 1, n)), D((subs,)), D((Q,)), D((subs,)), D((3,)), D((9 + LATE,)),
            ],
            compiler_params=pltpu.CompilerParams(
                collective_id=0, has_side_effects=True, vmem_limit_bytes=56 * 1024 * 1024),
        )(fr, fc, pr, pc, acc)
        made = [pltpu.with_memory_space_constraint(m, pltpu.VMEM) for m in made]
        done = pl.pallas_call(
            put,
            out_shape=tuple(jax.ShapeDtypeStruct(s, f32) for s in shapes),
            in_specs=[vmem] * 3,
            out_specs=(hbm,) * 3,
            scratch_shapes=[D((PIECES + 2,))],
        )(*made)
        return tuple(done)

    return jax.shard_map(local, mesh=mesh, in_specs=in_specs, out_specs=out_specs, check_vma=False)
```

```python
import functools

import jax
import jax.numpy as jnp
from jax import lax
from jax.experimental import pallas as pl
from jax.experimental.pallas import tpu as pltpu
from jax.sharding import PartitionSpec as P

decay_rate = 0.125
grad_scale = 0.25
MESH = pl.DeviceIdType.MESH
HALVES = 2
LEAD = 4
RELAY_SLOTS = 2
LATE = 2
PIECES = 8


def split(x):
    hi = x.astype(jnp.bfloat16)
    return hi, (x - hi.astype(jnp.float32)).astype(jnp.bfloat16)


def dot3(a, b, ca, cb):
    dims = (((ca,), (cb,)), ((), ()))
    f = functools.partial(lax.dot_general, dimension_numbers=dims, preferred_element_type=jnp.float32)
    return f(a[0], b[0]) + (f(a[0], b[1]) + f(a[1], b[0]))


def split3(x):
    hi = x.astype(jnp.bfloat16)
    rest = x - hi.astype(jnp.float32)
    mid = rest.astype(jnp.bfloat16)
    return hi, mid, (rest - mid.astype(jnp.float32)).astype(jnp.bfloat16)


def order(n, depth, y, t):
    src, chunk = y * 0, t * 0
    found = y < 0
    for _ in range(depth):
        lead = t < LEAD
        done = jnp.logical_or(lead, t >= LEAD + n * y)
        take = jnp.logical_and(done, jnp.logical_not(found))
        src = jnp.where(take, y, src)
        chunk = jnp.where(take, jnp.where(lead, t, t - n * y), chunk)
        found = jnp.logical_or(found, done)
        y, t = y - 1, t - LEAD
    return src, chunk


def ready(n, depth, z, s, chunks):
    def seq(y):
        own = [(y, i) for i in range(n)]
        return own if y == 0 else own[:LEAD] + seq(y - 1) + own[LEAD:]

    if s == z:
        return 0
    y, ys = (z, s) if s < z else (depth - 1 - z, depth - 1 - s)
    return 1 + max(t for t, (a, i) in enumerate(seq(y - 1)) if a == ys and i in chunks)


def plan(Q, depth):
    n = HALVES * Q
    table, need, early = [], [], []
    steps = [(2 * j, 2 * j + 1) for j in range(HALVES * depth // 2 - 1)]
    steps += [(HALVES * depth - 2,), (HALVES * depth - 1,)]
    for z in range(depth):
        own = [(z, h) for h in range(HALVES)]
        far = [(s, h) for s in range(depth) for h in range(HALVES) if s != z]
        at = {(s, h): ready(n, depth, z, s, range(h * Q, h * Q + Q)) for s, h in own + far}
        end = z in (0, depth - 1)
        far = sorted(far, key=lambda u: (at[u], -abs(u[0] - z)) if end else (u[0] not in (0, depth - 1),))
        subs = own + far if end else far + own
        total = n * max(z, depth - 1 - z)
        late = max(ready(n, depth, z, s, (h * Q,)) for s, h in subs[-LATE:])
        first = min(total, max(late, n + LEAD - 2))
        early.append((first,))
        taken, row = first if end else total, []
        for j, step in enumerate(steps):
            taken = max(taken, min(total, max(at[subs[i]] for i in step)) if j else taken)
            row.append(taken if len(step) > 1 else total)
        table.append([s * HALVES + h for s, h in subs])
        need.append(row)
    return table, need, early


def pick(values, at):
    out = jnp.int32(values[0])
    for i, v in enumerate(values[1:], 1):
        out = jnp.where(at == i, jnp.int32(v), out)
    return out


def kernel(R, C, fr, fc, pr, pc, acc, accv, gr_out, gc_out,
           rows, cols, chi, clo, tall, thi, tlo, ncol, rowp, sibp, sumb, inbox, csum, colacc, colr, cmid, lfeat, wlate, wlin,
           lsem, rrecv, srecv, crecv, xrecv, sends, bulk):
    me_r, me_c = lax.axis_index("row"), lax.axis_index("col")
    z, k = me_c // 2, me_c % 2
    Z = C // 2
    NR, F = fr.shape
    NC = fc.shape[0]
    Q = 1 + pr.shape[1] // F
    n = HALVES * Q
    hr = NR // HALVES
    UR = 2 * hr
    sibling = (me_r, me_c + 1 - 2 * k)
    place = (z, Z - 1 - z)
    step_to = (2, -2)
    table, need, early = plan(Q, Z)
    square = R == 4
    near = (me_r // 2 * 2 + 1 - me_r % 2, (1 - me_r // 2) * 2 + me_r % 2)
    across = R - 1 - me_r
    sent = sends.at[2]
    row_in, grad_in, feat_in, pass_in, relay_in = (bulk.at[i] for i in range(5))
    half_in, w_in = 5, bulk.at[pl.ds(5 + HALVES + 2, LATE)]

    def at(start, size, mult):
        return pl.ds(pl.multiple_of(start, mult), size)

    def remote(src, dst, ss, rs, dev):
        return pltpu.make_async_remote_copy(src_ref=src, dst_ref=dst, send_sem=ss, recv_sem=rs, device_id=dev, device_id_type=MESH)

    def landed(ref, sem):
        pltpu.make_async_copy(ref, ref, sem).wait()

    def place_of(zs, h, core):
        return ((zs * HALVES + h) * 2 + core) * hr

    def rchunk(zs, core, i):
        return rows.at[i % Q, at(place_of(zs, i // Q, core), hr, 8), :]

    def own_chunk(i):
        q, h = i % Q, i // Q
        src = fr if q == 0 else pr
        return src.at[pl.ds(h * hr, hr), pl.ds(max(q - 1, 0) * F, F)]

    def own_cols(q):
        return fc if q == 0 else pc.at[:, pl.ds((q - 1) * F, F)]

    def far(zs, d):
        return zs if d == 0 else zs - 1

    def zcopy(d, zs, i, src=None):
        dst = rchunk(zs, k, i)
        return remote(dst if src is None else src, dst, sends.at[d], rrecv.at[far(zs, d), i], (me_r, me_c + step_to[d]))

    def scopy(zs, i, src=None):
        dst = rchunk(zs, k, i)
        return remote(dst if src is None else src, dst, sent, srecv.at[zs * HALVES + i // Q], sibling)

    barrier = pltpu.get_barrier_semaphore()
    if square:
        for axis in range(2):
            pl.semaphore_signal(barrier, inc=1, device_id=(near[axis], me_c), device_id_type=MESH)
    else:
        def greet(p, carry):
            pl.semaphore_signal(barrier, inc=1, device_id=((me_r + p) % R, me_c), device_id_type=MESH)
            return carry

        lax.fori_loop(1, R, greet, 0)
    pl.semaphore_signal(barrier, inc=1, device_id=sibling, device_id_type=MESH)
    for d in range(2):
        @pl.when(place[d] < Z - 1)
        def _():
            pl.semaphore_signal(barrier, inc=1, device_id=(me_r, me_c + step_to[d]), device_id_type=MESH)
    for q in range(Q):
        for h in range(HALVES):
            pltpu.make_async_copy(own_chunk(h * Q + q), rchunk(z, k, h * Q + q), lsem.at[0]).start()
        pltpu.make_async_copy(own_cols(q), cols.at[q, at(me_r * NC, NC, 8), :], lsem.at[1]).start()
    acc_in = pltpu.make_async_copy(acc, accv, lsem.at[2])
    acc_in.start()

    greeted = (2 if square else R - 1) + 1
    pl.semaphore_wait(barrier, greeted + (z > 0).astype(jnp.int32) + (z < Z - 1).astype(jnp.int32))

    def zown(d, lo, hi):
        for i in range(lo, hi):
            zcopy(d, z, i, own_chunk(i)).start()

    for d in range(2):
        @pl.when(place[d] < Z - 1)
        def _():
            zown(d, 0, LEAD)

    def own_push(axis, q):
        block = cols.at[q, at(me_r * NC, NC, 8), :]
        return remote(own_cols(q), block, sent, crecv.at[q], (near[axis], me_c))

    def relay(axis, q):
        block = cols.at[q, at(near[axis] * NC + axis * (NC // 2), NC // 2, 8), :]
        return remote(block, block, sent, relay_in, (near[1 - axis], me_c))

    def push_cols(p, carry):
        for q in range(Q):
            block = cols.at[q, at(me_r * NC, NC, 8), :]
            remote(own_cols(q), block, sent, relay_in, ((me_r + p) % R, me_c)).start()
        return carry

    if square:
        for q in range(Q):
            for axis in range(2):
                own_push(axis, q).start()
    else:
        lax.fori_loop(1, R, push_cols, 0)
    for d in range(2):
        @pl.when(place[d] == 0)
        def _():
            zown(d, LEAD, n)
    for i in range(n):
        scopy(z, i, own_chunk(i)).start()

    def slot(t, carry):
        for d in range(2):
            y = place[d]

            @pl.when(t < n * y)
            def _():
                ys, i = order(n, Z, y - 1, t)
                zs = ys if d == 0 else Z - 1 - ys
                zcopy(d, zs, i).wait_recv()

                @pl.when(y < Z - 1)
                def _():
                    zcopy(d, zs, i).start()

                scopy(zs, i).start()

                @pl.when(jnp.logical_and(t == n * y - 1, y < Z - 1))
                def _():
                    zown(d, LEAD, n)

        return carry

    def by_place(values, j):
        out = pick([row[j] for row in values], z) if isinstance(j, int) else None
        if out is None:
            out = pick(values[0], j)
            for place_z in range(1, Z):
                out = jnp.where(z == place_z, pick(values[place_z], j), out)
        return out

    passed = 0
    if square:
        for q in range(Q):
            until = min(RELAY_SLOTS * (q + 1) - q // 2, min(row[0] for row in early))
            lax.fori_loop(passed, until, slot, 0)
            passed = until
            landed(cols.at[q, pl.ds(0, 2 * NC), :], crecv.at[q])
            for axis in range(2):
                relay(axis, q).start()
    lax.fori_loop(passed, by_place(early, 0), slot, 0)

    landed(rows.at[:, pl.ds(0, NR), :], lsem.at[0])
    landed(cols.at[:, pl.ds(0, NC), :], lsem.at[1])
    acc_in.wait()
    landed(cols.at[:, pl.ds(0, NC if square else (R - 1) * NC), :], relay_in)

    late = [by_place(table, HALVES * Z - LATE + s) for s in range(LATE)]

    def push_late(p, carry):
        for s in range(LATE):
            src = rows.at[0, at(late[s] * UR + k * hr, hr, 8), :]
            remote(src, lfeat.at[me_r, s, k], sent, feat_in, ((me_r + p) % R, me_c)).start()
        return carry

    lax.fori_loop(1, R, push_late, 0)

    for q in range(Q):
        turned = cols[q].T
        hi, lo = split(turned)
        if q == 0:
            tall[...] = turned
        else:
            thi[q - 1] = hi
            tlo[q - 1] = lo
    feats = cols[0]
    hi, lo = split(feats)
    chi[...] = hi
    clo[...] = lo
    ones = jnp.ones((8, F), jnp.bfloat16)
    ncol[...] = sum(lax.dot_general(
        ones, piece, (((1,), (1,)), ((), ())), preferred_element_type=jnp.float32) for piece in reversed(split3(feats * feats)))
    colacc[...] = jnp.zeros_like(colacc)

    def exchange(sub):
        return remote(rowp.at[at(sub * UR + (1 - k) * hr, hr, 8), :], sibp.at[sub], sent, xrecv.at[sub], sibling)

    def weigh(subs):
        for sub in subs:
            landed(rows.at[:, pl.ds(0, hr), :], srecv.at[sub])
        blocks = [at(sub * UR, UR, 8) for sub in subs]
        parts = [at((2 * (sub // HALVES) + core) * NR + sub % HALVES * hr, hr, 8) for sub in subs for core in range(2)]
        f = jnp.concatenate([rows[0, b, :] for b in blocks], axis=0)
        cross = lax.dot_general(f, tall[...], (((1,), (0,)), ((), ())), precision=lax.Precision.HIGHEST, preferred_element_type=jnp.float32)
        g = jnp.concatenate([accv[b, :] for b in parts], axis=0)
        for q in range(1, Q):
            panel = jnp.concatenate([rows[q, b, :] for b in blocks], axis=0)
            g = g + dot3(split(panel), (thi[q - 1], tlo[q - 1]), 1, 0)
        for i, b in enumerate(parts):
            accv[b, :] = g[i * hr:(i + 1) * hr, :]
        dist = jnp.sum(f * f, axis=1, keepdims=True) + ncol[0:1, :] - 2.0 * cross
        return f, g * jnp.exp(-decay_rate * dist)

    def row_part(subs, f, w):
        s = jnp.sum(w, axis=1, keepdims=True)
        part = grad_scale * (dot3(split(w), (chi[...], clo[...]), 1, 0) - s * f)
        for i, sub in enumerate(subs):
            rowp[at(sub * UR, UR, 8), :] = part[i * UR:(i + 1) * UR, :]
        for sub in subs:
            exchange(sub).start()

    def inward(end):
        return 1 if end == 0 else Z - 2

    def finish(subs):
        for sub in subs:
            exchange(sub).wait_recv()
            zs, h = sub // HALVES, sub % HALVES
            total = rowp[at(sub * UR + k * hr, hr, 8), :] + sibp[sub]
            own = zs == z
            straight = jnp.logical_or(own, zs == Z - 1 - z)
            group = jnp.where(straight, 0, jnp.where(zs == 0, 1, jnp.where(zs == Z - 1, 2, 0)))
            to = jnp.where(group == 0, zs, jnp.where(group == 1, inward(0), inward(1)))
            dst = inbox.at[group * Z + z, at(h * hr, hr, 8), :]

            @pl.when(to == z)
            def _():
                dst[...] = total

            @pl.when(to != z)
            def _():
                sumb[sub] = total
                got = bulk.at[jnp.where(group > 0, half_in + h, 0)]
                remote(sumb.at[sub], dst, sent, got, (me_r, 2 * to + k)).start()

    def collect():
        for e, end in enumerate((0, Z - 1)):
            @pl.when(jnp.logical_and(z == inward(end), z != end))
            def _():
                for h in range(HALVES):
                    part = pl.ds(h * hr, hr)
                    if Z > 3:
                        landed(inbox.at[pl.ds(0, Z - 3), part, :], bulk.at[half_in + h])
                    terms = [inbox[(e + 1) * Z + zs, part, :] for zs in range(1, Z - 1)]
                    csum[e, part, :] = sum(terms[1:], terms[0])
                    remote(csum.at[e, part, :], inbox.at[z, part, :], sent, row_in, (me_r, 2 * end + k)).start()

    pairs = HALVES * Z // 2 - 1

    def pair_at(j):
        return [by_place(table, 2 * j + i) for i in range(2)]

    lax.fori_loop(by_place(early, 0), by_place(need, 0), slot, 0)

    def upto(a, b):
        lax.fori_loop(a, b, slot, 0)

    def col_part(f, w):
        turned = w.T
        part = dot3(split(turned), split(f), 1, 0)
        colacc[...] += grad_scale * (part - jnp.sum(turned, axis=1, keepdims=True) * cols[0])

    def step(j, carry):
        @pl.when(j > 0)
        def _():
            upto(by_place(need, j - 1), by_place(need, j))

        subs = pair_at(j)
        f, w = weigh(subs)
        row_part(subs, f, w)
        col_part(f, w)

        @pl.when(j > 0)
        def _():
            finish(pair_at(j - 1))

        return carry

    lax.fori_loop(0, pairs - 1, step, 0)
    if pairs > 1:
        upto(by_place(need, pairs - 2), by_place(need, pairs - 1))
        finish(pair_at(pairs - 2))
    final = pair_at(pairs - 1)
    stops = [by_place(need, pairs - 1)] + [by_place([[row[-1] - 2 + i] for row in need], 0) for i in range(3)]
    stops = [jnp.maximum(stops[0], stop) for stop in stops]
    f, w = weigh(final)
    row_part(final, f, w)
    col_part(f, w)

    def push_grad(p, carry):
        to = (me_r + p) % R
        remote(colacc.at[at(to * NC, NC, 8), :], colr.at[me_r], sent, grad_in, (to, me_c)).start()
        return carry

    def half_of(axis):
        return pl.ds(axis * (F // 2), F // 2)

    def grad_near(axis, half):
        block = colacc.at[at(near[axis] * NC, NC, 8), half_of(half)]
        return remote(block, colr.at[axis, :, half_of(half)], sent, grad_in, (near[axis], me_c))

    def grad_across(axis):
        block = colacc.at[at(across * NC, NC, 8), half_of(axis)]
        return remote(block, cmid.at[axis], sent, bulk.at[half_in + HALVES + axis], (near[axis], me_c))

    if square:
        for axis in range(2):
            grad_across(axis).start()
    else:
        lax.fori_loop(1, R, push_grad, 0)
    upto(stops[0], stops[1])
    if square:
        for axis in range(2):
            grad_near(axis, axis).start()
    finish(final)
    upto(stops[1], stops[3])

    landed(lfeat.at[pl.ds(0, R - 1), :, 0], feat_in)

    def pass_on(p, carry):
        block = lfeat.at[(me_r + p) % R, :, k]
        remote(block, block, sent, pass_in, sibling).start()
        return carry

    lax.fori_loop(1, R, pass_on, 0)

    for s in range(LATE):
        f, w = weigh([late[s]])
        turned, half = w.T, NC // 2
        for p in range(R):
            wlate[s, p * half:(p + 1) * half, :] = jnp.concatenate(
                [turned[p * NC + side * half:p * NC + (side + 1) * half, :] for side in range(2)], axis=1)
        for core in range(2):
            lfeat[me_r, s, core] = f[core * hr:(core + 1) * hr, :]

        def push_w(p, carry, s=s):
            to = (me_r + p) % R
            remote(wlate.at[s, at(to * (NC // 2), NC // 2, 8), :], wlin.at[s, me_r], sent, w_in.at[s], (to, me_c)).start()
            return carry

        lax.fori_loop(1, R, push_w, 0)
        wlin[s, me_r] = wlate[s, at(me_r * half, half, 8), :]
        row_part([late[s]], f, w)
        if s == 0 and square:
            for axis in range(2):
                other = 1 - axis
                grad_across(other).wait_recv()
                colacc[at(near[axis] * NC, NC, 8), half_of(other)] += cmid[other]
                grad_near(axis, other).start()
        if s == 0:
            collect()
            finish([late[0]])
    landed(lfeat.at[pl.ds(0, R - 1), :, 0], pass_in)
    finish([late[LATE - 1]])
    mine = at(me_r * NC, NC, 8)

    def late_part(s):
        landed(wlin.at[s, pl.ds(0, R - 1)], w_in.at[s])
        w = jnp.concatenate([jnp.concatenate(
            [wlin[s, p, :, side * UR:(side + 1) * UR] for p in range(R)], axis=1) for side in range(2)], axis=0)
        there = lfeat[:, s].reshape(R * UR, F)
        return grad_scale * (dot3(split(w), split(there), 1, 0) - jnp.sum(w, axis=1, keepdims=True) * cols[0, mine, :])

    gc_out[...] = colacc[mine, :] + late_part(0)
    landed(colr.at[pl.ds(0, 2 if square else R - 1)], grad_in)
    if square:
        gc_out[...] += colr[0] + colr[1]
    else:
        def add_grad(p, carry):
            gc_out[...] += colr[(me_r + p) % R]
            return carry

        lax.fori_loop(1, R, add_grad, 0)
    for s in range(1, LATE):
        gc_out[...] += late_part(s)

    for end in (0, Z - 1):
        @pl.when(z == end)
        def _():
            landed(inbox.at[pl.ds(0, 2)], row_in)
            gr_out[...] = inbox[end] + (inbox[inward(end)] + inbox[Z - 1 - end])

    @pl.when(jnp.logical_and(z > 0, z < Z - 1))
    def _():
        landed(inbox.at[pl.ds(0, Z - 1)], row_in)
        total = inbox[0]
        for zs in range(1, Z):
            total = total + inbox[zs]
        gr_out[...] = total

    for d in range(2):
        for y in range(Z - 1):
            @pl.when(place[d] == y)
            def _():
                landed(rows.at[:, pl.ds(0, (y + 1) * NR), :], sends.at[d])
    landed(rows.at[:, pl.ds(0, Z * NR), :], sent)
    landed(cols.at[:, pl.ds(0, (2 if square else R - 1) * NC), :], sent)
    if square:
        landed(cols.at[:, pl.ds(0, NC), :], sent)
    landed(sibp, sent)
    landed(inbox.at[pl.ds(0, Z - 1)], sent)
    landed(colr.at[pl.ds(0, R - 1)], sent)
    landed(wlin.at[:, pl.ds(0, R - 1)], sent)
    landed(lfeat.at[pl.ds(0, R - 1), :, 0], sent)
    landed(lfeat.at[pl.ds(0, R - 1), :, 0], sent)


def put(a, b, c, x, y, w, sem):
    size = a.shape[0] // PIECES
    parts = [(a.at[pl.ds(i * size, size), :], x.at[pl.ds(i * size, size), :]) for i in range(PIECES)]
    copies = [pltpu.make_async_copy(u, v, sem.at[i]) for i, (u, v) in enumerate(parts + [(b, y), (c, w)])]
    for copy in copies:
        copy.start()
    for copy in copies:
        copy.wait()


def solution(mesh):
    R, C = mesh.shape["row"], mesh.shape["col"]
    in_specs = (
        P(("row", "col"), None),
        P(("col", "row"), None),
        P(("row", "col"), None),
        P(("col", "row"), None),
        P("row", "col"),
    )
    out_specs = (P("row", "col"), P(("row", "col"), None), P(("col", "row"), None))

    def local(fr, fc, pr, pc, acc):
        NR, F = fr.shape
        NC = fc.shape[0]
        Q = 1 + pr.shape[1] // F
        Z, n = C // 2, HALVES * Q
        hr, subs = NR // HALVES, HALVES * (C // 2)
        f32, bf16 = jnp.float32, jnp.bfloat16
        V, D = pltpu.VMEM, pltpu.SemaphoreType.DMA
        hbm = pl.BlockSpec(memory_space=pl.ANY)
        vmem = pl.BlockSpec(memory_space=pltpu.VMEM)
        shapes = (acc.shape, fr.shape, fc.shape)
        made = pl.pallas_call(
            functools.partial(kernel, R, C),
            out_shape=tuple(pltpu.VMEM(s, f32) for s in shapes),
            in_specs=[hbm] * 5,
            out_specs=(vmem,) * 3,
            scratch_shapes=[
                V((Q, C * NR, F), f32), V((Q, R * NC, F), f32),
                V((R * NC, F), bf16), V((R * NC, F), bf16), V((F, R * NC), f32),
                V((Q - 1, F, R * NC), bf16), V((Q - 1, F, R * NC), bf16),
                V((8, R * NC), f32),
                V((C * NR, F), f32), V((subs, hr, F), f32), V((subs, hr, F), f32), V((3 * Z, NR, F), f32), V((2, NR, F), f32),
                V((R * NC, F), f32), V((R, NC, F), f32), V((2, NC, F // 2), f32),
                V((R, LATE, 2, hr, F), f32), V((LATE, R * NC // 2, 4 * hr), f32), V((LATE, R, NC // 2, 4 * hr), f32),
                D((3,)), D((Z - 1, n)), D((subs,)), D((Q,)), D((subs,)), D((3,)), D((9 + LATE,)),
            ],
            compiler_params=pltpu.CompilerParams(
                collective_id=0, has_side_effects=True, vmem_limit_bytes=56 * 1024 * 1024),
        )(fr, fc, pr, pc, acc)
        made = [pltpu.with_memory_space_constraint(m, pltpu.VMEM) for m in made]
        done = pl.pallas_call(
            put,
            out_shape=tuple(jax.ShapeDtypeStruct(s, f32) for s in shapes),
            in_specs=[vmem] * 3,
            out_specs=(hbm,) * 3,
            scratch_shapes=[D((PIECES + 2,))],
        )(*made)
        return tuple(done)

    return jax.shard_map(local, mesh=mesh, in_specs=in_specs, out_specs=out_specs, check_vma=False)
```

```python
import functools

import jax
import jax.numpy as jnp
from jax import lax
from jax.experimental import pallas as pl
from jax.experimental.pallas import tpu as pltpu
from jax.sharding import PartitionSpec as P

decay_rate = 0.125
grad_scale = 0.25
MESH = pl.DeviceIdType.MESH
HALVES = 2
LEAD = 4
RELAY_SLOTS = 2
LATE = 2
PIECES = 8


def split(x):
    hi = x.astype(jnp.bfloat16)
    return hi, (x - hi.astype(jnp.float32)).astype(jnp.bfloat16)


def dot3(a, b, ca, cb):
    dims = (((ca,), (cb,)), ((), ()))
    f = functools.partial(lax.dot_general, dimension_numbers=dims, preferred_element_type=jnp.float32)
    return f(a[0], b[0]) + (f(a[0], b[1]) + f(a[1], b[0]))


def split3(x):
    hi = x.astype(jnp.bfloat16)
    rest = x - hi.astype(jnp.float32)
    mid = rest.astype(jnp.bfloat16)
    return hi, mid, (rest - mid.astype(jnp.float32)).astype(jnp.bfloat16)


def order(n, depth, y, t):
    src, chunk = y * 0, t * 0
    found = y < 0
    for _ in range(depth):
        lead = t < LEAD
        done = jnp.logical_or(lead, t >= LEAD + n * y)
        take = jnp.logical_and(done, jnp.logical_not(found))
        src = jnp.where(take, y, src)
        chunk = jnp.where(take, jnp.where(lead, t, t - n * y), chunk)
        found = jnp.logical_or(found, done)
        y, t = y - 1, t - LEAD
    return src, chunk


def ready(n, depth, z, s, chunks):
    def seq(y):
        own = [(y, i) for i in range(n)]
        return own if y == 0 else own[:LEAD] + seq(y - 1) + own[LEAD:]

    if s == z:
        return 0
    y, ys = (z, s) if s < z else (depth - 1 - z, depth - 1 - s)
    return 1 + max(t for t, (a, i) in enumerate(seq(y - 1)) if a == ys and i in chunks)


def plan(Q, depth):
    n = HALVES * Q
    table, need, early = [], [], []
    steps = [(2 * j, 2 * j + 1) for j in range(HALVES * depth // 2 - 1)]
    steps += [(HALVES * depth - 2,), (HALVES * depth - 1,)]
    for z in range(depth):
        own = [(z, h) for h in range(HALVES)]
        far = [(s, h) for s in range(depth) for h in range(HALVES) if s != z]
        at = {(s, h): ready(n, depth, z, s, range(h * Q, h * Q + Q)) for s, h in own + far}
        end = z in (0, depth - 1)
        far = sorted(far, key=lambda u: (at[u], -abs(u[0] - z)) if end else (u[0] not in (0, depth - 1),))
        subs = own + far if end else far + own
        total = n * max(z, depth - 1 - z)
        late = max(ready(n, depth, z, s, (h * Q,)) for s, h in subs[-LATE:])
        first = min(total, max(late, n + LEAD - 2))
        early.append((first,))
        taken, row = first if end else total, []
        for j, step in enumerate(steps):
            taken = max(taken, min(total, max(at[subs[i]] for i in step)) if j else taken)
            row.append(taken if len(step) > 1 else total)
        table.append([s * HALVES + h for s, h in subs])
        need.append(row)
    return table, need, early


def pick(values, at):
    out = jnp.int32(values[0])
    for i, v in enumerate(values[1:], 1):
        out = jnp.where(at == i, jnp.int32(v), out)
    return out


def kernel(R, C, fr, fc, pr, pc, acc, accv, gr_out, gc_out,
           rows, cols, chi, clo, tall, thi, tlo, ncol, rowp, sibp, sumb, inbox, csum, colacc, colr, cmid, lfeat, wlate, wlin,
           lsem, rrecv, srecv, crecv, xrecv, sends, bulk):
    me_r, me_c = lax.axis_index("row"), lax.axis_index("col")
    z, k = me_c // 2, me_c % 2
    Z = C // 2
    NR, F = fr.shape
    NC = fc.shape[0]
    Q = 1 + pr.shape[1] // F
    n = HALVES * Q
    hr = NR // HALVES
    UR = 2 * hr
    sibling = (me_r, me_c + 1 - 2 * k)
    place = (z, Z - 1 - z)
    step_to = (2, -2)
    table, need, early = plan(Q, Z)
    square = R == 4
    near = (me_r // 2 * 2 + 1 - me_r % 2, (1 - me_r // 2) * 2 + me_r % 2)
    across = R - 1 - me_r
    sent = sends.at[2]
    row_in, grad_in, feat_in, pass_in, relay_in = (bulk.at[i] for i in range(5))
    half_in, w_in = 5, bulk.at[pl.ds(5 + HALVES + 2, LATE)]

    def at(start, size, mult):
        return pl.ds(pl.multiple_of(start, mult), size)

    def remote(src, dst, ss, rs, dev):
        return pltpu.make_async_remote_copy(src_ref=src, dst_ref=dst, send_sem=ss, recv_sem=rs, device_id=dev, device_id_type=MESH)

    def landed(ref, sem):
        pltpu.make_async_copy(ref, ref, sem).wait()

    def place_of(zs, h, core):
        return ((zs * HALVES + h) * 2 + core) * hr

    def rchunk(zs, core, i):
        return rows.at[i % Q, at(place_of(zs, i // Q, core), hr, 8), :]

    def own_chunk(i):
        q, h = i % Q, i // Q
        src = fr if q == 0 else pr
        return src.at[pl.ds(h * hr, hr), pl.ds(max(q - 1, 0) * F, F)]

    def own_cols(q):
        return fc if q == 0 else pc.at[:, pl.ds((q - 1) * F, F)]

    def far(zs, d):
        return zs if d == 0 else zs - 1

    def zcopy(d, zs, i, src=None):
        dst = rchunk(zs, k, i)
        return remote(dst if src is None else src, dst, sends.at[d], rrecv.at[far(zs, d), i], (me_r, me_c + step_to[d]))

    def scopy(zs, i, src=None):
        dst = rchunk(zs, k, i)
        return remote(dst if src is None else src, dst, sent, srecv.at[zs * HALVES + i // Q], sibling)

    barrier = pltpu.get_barrier_semaphore()
    if square:
        for axis in range(2):
            pl.semaphore_signal(barrier, inc=1, device_id=(near[axis], me_c), device_id_type=MESH)
    else:
        def greet(p, carry):
            pl.semaphore_signal(barrier, inc=1, device_id=((me_r + p) % R, me_c), device_id_type=MESH)
            return carry

        lax.fori_loop(1, R, greet, 0)
    pl.semaphore_signal(barrier, inc=1, device_id=sibling, device_id_type=MESH)
    for d in range(2):
        @pl.when(place[d] < Z - 1)
        def _():
            pl.semaphore_signal(barrier, inc=1, device_id=(me_r, me_c + step_to[d]), device_id_type=MESH)
    for q in range(Q):
        for h in range(HALVES):
            pltpu.make_async_copy(own_chunk(h * Q + q), rchunk(z, k, h * Q + q), lsem.at[0]).start()
        pltpu.make_async_copy(own_cols(q), cols.at[q, at(me_r * NC, NC, 8), :], lsem.at[1]).start()
    acc_in = pltpu.make_async_copy(acc, accv, lsem.at[2])
    acc_in.start()

    greeted = (2 if square else R - 1) + 1
    pl.semaphore_wait(barrier, greeted + (z > 0).astype(jnp.int32) + (z < Z - 1).astype(jnp.int32))

    def zown(d, lo, hi):
        for i in range(lo, hi):
            zcopy(d, z, i, own_chunk(i)).start()

    for d in range(2):
        @pl.when(place[d] < Z - 1)
        def _():
            zown(d, 0, LEAD)

    def own_push(axis, q):
        block = cols.at[q, at(me_r * NC, NC, 8), :]
        return remote(own_cols(q), block, sent, crecv.at[q], (near[axis], me_c))

    def relay(axis, q):
        block = cols.at[q, at(near[axis] * NC + axis * (NC // 2), NC // 2, 8), :]
        return remote(block, block, sent, relay_in, (near[1 - axis], me_c))

    def push_cols(p, carry):
        for q in range(Q):
            block = cols.at[q, at(me_r * NC, NC, 8), :]
            remote(own_cols(q), block, sent, relay_in, ((me_r + p) % R, me_c)).start()
        return carry

    if square:
        for q in range(Q):
            for axis in range(2):
                own_push(axis, q).start()
    else:
        lax.fori_loop(1, R, push_cols, 0)
    for d in range(2):
        @pl.when(place[d] == 0)
        def _():
            zown(d, LEAD, n)
    for i in range(n):
        scopy(z, i, own_chunk(i)).start()

    def slot(t, carry):
        for d in range(2):
            y = place[d]

            @pl.when(t < n * y)
            def _():
                ys, i = order(n, Z, y - 1, t)
                zs = ys if d == 0 else Z - 1 - ys
                zcopy(d, zs, i).wait_recv()

                @pl.when(y < Z - 1)
                def _():
                    zcopy(d, zs, i).start()

                scopy(zs, i).start()

                @pl.when(jnp.logical_and(t == n * y - 1, y < Z - 1))
                def _():
                    zown(d, LEAD, n)

        return carry

    def by_place(values, j):
        out = pick([row[j] for row in values], z) if isinstance(j, int) else None
        if out is None:
            out = pick(values[0], j)
            for place_z in range(1, Z):
                out = jnp.where(z == place_z, pick(values[place_z], j), out)
        return out

    passed = 0
    if square:
        for q in range(Q):
            until = min(RELAY_SLOTS * (q + 1) - q // 2, min(row[0] for row in early))
            lax.fori_loop(passed, until, slot, 0)
            passed = until
            landed(cols.at[q, pl.ds(0, 2 * NC), :], crecv.at[q])
            for axis in range(2):
                relay(axis, q).start()
    lax.fori_loop(passed, by_place(early, 0), slot, 0)

    landed(rows.at[:, pl.ds(0, NR), :], lsem.at[0])
    landed(cols.at[:, pl.ds(0, NC), :], lsem.at[1])
    acc_in.wait()
    landed(cols.at[:, pl.ds(0, NC if square else (R - 1) * NC), :], relay_in)

    late = [by_place(table, HALVES * Z - LATE + s) for s in range(LATE)]

    def push_late(p, carry):
        for s in range(LATE):
            src = rows.at[0, at(late[s] * UR + k * hr, hr, 8), :]
            remote(src, lfeat.at[me_r, s, k], sent, feat_in, ((me_r + p) % R, me_c)).start()
        return carry

    lax.fori_loop(1, R, push_late, 0)

    for q in range(Q):
        turned = cols[q].T
        hi, lo = split(turned)
        if q == 0:
            tall[...] = turned
        else:
            thi[q - 1] = hi
            tlo[q - 1] = lo
    feats = cols[0]
    hi, lo = split(feats)
    chi[...] = hi
    clo[...] = lo
    ones = jnp.ones((8, F), jnp.bfloat16)
    ncol[...] = sum(lax.dot_general(
        ones, piece, (((1,), (1,)), ((), ())), preferred_element_type=jnp.float32) for piece in reversed(split3(feats * feats)))
    colacc[...] = jnp.zeros_like(colacc)

    def exchange(sub):
        return remote(rowp.at[at(sub * UR + (1 - k) * hr, hr, 8), :], sibp.at[sub], sent, xrecv.at[sub], sibling)

    def weigh(subs):
        for sub in subs:
            landed(rows.at[:, pl.ds(0, hr), :], srecv.at[sub])
        blocks = [at(sub * UR, UR, 8) for sub in subs]
        parts = [at((2 * (sub // HALVES) + core) * NR + sub % HALVES * hr, hr, 8) for sub in subs for core in range(2)]
        f = jnp.concatenate([rows[0, b, :] for b in blocks], axis=0)
        cross = lax.dot_general(f, tall[...], (((1,), (0,)), ((), ())), precision=lax.Precision.HIGHEST, preferred_element_type=jnp.float32)
        g = jnp.concatenate([accv[b, :] for b in parts], axis=0)
        for q in range(1, Q):
            panel = jnp.concatenate([rows[q, b, :] for b in blocks], axis=0)
            g = g + dot3(split(panel), (thi[q - 1], tlo[q - 1]), 1, 0)
        for i, b in enumerate(parts):
            accv[b, :] = g[i * hr:(i + 1) * hr, :]
        dist = jnp.sum(f * f, axis=1, keepdims=True) + ncol[0:1, :] - 2.0 * cross
        return f, g * jnp.exp(-decay_rate * dist)

    def row_part(subs, f, w):
        s = jnp.sum(w, axis=1, keepdims=True)
        part = grad_scale * (dot3(split(w), (chi[...], clo[...]), 1, 0) - s * f)
        for i, sub in enumerate(subs):
            rowp[at(sub * UR, UR, 8), :] = part[i * UR:(i + 1) * UR, :]
        for sub in subs:
            exchange(sub).start()

    def inward(end):
        return 1 if end == 0 else Z - 2

    def finish(subs):
        for sub in subs:
            exchange(sub).wait_recv()
            zs, h = sub // HALVES, sub % HALVES
            total = rowp[at(sub * UR + k * hr, hr, 8), :] + sibp[sub]
            own = zs == z
            straight = jnp.logical_or(own, zs == Z - 1 - z)
            group = jnp.where(straight, 0, jnp.where(zs == 0, 1, jnp.where(zs == Z - 1, 2, 0)))
            to = jnp.where(group == 0, zs, jnp.where(group == 1, inward(0), inward(1)))
            dst = inbox.at[group * Z + z, at(h * hr, hr, 8), :]

            @pl.when(to == z)
            def _():
                dst[...] = total

            @pl.when(to != z)
            def _():
                sumb[sub] = total
                got = bulk.at[jnp.where(group > 0, half_in + h, 0)]
                remote(sumb.at[sub], dst, sent, got, (me_r, 2 * to + k)).start()

    def collect():
        for e, end in enumerate((0, Z - 1)):
            @pl.when(jnp.logical_and(z == inward(end), z != end))
            def _():
                for h in range(HALVES):
                    part = pl.ds(h * hr, hr)
                    if Z > 3:
                        landed(inbox.at[pl.ds(0, Z - 3), part, :], bulk.at[half_in + h])
                    terms = [inbox[(e + 1) * Z + zs, part, :] for zs in range(1, Z - 1)]
                    csum[e, part, :] = sum(terms[1:], terms[0])
                    remote(csum.at[e, part, :], inbox.at[z, part, :], sent, row_in, (me_r, 2 * end + k)).start()

    pairs = HALVES * Z // 2 - 1

    def pair_at(j):
        return [by_place(table, 2 * j + i) for i in range(2)]

    lax.fori_loop(by_place(early, 0), by_place(need, 0), slot, 0)

    def upto(a, b):
        lax.fori_loop(a, b, slot, 0)

    def col_part(f, w):
        turned = w.T
        part = dot3(split(turned), split(f), 1, 0)
        colacc[...] += grad_scale * (part - jnp.sum(turned, axis=1, keepdims=True) * cols[0])

    def step(j, carry):
        @pl.when(j > 0)
        def _():
            upto(by_place(need, j - 1), by_place(need, j))

        subs = pair_at(j)
        f, w = weigh(subs)
        row_part(subs, f, w)
        col_part(f, w)

        @pl.when(j > 0)
        def _():
            finish(pair_at(j - 1))

        return carry

    lax.fori_loop(0, pairs - 1, step, 0)
    if pairs > 1:
        upto(by_place(need, pairs - 2), by_place(need, pairs - 1))
        finish(pair_at(pairs - 2))
    final = pair_at(pairs - 1)
    stops = [by_place(need, pairs - 1)] + [by_place([[row[-1] - 2 + i] for row in need], 0) for i in range(3)]
    stops = [jnp.maximum(stops[0], stop) for stop in stops]
    f, w = weigh(final)
    col_part(f, w)

    def push_grad(p, carry):
        to = (me_r + p) % R
        remote(colacc.at[at(to * NC, NC, 8), :], colr.at[me_r], sent, grad_in, (to, me_c)).start()
        return carry

    def half_of(axis):
        return pl.ds(axis * (F // 2), F // 2)

    def grad_near(axis, half):
        block = colacc.at[at(near[axis] * NC, NC, 8), half_of(half)]
        return remote(block, colr.at[axis, :, half_of(half)], sent, grad_in, (near[axis], me_c))

    def grad_across(axis):
        block = colacc.at[at(across * NC, NC, 8), half_of(axis)]
        return remote(block, cmid.at[axis], sent, bulk.at[half_in + HALVES + axis], (near[axis], me_c))

    if square:
        for axis in range(2):
            grad_across(axis).start()
    else:
        lax.fori_loop(1, R, push_grad, 0)
    row_part(final, f, w)
    upto(stops[0], stops[1])
    if square:
        for axis in range(2):
            grad_near(axis, axis).start()
    finish(final)
    upto(stops[1], stops[3])

    landed(lfeat.at[pl.ds(0, R - 1), :, 0], feat_in)

    def pass_on(p, carry):
        block = lfeat.at[(me_r + p) % R, :, k]
        remote(block, block, sent, pass_in, sibling).start()
        return carry

    lax.fori_loop(1, R, pass_on, 0)

    for s in range(LATE):
        f, w = weigh([late[s]])
        turned, half = w.T, NC // 2
        for p in range(R):
            wlate[s, p * half:(p + 1) * half, :] = jnp.concatenate(
                [turned[p * NC + side * half:p * NC + (side + 1) * half, :] for side in range(2)], axis=1)
        for core in range(2):
            lfeat[me_r, s, core] = f[core * hr:(core + 1) * hr, :]

        def push_w(p, carry, s=s):
            to = (me_r + p) % R
            remote(wlate.at[s, at(to * (NC // 2), NC // 2, 8), :], wlin.at[s, me_r], sent, w_in.at[s], (to, me_c)).start()
            return carry

        lax.fori_loop(1, R, push_w, 0)
        wlin[s, me_r] = wlate[s, at(me_r * half, half, 8), :]
        row_part([late[s]], f, w)
        if s == 0 and square:
            for axis in range(2):
                other = 1 - axis
                grad_across(other).wait_recv()
                colacc[at(near[axis] * NC, NC, 8), half_of(other)] += cmid[other]
                grad_near(axis, other).start()
        if s == 0:
            collect()
            finish([late[0]])
    landed(lfeat.at[pl.ds(0, R - 1), :, 0], pass_in)
    finish([late[LATE - 1]])
    mine = at(me_r * NC, NC, 8)

    def late_part(s):
        landed(wlin.at[s, pl.ds(0, R - 1)], w_in.at[s])
        w = jnp.concatenate([jnp.concatenate(
            [wlin[s, p, :, side * UR:(side + 1) * UR] for p in range(R)], axis=1) for side in range(2)], axis=0)
        there = lfeat[:, s].reshape(R * UR, F)
        return grad_scale * (dot3(split(w), split(there), 1, 0) - jnp.sum(w, axis=1, keepdims=True) * cols[0, mine, :])

    gc_out[...] = colacc[mine, :] + late_part(0)
    landed(colr.at[pl.ds(0, 2 if square else R - 1)], grad_in)
    if square:
        gc_out[...] += colr[0] + colr[1]
    else:
        def add_grad(p, carry):
            gc_out[...] += colr[(me_r + p) % R]
            return carry

        lax.fori_loop(1, R, add_grad, 0)
    for s in range(1, LATE):
        gc_out[...] += late_part(s)

    for end in (0, Z - 1):
        @pl.when(z == end)
        def _():
            landed(inbox.at[pl.ds(0, 2)], row_in)
            gr_out[...] = inbox[end] + (inbox[inward(end)] + inbox[Z - 1 - end])

    @pl.when(jnp.logical_and(z > 0, z < Z - 1))
    def _():
        landed(inbox.at[pl.ds(0, Z - 1)], row_in)
        total = inbox[0]
        for zs in range(1, Z):
            total = total + inbox[zs]
        gr_out[...] = total

    for d in range(2):
        for y in range(Z - 1):
            @pl.when(place[d] == y)
            def _():
                landed(rows.at[:, pl.ds(0, (y + 1) * NR), :], sends.at[d])
    landed(rows.at[:, pl.ds(0, Z * NR), :], sent)
    landed(cols.at[:, pl.ds(0, (2 if square else R - 1) * NC), :], sent)
    if square:
        landed(cols.at[:, pl.ds(0, NC), :], sent)
    landed(sibp, sent)
    landed(inbox.at[pl.ds(0, Z - 1)], sent)
    landed(colr.at[pl.ds(0, R - 1)], sent)
    landed(wlin.at[:, pl.ds(0, R - 1)], sent)
    landed(lfeat.at[pl.ds(0, R - 1), :, 0], sent)
    landed(lfeat.at[pl.ds(0, R - 1), :, 0], sent)


def put(a, b, c, x, y, w, sem):
    size = a.shape[0] // PIECES
    parts = [(a.at[pl.ds(i * size, size), :], x.at[pl.ds(i * size, size), :]) for i in range(PIECES)]
    copies = [pltpu.make_async_copy(u, v, sem.at[i]) for i, (u, v) in enumerate(parts + [(b, y), (c, w)])]
    for copy in copies:
        copy.start()
    for copy in copies:
        copy.wait()


def solution(mesh):
    R, C = mesh.shape["row"], mesh.shape["col"]
    in_specs = (
        P(("row", "col"), None),
        P(("col", "row"), None),
        P(("row", "col"), None),
        P(("col", "row"), None),
        P("row", "col"),
    )
    out_specs = (P("row", "col"), P(("row", "col"), None), P(("col", "row"), None))

    def local(fr, fc, pr, pc, acc):
        NR, F = fr.shape
        NC = fc.shape[0]
        Q = 1 + pr.shape[1] // F
        Z, n = C // 2, HALVES * Q
        hr, subs = NR // HALVES, HALVES * (C // 2)
        f32, bf16 = jnp.float32, jnp.bfloat16
        V, D = pltpu.VMEM, pltpu.SemaphoreType.DMA
        hbm = pl.BlockSpec(memory_space=pl.ANY)
        vmem = pl.BlockSpec(memory_space=pltpu.VMEM)
        shapes = (acc.shape, fr.shape, fc.shape)
        made = pl.pallas_call(
            functools.partial(kernel, R, C),
            out_shape=tuple(pltpu.VMEM(s, f32) for s in shapes),
            in_specs=[hbm] * 5,
            out_specs=(vmem,) * 3,
            scratch_shapes=[
                V((Q, C * NR, F), f32), V((Q, R * NC, F), f32),
                V((R * NC, F), bf16), V((R * NC, F), bf16), V((F, R * NC), f32),
                V((Q - 1, F, R * NC), bf16), V((Q - 1, F, R * NC), bf16),
                V((8, R * NC), f32),
                V((C * NR, F), f32), V((subs, hr, F), f32), V((subs, hr, F), f32), V((3 * Z, NR, F), f32), V((2, NR, F), f32),
                V((R * NC, F), f32), V((R, NC, F), f32), V((2, NC, F // 2), f32),
                V((R, LATE, 2, hr, F), f32), V((LATE, R * NC // 2, 4 * hr), f32), V((LATE, R, NC // 2, 4 * hr), f32),
                D((3,)), D((Z - 1, n)), D((subs,)), D((Q,)), D((subs,)), D((3,)), D((9 + LATE,)),
            ],
            compiler_params=pltpu.CompilerParams(
                collective_id=0, has_side_effects=True, vmem_limit_bytes=56 * 1024 * 1024),
        )(fr, fc, pr, pc, acc)
        made = [pltpu.with_memory_space_constraint(m, pltpu.VMEM) for m in made]
        done = pl.pallas_call(
            put,
            out_shape=tuple(jax.ShapeDtypeStruct(s, f32) for s in shapes),
            in_specs=[vmem] * 3,
            out_specs=(hbm,) * 3,
            scratch_shapes=[D((PIECES + 2,))],
        )(*made)
        return tuple(done)

    return jax.shard_map(local, mesh=mesh, in_specs=in_specs, out_specs=out_specs, check_vma=False)
```
